32 devices in a mesh: lat: 4 (over y, x), lon: 8 (over z, core).
Axes of the slice: x: 2, y: 2, z: 4, core: 2. Of those that a mesh axis runs over, the one named last changes fastest.
Arguments:
- tracers: bfloat16 [64, 256, 1024], P('lat', 'lon'), may hold values from -6 to 6
- east_wind: bfloat16 [64, 256, 128], P('lat', 'lon'), may hold values from -0.5 to 0.5
- north_wind: bfloat16 [64, 256, 128], P('lat', 'lon'), may hold values from -0.5 to 0.5
- span_of: int32 [64, 256], P('lat', 'lon'), may hold values from 0 to 511, as said below
- slot_of: int32 [64, 256], P('lat', 'lon'), may hold values from 0 to 47
- inverses: bfloat16 [512, 128, 128], P(('lat', 'lon'))
Outputs:
- tendency: float32 [64, 256, 1024], P('lat', 'lon')
The draws below stay inside these ranges and needn't reach their ends.
Inputs may be any that keep to these rules, and one draw needn't show every extreme that they name: `span_of`: together with slot_of, every (span, slot) pair is named by at most one column. Span c belongs to device c // 16 in the mesh's order (lat index times the lon size plus lon index). The columns of one device name spans of one owner at most 24 times, and in every draw some owner gets exactly 24 columns from every device.
All inputs are finite; a program needn't handle non-finite values.
Results may differ from the reference program's by a relative error of at most 0.0028.
Values may be sent and summed in bfloat16 or wider, within the bound.
No kernel may reach another device: no remote copies, remote signals or barrier semaphores. Data moves between devices by JAX's collectives and lax.ppermute only.
A program may use at most 64 MiB of HBM per device.

```python
import jax
import jax.numpy as jnp
from jax import lax

TRC = 8
LEV = 128
CLAT = 16
CLON = 32
CAP = 64
CHK_DEV = 16
SPANS = 512
NLAT = 64
NLON = 256
N_LAT = 4
N_LON = 8


def make_span_map(key):
    devices = N_LAT * N_LON
    half = devices // 2
    columns = CLAT * CLON
    quarter = CAP // 4
    base = jax.random.fold_in(key, 911)
    key_extra, key_order = jax.random.split(base, 2)
    extra = jax.random.randint(key_extra, (half, CHK_DEV), 0, 2 * quarter + 1)
    amount = quarter + extra
    amount = amount.at[0].set(3 * quarter)
    counts = jnp.concatenate([amount, CAP - amount], axis=0).reshape(-1).astype(jnp.int32)
    ends = jnp.cumsum(counts)
    starts = ends - counts
    total = devices * columns
    positions = jnp.arange(total, dtype=jnp.int32)
    span_at = jnp.searchsorted(ends, positions, side='right').astype(jnp.int32)
    slot_at = positions - starts[span_at]
    source = positions % devices
    within = positions // devices
    order_keys = jax.random.split(key_order, devices)
    orders = jax.vmap(lambda single: jax.random.permutation(single, columns))(order_keys)
    local = orders[source, within]
    lat_index = source // N_LON * CLAT + local // CLON
    lon_index = source % N_LON * CLON + local % CLON
    span_map = jnp.zeros((CLAT * N_LAT, CLON * N_LON), jnp.int32).at[lat_index, lon_index].set(span_at)
    slot_map = jnp.zeros((CLAT * N_LAT, CLON * N_LON), jnp.int32).at[lat_index, lon_index].set(slot_at)
    return (span_map, slot_map)


def draw_span_of(key, part):
    return make_span_map(key)[0]


def draw_slot_of(key, part):
    return make_span_map(key)[1]


def draw_inverses(key, part):
    total = CHK_DEV * N_LAT * N_LON
    key_off, key_diag = jax.random.split(jax.random.fold_in(key, 313))
    identity = jnp.eye(LEV, dtype=jnp.float32)
    off = 0.45 * jax.random.normal(key_off, (total, LEV, LEV), jnp.float32) / jnp.sqrt(jnp.float32(LEV))
    diag = jax.random.uniform(key_diag, (total, LEV, 1), jnp.float32, 0.9, 1.3)
    return (identity * diag + off).astype(jnp.bfloat16)


def shard_levels(rng, dims, cuts, least, high):
    level, own = 1.0, jax.random.fold_in(rng, 6)
    for position, shards_of in cuts:
        steps = jnp.exp(jax.random.uniform(jax.random.fold_in(own, position), (shards_of,), jnp.float32, least / len(cuts), high / len(cuts)))
        level = level * jnp.repeat(steps, dims[position] // shards_of).reshape([-1 if axis == position else 1 for axis in range(len(dims))])
    return level


def gaussian(key, extent, deviation, limit, pieces=(), kind=jnp.bfloat16):
    drawn = jax.random.normal(key, extent, jnp.float32) * deviation
    if len(pieces) > 0:
        drawn = shard_levels(key, extent, pieces, -0.22, 0.18) * drawn
    return jnp.clip(drawn, min=-limit, max=limit).astype(kind)


def setup_inputs(seed: int = 0) -> dict:
    arg_keys = jax.random.split(jax.random.key(seed), 7)
    return {
        "tracers": gaussian(arg_keys[0], (NLAT, NLON, TRC * LEV), 1.0, 6.0, ((0, 4), (1, 8))),
        "east_wind": jnp.clip(jax.random.uniform(arg_keys[1], (NLAT, NLON, LEV), jnp.float32, -0.5, 0.5) * shard_levels(arg_keys[1], (NLAT, NLON, LEV), ((0, 4), (1, 8)), -0.4, 0.0), -0.5, 0.5).astype(jnp.bfloat16),
        "north_wind": jnp.clip(jax.random.uniform(arg_keys[2], (NLAT, NLON, LEV), jnp.float32, -0.5, 0.5) * shard_levels(arg_keys[2], (NLAT, NLON, LEV), ((0, 4), (1, 8)), -0.4, 0.0), -0.5, 0.5).astype(jnp.bfloat16),
        "span_of": draw_span_of(jax.random.fold_in(arg_keys[6], 71), 0),
        "slot_of": draw_slot_of(jax.random.fold_in(arg_keys[6], 71), 0),
        "inverses": draw_inverses(jax.random.fold_in(arg_keys[6], 71), 0),
    }


DIFFUSE = 0.1


def dynamics_one(args):
    field, east, north = args
    field = field.astype(jnp.float32)
    east = east.astype(jnp.float32)
    north = north.astype(jnp.float32)
    field_east = jnp.roll(field, -1, axis=1)
    wind_east = 0.5 * (east + jnp.roll(east, -1, axis=1))
    flux_x = wind_east * (0.5 * (field + field_east)) - DIFFUSE * (field_east - field)
    tend_x = -(flux_x - jnp.roll(flux_x, 1, axis=1))
    zero_row = jnp.zeros_like(field[:1])
    field_north = jnp.concatenate([field[1:], zero_row], axis=0)
    wind_north = jnp.concatenate([north[1:], zero_row], axis=0)
    flux_y = 0.5 * (north + wind_north) * (0.5 * (field + field_north)) - DIFFUSE * (field_north - field)
    rows = jnp.arange(NLAT, dtype=jnp.int32)
    flux_y = jnp.where((rows < NLAT - 1)[:, None, None], flux_y, jnp.float32(0.0))
    flux_s = jnp.concatenate([zero_row, flux_y[:-1]], axis=0)
    tend_y = -(flux_y - flux_s)
    return tend_x + tend_y


def reference(tracers, east_wind, north_wind, span_of, slot_of, inverses):
    fields = tracers.reshape(NLAT, NLON, TRC, LEV).transpose(2, 0, 1, 3)

    def per_tracer(field):
        return dynamics_one((field, east_wind, north_wind))

    dynamics = lax.map(per_tracer, fields).transpose(1, 2, 0, 3).reshape(NLAT * NLON, TRC * LEV)
    state = (tracers.reshape(NLAT * NLON, TRC * LEV).astype(jnp.float32) + dynamics).astype(jnp.bfloat16)
    ncols = NLAT * NLON
    padded = jnp.concatenate([state, jnp.zeros((1, TRC * LEV), jnp.bfloat16)], axis=0)
    slot_ids = (span_of * CAP + slot_of).reshape(-1).astype(jnp.int32)
    col_of_slot = jnp.full((SPANS * CAP,), ncols, jnp.int32).at[slot_ids].set(jnp.arange(ncols, dtype=jnp.int32))
    groups = col_of_slot.reshape(N_LAT * N_LON, CHK_DEV * CAP)
    inv_groups = inverses.reshape(N_LAT * N_LON, CHK_DEV, LEV, LEV)

    def per_owner(args):
        columns, matrices = args
        block = padded[columns].reshape(CHK_DEV, CAP, TRC, LEV).astype(jnp.float32)
        relaxed = jnp.einsum("clm,cstm->cstl", matrices.astype(jnp.float32), block)
        return (relaxed - block).astype(jnp.bfloat16).reshape(CHK_DEV * CAP, TRC * LEV)

    physics_slots = lax.map(per_owner, (groups, inv_groups)).reshape(SPANS * CAP, TRC * LEV)
    physics = physics_slots[slot_ids]
    tendency = dynamics + physics.astype(jnp.float32)
    return tendency.reshape(NLAT, NLON, TRC * LEV)
```

```python
import functools

import jax
import jax.numpy as jnp
from jax import lax
from jax.experimental import pallas as pl
from jax.experimental.pallas import tpu as pltpu
from jax.sharding import Mesh
from jax.sharding import PartitionSpec as P

SLOTS = 48
GROUP = 16
DIFFUSE = 0.1
GROUP_AXES = ("lat", "lo")
LON_AXES = ("hi", "lo")
COUNT_LANE = 127

VMEM = pl.BlockSpec(memory_space=pltpu.VMEM)
SMEM = pl.BlockSpec(memory_space=pltpu.SMEM)


def plan_kernel(cap, me_ref, packed_ref, pos_ref, meta_ref, count):
    me = me_ref[0]
    rows, cells = packed_ref.shape
    peers = meta_ref.shape[0]
    for x in range(peers):
        count[x] = 0

    def row(i, carry):
        for j in range(cells):
            packed = packed_ref[i, j]
            peer = packed >> 8
            rank = count[peer]
            count[peer] = rank + 1
            meta_ref[peer, rank] = packed & 255
            pos_ref[i * cells + j] = (peer ^ me) * cap + rank
        return carry

    lax.fori_loop(0, rows, row, 0)
    for x in range(peers):
        meta_ref[x, COUNT_LANE] = count[x]


def sort_kernel(cap, me_ref, meta_ref, list_ref, count_ref):
    me = me_ref[0]
    spans = count_ref.shape[0]
    for k in range(spans):
        count_ref[k] = 0

    def peer(x, carry):
        base = (x ^ me) * cap

        def column(r, carry):
            k = meta_ref[x, r]
            n = count_ref[k]
            count_ref[k] = n + 1
            list_ref[k * SLOTS + n] = base + r
            return carry

        return lax.fori_loop(0, meta_ref[x, COUNT_LANE], column, carry)

    lax.fori_loop(0, meta_ref.shape[0], peer, 0)

    def pad(k, carry):
        n = count_ref[k]
        last = list_ref[k * SLOTS + jnp.maximum(n - 1, 0)]

        def fill(r, carry):
            list_ref[k * SLOTS + r] = last
            return carry

        return lax.fori_loop(n, (n + GROUP - 1) // GROUP * GROUP, fill, carry)

    lax.fori_loop(0, spans, pad, 0)


def flux_kernel(
    pos_ref,
    open_ref,
    q_ref,
    u_ref,
    v_ref,
    west_ref,
    east_ref,
    south_ref,
    north_ref,
    send_ref,
    dyn_ref,
    cell,
    wind,
    face_x,
    wind_y,
    face_y,
    edge,
    flux_y,
):
    rows, cells, width = q_ref.shape
    levels = u_ref.shape[2]
    tracers = width // levels
    f32 = jnp.float32
    line = (cells + 2) * tracers

    def spread(block, first, count, stride):
        for t in range(tracers):
            cell[pl.ds(first + t, count, stride=stride), :] = block(t).astype(f32)

    lanes = lambda t: slice(t * levels, (t + 1) * levels)
    spread(lambda t: south_ref[:, lanes(t)], tracers, cells, tracers)
    spread(lambda t: north_ref[:, lanes(t)], (rows + 1) * line + tracers, cells, tracers)
    spread(lambda t: west_ref[:, lanes(t)], line, rows, line)
    spread(lambda t: east_ref[:, lanes(t)], line + (cells + 1) * tracers, rows, line)

    def relayout(i, carry):
        spread(
            lambda t: q_ref[i, :, lanes(t)], (i + 1) * line + tracers, cells, tracers
        )
        return carry

    lax.fori_loop(0, rows, relayout, 0)

    edge[0:rows, :] = west_ref[:, width:].astype(f32)
    edge[rows : 2 * rows, :] = east_ref[:, width:].astype(f32)
    stride = face_x.shape[0] // rows

    def faces(i, carry):
        wind[0:1, :] = edge[pl.ds(i, 1), :]
        wind[1 : cells + 1, :] = u_ref[i].astype(f32)
        wind[cells + 1 : cells + 2, :] = edge[pl.ds(rows + i, 1), :]
        face_x[pl.ds(pl.multiple_of(i * stride, 8), stride), :] = 0.25 * (
            wind[0:stride, :] + wind[1 : stride + 1, :]
        )
        return carry

    lax.fori_loop(0, rows, faces, 0)
    wind_y[0:cells, :] = south_ref[:, width:].astype(f32)
    wind_y[cells : (rows + 1) * cells, :] = v_ref[...].reshape(rows * cells, levels).astype(f32)
    wind_y[(rows + 1) * cells :, :] = north_ref[:, width:].astype(f32)
    face_y[...] = 0.25 * (wind_y[: (rows + 1) * cells, :] + wind_y[cells:, :])
    south_open, north_open = open_ref[0].astype(f32), open_ref[1].astype(f32)
    face_y[0:cells, :] = face_y[0:cells, :] * south_open
    face_y[rows * cells :, :] = face_y[rows * cells :, :] * north_open

    def tile(i, j):
        first = (i * (cells + 2) + j) * tracers
        return cell[pl.ds(pl.multiple_of(first, tracers), tracers), :]

    def spread_row(ref, r):
        return jnp.broadcast_to(ref[pl.ds(r, 1), :], (tracers, levels))

    for j in range(cells):
        low, high = tile(0, j + 1), tile(1, j + 1)
        flux_y[j * tracers : (j + 1) * tracers, :] = spread_row(face_y, j) * (low + high) - (
            DIFFUSE * south_open
        ) * (high - low)

    def row(i, carry):
        diffuse_y = DIFFUSE * jnp.where(i == rows - 1, north_open, 1.0)
        here = tile(i + 1, 1)
        last = tile(i + 1, 0)
        flux_w = spread_row(face_x, i * stride) * (last + here) - DIFFUSE * (here - last)
        for j in range(cells):
            after = tile(i + 1, j + 2)
            flux_e = spread_row(face_x, i * stride + j + 1) * (here + after) - DIFFUSE * (
                after - here
            )
            above = tile(i + 2, j + 1)
            flux_n = spread_row(face_y, (i + 1) * cells + j) * (here + above) - diffuse_y * (
                above - here
            )
            flux_s = flux_y[j * tracers : (j + 1) * tracers, :]
            flux_y[j * tracers : (j + 1) * tracers, :] = flux_n
            dyn = (flux_w - flux_e) + (flux_s - flux_n)
            column = i * cells + j
            dyn_ref[pl.ds(pl.multiple_of(column * tracers, tracers), tracers), :] = dyn
            send_ref[pos_ref[column]] = (here + dyn).astype(jnp.bfloat16)
            here, flux_w = after, flux_e
        return carry

    lax.fori_loop(0, rows, row, 0)


def relax_kernel(list_ref, count_ref, x_ref, own_ref, pair_ref, y_ref):
    tracers, levels = x_ref.shape[1:]
    owned = own_ref.shape[0]

    def relax(w_ref, first):
        def span(k, carry):
            n = count_ref[first + k]
            for part in range(SLOTS // GROUP):

                @pl.when(n > part * GROUP)
                def _():
                    base = (first + k) * SLOTS + part * GROUP
                    at = [list_ref[base + c] for c in range(GROUP)]
                    x = jnp.concatenate([x_ref[a].astype(jnp.float32) for a in at], axis=0)
                    y = lax.dot_general(
                        x.astype(jnp.bfloat16),
                        w_ref[k],
                        (((1,), (1,)), ((), ())),
                        preferred_element_type=jnp.float32,
                    )
                    y = y - x
                    for c, a in enumerate(at):
                        y_ref[a] = y[c * tracers : (c + 1) * tracers].astype(jnp.bfloat16)

            return carry

        lax.fori_loop(0, owned, span, 0)

    relax(own_ref, 0)
    relax(pair_ref, owned)


def finish_kernel(pos_ref, y_ref, dyn_ref, out_ref, total):
    rows, cells, width = out_ref.shape
    tracers, levels = y_ref.shape[1:]
    first = pl.program_id(0) * rows * cells

    def row(i, carry):
        for j in range(cells):
            column = i * cells + j
            at = pl.multiple_of(column * tracers, tracers)
            total[j * tracers : (j + 1) * tracers, :] = dyn_ref[pl.ds(at, tracers), :] + y_ref[
                pos_ref[first + column]
            ].astype(jnp.float32)
        for t in range(tracers):
            out_ref[i, :, t * levels : (t + 1) * levels] = total[
                pl.ds(t, cells, stride=tracers), :
            ]
        return carry

    lax.fori_loop(0, rows, row, 0)


def shift(x, axis, by, closed):
    count = lax.axis_size(axis)
    pairs = [(i, (i + by) % count) for i in range(count) if closed or 0 <= i + by < count]
    return lax.ppermute(x, axis, pairs)


def shards(tracers, east_wind, north_wind, span_of, slot_of, inverses):
    levels = east_wind.shape[2]
    rows, cells, width = tracers.shape
    kinds = width // levels
    columns = rows * cells
    lats, lows = lax.axis_size("lat"), lax.axis_size("lo")
    lons = lax.axis_size("hi") * lows
    peers = lats * lows
    owned = inverses.shape[0]
    cap = 2 * (3 * columns // (2 * lats * lons))
    lat, hi, lo = lax.axis_index("lat"), lax.axis_index("hi"), lax.axis_index("lo")
    me = (lat * lows + lo).astype(jnp.int32)
    me_arg = me.reshape(1)

    lon_edge = lambda j: jnp.concatenate([tracers[:, j, :], east_wind[:, j, :]], axis=1)
    lat_edge = lambda i: jnp.concatenate([tracers[i], north_wind[i]], axis=1)
    west = shift(lon_edge(cells - 1), LON_AXES, 1, True)
    east = shift(lon_edge(0), LON_AXES, -1, True)
    south = shift(lat_edge(rows - 1), "lat", 1, False)
    north = shift(lat_edge(0), "lat", -1, False)
    pair = lax.ppermute(inverses, "hi", [(0, 1), (1, 0)])

    owner = span_of // owned
    owner_lon = owner % lons
    peer = (owner // lons * lows + owner_lon % lows) ^ me
    local = jnp.where(owner_lon // lows == hi, 0, owned) + span_of % owned
    packed = peer * 256 + local

    pos, meta = pl.pallas_call(
        functools.partial(plan_kernel, cap),
        out_shape=(
            jax.ShapeDtypeStruct((columns,), jnp.int32),
            jax.ShapeDtypeStruct((peers, 128), jnp.int32),
        ),
        in_specs=[SMEM, SMEM],
        out_specs=(SMEM, SMEM),
        scratch_shapes=[pltpu.SMEM((peers,), jnp.int32)],
        name="plan",
    )(me_arg, packed)

    open_faces = jnp.stack([lat > 0, lat < lats - 1]).astype(jnp.int32)
    stride = (cells + 1 + 7) // 8 * 8
    f32 = jnp.float32
    send, dyn = pl.pallas_call(
        flux_kernel,
        out_shape=(
            jax.ShapeDtypeStruct((peers * cap, kinds, levels), jnp.bfloat16),
            jax.ShapeDtypeStruct((columns * kinds, levels), f32),
        ),
        in_specs=[SMEM, SMEM] + [VMEM] * 7,
        out_specs=(VMEM, VMEM),
        scratch_shapes=[
            pltpu.VMEM(((rows + 2) * (cells + 2) * kinds, levels), f32),
            pltpu.VMEM((stride + 8, levels), f32),
            pltpu.VMEM((rows * stride, levels), f32),
            pltpu.VMEM(((rows + 2) * cells, levels), f32),
            pltpu.VMEM(((rows + 1) * cells, levels), f32),
            pltpu.VMEM((2 * rows, levels), f32),
            pltpu.VMEM((cells * kinds, levels), f32),
        ],
        compiler_params=pltpu.CompilerParams(vmem_limit_bytes=24 << 20),
        name="flux",
    )(pos, open_faces, tracers, east_wind, north_wind, west, east, south, north)

    def exchange(x):
        x = x.reshape(peers, cap, kinds, levels)
        x = lax.all_to_all(x, GROUP_AXES, split_axis=0, concat_axis=0, tiled=True)
        return x.reshape(peers * cap, kinds, levels)

    send, meta = lax.optimization_barrier((send, meta))
    arrived = exchange(send)
    bits = [(axis, b) for axis, n in (("lat", lats), ("lo", lows)) for b in reversed(range(n.bit_length() - 1))]
    meta = meta.reshape((2,) * len(bits) + (128,))
    for axis, b in bits:
        n = lax.axis_size(axis)
        other = lax.ppermute(meta[1], axis, [(i, i ^ (1 << b)) for i in range(n)])
        meta = jnp.stack([meta[0], other], axis=-2)
    meta = meta.reshape(peers, 128)

    spans = 2 * owned
    order, count = pl.pallas_call(
        functools.partial(sort_kernel, cap),
        out_shape=(
            jax.ShapeDtypeStruct((spans * SLOTS,), jnp.int32),
            jax.ShapeDtypeStruct((spans,), jnp.int32),
        ),
        in_specs=[SMEM, SMEM],
        out_specs=(SMEM, SMEM),
        name="sort",
    )(me_arg, meta)

    physics = pl.pallas_call(
        relax_kernel,
        out_shape=jax.ShapeDtypeStruct((peers * cap, kinds, levels), jnp.bfloat16),
        in_specs=[SMEM, SMEM, VMEM, VMEM, VMEM],
        out_specs=VMEM,
        compiler_params=pltpu.CompilerParams(vmem_limit_bytes=16 << 20),
        name="relax",
    )(order, count, arrived, inverses, pair)

    returned = exchange(physics)
    step = 4
    return pl.pallas_call(
        finish_kernel,
        out_shape=jax.ShapeDtypeStruct((rows, cells, width), f32),
        grid=(rows // step,),
        in_specs=[
            SMEM,
            pl.BlockSpec((peers * cap, kinds, levels), lambda i: (0, 0, 0)),
            pl.BlockSpec((step * cells * kinds, levels), lambda i: (i, 0)),
        ],
        out_specs=pl.BlockSpec((step, cells, width), lambda i: (i, 0, 0)),
        scratch_shapes=[pltpu.VMEM((cells * kinds, levels), f32)],
        compiler_params=pltpu.CompilerParams(vmem_limit_bytes=16 << 20),
        name="finish",
    )(pos, returned, dyn)


def solution(mesh):
    lats, lons = mesh.devices.shape
    split = Mesh(mesh.devices.reshape(lats, 2, lons // 2), ("lat", "hi", "lo"))
    block = P("lat", LON_AXES, None)
    in_specs = (
        block,
        block,
        block,
        P("lat", LON_AXES),
        P("lat", LON_AXES),
        P(("lat", "hi", "lo"), None, None),
    )
    return jax.shard_map(shards, mesh=split, in_specs=in_specs, out_specs=block, check_vma=False)
```

```python
import functools

import jax
import jax.numpy as jnp
from jax import lax
from jax.experimental import pallas as pl
from jax.experimental.pallas import tpu as pltpu
from jax.sharding import Mesh
from jax.sharding import PartitionSpec as P

SLOTS = 48
DIFFUSE = 0.1
GROUP_AXES = ("lat", "lo")
LON_AXES = ("hi", "lo")

VMEM = pl.BlockSpec(memory_space=pltpu.VMEM)
ANY = pl.BlockSpec(memory_space=pl.ANY)
SMEM = pl.BlockSpec(memory_space=pltpu.SMEM)


def log2(n):
    return n.bit_length() - 1


def edge_kernel(q_hbm, u_hbm, v_hbm, first_ref, last_ref, low_ref, high_ref, q_side, u_side, wide, sems):
    rows, cells, width = q_hbm.shape
    side = q_side.shape[2]
    copies = []

    def copy(source, target):
        copies.append(pltpu.make_async_copy(source, target, sems.at[len(copies)]))
        copies[-1].start()

    copy(q_hbm.at[:, 0:side, :], q_side.at[0])
    copy(u_hbm.at[:, 0:side, :], u_side.at[0])
    copy(q_hbm.at[:, cells - side : cells, :], q_side.at[1])
    copy(u_hbm.at[:, cells - side : cells, :], u_side.at[1])
    copy(q_hbm.at[0], low_ref.at[:, 0:width])
    copy(v_hbm.at[0], low_ref.at[:, width:])
    copy(q_hbm.at[rows - 1], high_ref.at[:, 0:width])
    copy(v_hbm.at[rows - 1], high_ref.at[:, width:])
    for c in copies:
        c.wait()
    for n, (ref, j) in enumerate(((first_ref, 0), (last_ref, side - 1))):
        for i in range(rows):
            wide[i : i + 1, 0:width] = q_side[n, i].astype(jnp.float32)[j : j + 1]
            wide[i : i + 1, width:] = u_side[n, i].astype(jnp.float32)[j : j + 1]
        ref[...] = wide[...].astype(jnp.bfloat16)


def plan(place_ref, span_ref, slot_ref, send_ref, pos_ref, member, pos, cap, owned, lons, lows):
    rows, cells = span_ref.shape
    stored = cap + 1
    peers = send_ref.shape[0] // stored
    f32, bf16 = jnp.float32, jnp.bfloat16
    span, slot = span_ref[...], slot_ref[...]
    owner = span >> log2(owned)
    owner_lon = owner & (lons - 1)
    peer = ((owner >> log2(lons)) << log2(lows)) + (owner_lon & (lows - 1))
    far = (owner_lon >> log2(lows)) != place_ref[0]
    local = (span & (owned - 1)) + jnp.where(far, owned, 0)
    iota = lambda shape, axis: lax.broadcasted_iota(jnp.int32, shape, axis)
    for i in range(rows):
        member[i * peers : (i + 1) * peers, :] = jnp.where(
            iota((peers, cells), 0) == peer[i : i + 1], 1.0, 0.0
        )
    hot = member[...].astype(bf16)
    dot = functools.partial(jnp.dot, preferred_element_type=f32)
    within = dot(hot, (iota((cells, cells), 0) < iota((cells, cells), 1)).astype(f32).astype(bf16))
    pairs = (rows * peers, rows * peers)
    to, of = iota(pairs, 0), iota(pairs, 1)
    same = (to & (peers - 1)) == (of & (peers - 1))
    lower = jnp.where(same & (of < (to & -peers)), 1.0, 0.0).astype(bf16)
    before = within + jnp.sum(dot(lower, hot), axis=1, keepdims=True)
    before = before * member[...]
    lists = jnp.zeros((3 * peers, 128), f32)
    for i in range(rows):
        block = slice(i * peers, (i + 1) * peers)
        rank = jnp.sum(before[block], axis=0, keepdims=True).astype(jnp.int32)
        pos[i : i + 1, 0:cells] = peer[i : i + 1] * stored + rank
        pos_ref[i : i + 1, 0:cells] = peer[i : i + 1] * cap + rank
        chosen = jnp.where(iota((128, cells), 0) == rank, 1.0, 0.0).astype(bf16)
        mine = member[block]
        values = jnp.concatenate(
            [mine * local[i : i + 1].astype(f32), mine * slot[i : i + 1].astype(f32), mine], axis=0
        )
        lists = lists + lax.dot_general(
            values.astype(bf16), chosen, (((1,), (1,)), ((), ())), preferred_element_type=f32
        )
    spans = jnp.where(lists[2 * peers :] > 0.5, lists[:peers], 2.0 * owned)
    slots = lists[peers : 2 * peers]
    tile = send_ref.shape[1:]
    for p in range(peers):
        send_ref[p * stored + cap] = jnp.where(
            iota(tile, 0) == 0,
            jnp.broadcast_to(spans[p : p + 1], tile),
            jnp.broadcast_to(slots[p : p + 1], tile),
        ).astype(bf16)


def flux_kernel(
    cap,
    owned,
    lons,
    lows,
    place_ref,
    span_ref,
    slot_ref,
    q_ref,
    u_hbm,
    v_hbm,
    west_ref,
    east_ref,
    south_ref,
    north_ref,
    send_ref,
    pos_ref,
    dyn_hbm,
    member,
    pos,
    pos_s,
    u_ref,
    v_ref,
    dyn_ref,
    sems,
    row_sems,
    cell,
    wind,
    face_x,
    wind_y,
    face_y,
    edge,
    flux_y,
):
    rows, cells, width = q_ref.shape
    levels = u_ref.shape[2]
    tracers = width // levels
    f32 = jnp.float32
    line = (cells + 2) * tracers
    u_copy = pltpu.make_async_copy(u_hbm, u_ref, sems.at[0])
    v_copy = pltpu.make_async_copy(v_hbm, v_ref, sems.at[1])
    u_copy.start()
    v_copy.start()
    plan(place_ref, span_ref, slot_ref, send_ref, pos_ref, member, pos, cap, owned, lons, lows)
    pos_copy = pltpu.make_async_copy(pos, pos_s, sems.at[2])
    pos_copy.start()

    def spread(block, first, count, stride):
        for t in range(tracers):
            cell[pl.ds(first + t, count, stride=stride), :] = block(t).astype(f32)

    lanes = lambda t: slice(t * levels, (t + 1) * levels)
    spread(lambda t: south_ref[:, lanes(t)], tracers, cells, tracers)
    spread(lambda t: north_ref[:, lanes(t)], (rows + 1) * line + tracers, cells, tracers)
    spread(lambda t: west_ref[:, lanes(t)], line, rows, line)
    spread(lambda t: east_ref[:, lanes(t)], line + (cells + 1) * tracers, rows, line)

    def relayout(i, carry):
        spread(
            lambda t: q_ref[i, :, lanes(t)], (i + 1) * line + tracers, cells, tracers
        )
        return carry

    lax.fori_loop(0, rows, relayout, 0)

    u_copy.wait()
    v_copy.wait()
    edge[0:rows, :] = west_ref[:, width:].astype(f32)
    edge[rows : 2 * rows, :] = east_ref[:, width:].astype(f32)
    stride = face_x.shape[0] // rows

    def faces(i, carry):
        wind[0:1, :] = edge[pl.ds(i, 1), :]
        wind[1 : cells + 1, :] = u_ref[i].astype(f32)
        wind[cells + 1 : cells + 2, :] = edge[pl.ds(rows + i, 1), :]
        face_x[pl.ds(pl.multiple_of(i * stride, 8), stride), :] = 0.25 * (
            wind[0:stride, :] + wind[1 : stride + 1, :]
        )
        return carry

    lax.fori_loop(0, rows, faces, 0)
    wind_y[0:cells, :] = south_ref[:, width:].astype(f32)
    wind_y[cells : (rows + 1) * cells, :] = v_ref[...].reshape(rows * cells, levels).astype(f32)
    wind_y[(rows + 1) * cells :, :] = north_ref[:, width:].astype(f32)
    face_y[...] = 0.25 * (wind_y[: (rows + 1) * cells, :] + wind_y[cells:, :])
    south_open, north_open = place_ref[1].astype(f32), place_ref[2].astype(f32)
    face_y[0:cells, :] = face_y[0:cells, :] * south_open
    face_y[rows * cells :, :] = face_y[rows * cells :, :] * north_open

    def tile(i, j):
        first = (i * (cells + 2) + j) * tracers
        return cell[pl.ds(pl.multiple_of(first, tracers), tracers), :]

    def spread_row(ref, r):
        return jnp.broadcast_to(ref[pl.ds(r, 1), :], (tracers, levels))

    for j in range(cells):
        low, high = tile(0, j + 1), tile(1, j + 1)
        flux_y[j * tracers : (j + 1) * tracers, :] = spread_row(face_y, j) * (low + high) - (
            DIFFUSE * south_open
        ) * (high - low)

    pos_copy.wait()

    def dyn_copy(i):
        rows_i = pl.ds(pl.multiple_of(i * cells * tracers, tracers), cells * tracers)
        return pltpu.make_async_copy(dyn_ref.at[rows_i], dyn_hbm.at[rows_i], row_sems.at[i])

    def row(i, carry):
        diffuse_y = DIFFUSE * jnp.where(i == rows - 1, north_open, 1.0)
        here = tile(i + 1, 1)
        last = tile(i + 1, 0)
        flux_w = spread_row(face_x, i * stride) * (last + here) - DIFFUSE * (here - last)
        for j in range(cells):
            after = tile(i + 1, j + 2)
            flux_e = spread_row(face_x, i * stride + j + 1) * (here + after) - DIFFUSE * (
                after - here
            )
            above = tile(i + 2, j + 1)
            flux_n = spread_row(face_y, (i + 1) * cells + j) * (here + above) - diffuse_y * (
                above - here
            )
            flux_s = flux_y[j * tracers : (j + 1) * tracers, :]
            flux_y[j * tracers : (j + 1) * tracers, :] = flux_n
            dyn = (flux_w - flux_e) + (flux_s - flux_n)
            column = i * cells + j
            dyn_ref[pl.ds(pl.multiple_of(column * tracers, tracers), tracers), :] = dyn
            send_ref[pos_s[i, j]] = (here + dyn).astype(jnp.bfloat16)
            here, flux_w = after, flux_e
        dyn_copy(i).start()
        return carry

    lax.fori_loop(0, rows, row, 0)

    def drain(i, carry):
        dyn_copy(i).wait()
        return carry

    lax.fori_loop(0, rows, drain, 0)


def relax_kernel(x_ref, own_ref, near_ref, far_ref, y_ref, pos, pos_s, sem, slots):
    tracers, levels = x_ref.shape[1:]
    owned = own_ref.shape[0]
    peers, lanes = pos.shape
    stored = x_ref.shape[0] // peers
    cap = stored - 1
    f32 = jnp.float32
    for p in range(peers):
        listed = x_ref[p * stored + cap].astype(f32)
        pos[p : p + 1, :] = (listed[0:1] * SLOTS + listed[1:2]).astype(jnp.int32)
    copy = pltpu.make_async_copy(pos, pos_s, sem)
    copy.start()
    copy.wait()

    def place(at):
        return pl.ds(pl.multiple_of(at * tracers, tracers), tracers)

    def scatter(p, carry):
        for r in range(cap):
            slots[place(pos_s[p, r]), :] = x_ref[p * stored + r].astype(f32)
        return carry

    lax.fori_loop(0, peers, scatter, 0)
    block = SLOTS * tracers

    def relax(w_ref, first):
        def span(k, carry):
            at = pl.ds(pl.multiple_of((first + k) * block, block), block)
            x = slots[at, :]
            y = lax.dot_general(
                x.astype(jnp.bfloat16),
                w_ref[k],
                (((1,), (1,)), ((), ())),
                preferred_element_type=f32,
            )
            slots[at, :] = y - x
            return carry

        lax.fori_loop(0, w_ref.shape[0], span, 0, unroll=2)

    relax(own_ref, 0)
    relax(near_ref, owned)
    relax(far_ref, owned + near_ref.shape[0])

    def gather(p, carry):
        for r in range(cap):
            y_ref[p * cap + r] = slots[place(pos_s[p, r]), :].astype(jnp.bfloat16)
        return carry

    lax.fori_loop(0, peers, gather, 0)


def finish_kernel(pos_ref, y_ref, dyn_ref, out_ref, total):
    rows, cells, width = out_ref.shape
    tracers, levels = y_ref.shape[1:]
    first = pl.program_id(0) * rows

    def row(i, carry):
        for j in range(cells):
            column = i * cells + j
            at = pl.multiple_of(column * tracers, tracers)
            total[j * tracers : (j + 1) * tracers, :] = dyn_ref[pl.ds(at, tracers), :] + y_ref[
                pos_ref[first + i, j]
            ].astype(jnp.float32)
        for t in range(tracers):
            out_ref[i, :, t * levels : (t + 1) * levels] = total[
                pl.ds(t, cells, stride=tracers), :
            ]
        return carry

    lax.fori_loop(0, rows, row, 0)


def shift(x, axis, by, closed):
    count = lax.axis_size(axis)
    pairs = [(i, (i + by) % count) for i in range(count) if closed or 0 <= i + by < count]
    return lax.ppermute(x, axis, pairs)


def shards(tracers, east_wind, north_wind, span_of, slot_of, inverses):
    levels = east_wind.shape[2]
    rows, cells, width = tracers.shape
    kinds = width // levels
    columns = rows * cells
    lats, lows = lax.axis_size("lat"), lax.axis_size("lo")
    lons = lax.axis_size("hi") * lows
    peers = lats * lows
    owned = inverses.shape[0]
    cap = 2 * (3 * columns // (2 * lats * lons))
    stored = cap + 1
    lat, hi = lax.axis_index("lat"), lax.axis_index("hi")
    f32, bf16, i32 = jnp.float32, jnp.bfloat16, jnp.int32
    dma = pltpu.SemaphoreType.DMA
    params = lambda mib: pltpu.CompilerParams(vmem_limit_bytes=mib << 20)

    side = 8
    first, last, low, high = pl.pallas_call(
        edge_kernel,
        out_shape=(jax.ShapeDtypeStruct((rows, width + levels), bf16),) * 2
        + (jax.ShapeDtypeStruct((cells, width + levels), bf16),) * 2,
        in_specs=[ANY] * 3,
        out_specs=(VMEM,) * 4,
        scratch_shapes=[
            pltpu.VMEM((2, rows, side, width), bf16),
            pltpu.VMEM((2, rows, side, levels), bf16),
            pltpu.VMEM((rows, width + levels), f32),
            dma((8,)),
        ],
        compiler_params=params(8),
        name="edges",
    )(tracers, east_wind, north_wind)
    south = shift(high, "lat", 1, False)
    north = shift(low, "lat", -1, False)
    west = shift(last, LON_AXES, 1, True)
    east = shift(first, LON_AXES, -1, True)
    swap = lambda x: lax.ppermute(x, "hi", [(0, 1), (1, 0)])
    near = swap(inverses[: owned // 2])
    far = swap(inverses[owned // 2 :])

    place = jnp.stack([hi, lat > 0, lat < lats - 1]).astype(i32)
    stride = (cells + 1 + 7) // 8 * 8
    send, pos, dyn = pl.pallas_call(
        functools.partial(flux_kernel, cap, owned, lons, lows),
        out_shape=(
            jax.ShapeDtypeStruct((peers * stored, kinds, levels), bf16),
            jax.ShapeDtypeStruct((rows, 128), i32),
            jax.ShapeDtypeStruct((columns * kinds, levels), f32),
        ),
        in_specs=[SMEM, VMEM, VMEM, VMEM, ANY, ANY] + [VMEM] * 4,
        out_specs=(VMEM, VMEM, ANY),
        scratch_shapes=[
            pltpu.VMEM((rows * peers, cells), f32),
            pltpu.VMEM((rows, 128), i32),
            pltpu.SMEM((rows, 128), i32),
            pltpu.VMEM((rows, cells, levels), bf16),
            pltpu.VMEM((rows, cells, levels), bf16),
            pltpu.VMEM((columns * kinds, levels), f32),
            dma((3,)),
            dma((rows,)),
            pltpu.VMEM(((rows + 2) * (cells + 2) * kinds, levels), f32),
            pltpu.VMEM((stride + 8, levels), f32),
            pltpu.VMEM((rows * stride, levels), f32),
            pltpu.VMEM(((rows + 2) * cells, levels), f32),
            pltpu.VMEM(((rows + 1) * cells, levels), f32),
            pltpu.VMEM((2 * rows, levels), f32),
            pltpu.VMEM((cells * kinds, levels), f32),
        ],
        compiler_params=params(24),
        name="flux",
    )(place, span_of, slot_of, tracers, east_wind, north_wind, west, east, south, north)

    def exchange(x):
        x = x.reshape(peers, -1, kinds, levels)
        x = lax.all_to_all(x, GROUP_AXES, split_axis=0, concat_axis=0, tiled=True)
        return x.reshape(-1, kinds, levels)

    send, near = lax.optimization_barrier((send, near))
    arrived = exchange(send)
    physics = pl.pallas_call(
        relax_kernel,
        out_shape=jax.ShapeDtypeStruct((peers * cap, kinds, levels), bf16),
        in_specs=[VMEM] * 4,
        out_specs=VMEM,
        scratch_shapes=[
            pltpu.VMEM((peers, 128), i32),
            pltpu.SMEM((peers, 128), i32),
            dma,
            pltpu.VMEM(((2 * owned * SLOTS + 1) * kinds, levels), f32),
        ],
        compiler_params=params(24),
        name="relax",
    )(arrived, inverses, near, far)

    returned = exchange(physics)
    step = 4
    return pl.pallas_call(
        finish_kernel,
        out_shape=jax.ShapeDtypeStruct((rows, cells, width), f32),
        grid=(rows // step,),
        in_specs=[
            SMEM,
            pl.BlockSpec((peers * cap, kinds, levels), lambda i: (0, 0, 0)),
            pl.BlockSpec((step * cells * kinds, levels), lambda i: (i, 0)),
        ],
        out_specs=pl.BlockSpec((step, cells, width), lambda i: (i, 0, 0)),
        scratch_shapes=[pltpu.VMEM((cells * kinds, levels), f32)],
        compiler_params=params(16),
        name="finish",
    )(pos, returned, dyn)


def solution(mesh):
    lats, lons = mesh.devices.shape
    split = Mesh(mesh.devices.reshape(lats, 2, lons // 2), ("lat", "hi", "lo"))
    block = P("lat", LON_AXES, None)
    in_specs = (
        block,
        block,
        block,
        P("lat", LON_AXES),
        P("lat", LON_AXES),
        P(("lat", "hi", "lo"), None, None),
    )
    return jax.shard_map(shards, mesh=split, in_specs=in_specs, out_specs=block, check_vma=False)
```

```python
import functools

import jax
import jax.numpy as jnp
from jax import lax
from jax.experimental import pallas as pl
from jax.experimental.pallas import tpu as pltpu
from jax.sharding import Mesh
from jax.sharding import PartitionSpec as P

FLUX_COST = 10
TURN_COST = 30
SLOTS = 48
DIFFUSE = 0.1
GROUP_AXES = ("lat", "lo")
LON_AXES = ("hi", "lo")

VMEM = pl.BlockSpec(memory_space=pltpu.VMEM)
ANY = pl.BlockSpec(memory_space=pltpu.HBM)
SMEM = pl.BlockSpec(memory_space=pltpu.SMEM)


def log2(n):
    return n.bit_length() - 1


def parities(place, lons):
    return place & 1, (place >> log2(lons)) & 1


def edge_kernel(
    lons, place_ref, q_hbm, u_hbm, v_hbm, lon_a, lon_b, lat_a, lat_b, q_side, u_side, wide, sems
):
    rows, cells, width = q_hbm.shape
    side = q_side.shape[2]
    odd_lon, odd_lat = parities(place_ref[0], lons)
    copies = []

    def copy(source, target):
        copies.append(pltpu.make_async_copy(source, target, sems.at[len(copies)]))
        copies[-1].start()

    for n, odd in enumerate((odd_lon, 1 - odd_lon)):
        near = pl.ds(pl.multiple_of(jnp.where(odd == 1, 0, cells - side), side), side)
        copy(q_hbm.at[:, near, :], q_side.at[n])
        copy(u_hbm.at[:, near, :], u_side.at[n])
    for ref, odd in ((lat_a, odd_lat), (lat_b, 1 - odd_lat)):
        i = jnp.where(odd == 1, 0, rows - 1)
        copy(q_hbm.at[i], ref.at[:, 0:width])
        copy(v_hbm.at[i], ref.at[:, width:])
    for c in copies[:4]:
        c.wait()
    for n, (ref, odd) in enumerate(((lon_a, odd_lon), (lon_b, 1 - odd_lon))):
        first = odd == 1
        for i in range(rows):
            q, u = q_side[n, i].astype(jnp.float32), u_side[n, i].astype(jnp.float32)
            wide[i : i + 1, 0:width] = jnp.where(first, q[0:1], q[side - 1 :])
            wide[i : i + 1, width:] = jnp.where(first, u[0:1], u[side - 1 :])
        ref[...] = wide[...].astype(jnp.bfloat16)
    for c in copies[4:]:
        c.wait()


def plan(place_ref, span_ref, slot_ref, send_ref, pos_ref, member, pos, cap, owned, lons, lows):
    rows, cells = span_ref.shape
    stored = cap + 1
    peers = send_ref.shape[0] // stored
    f32, bf16 = jnp.float32, jnp.bfloat16
    span, slot = span_ref[...], slot_ref[...]
    owner = span >> log2(owned)
    owner_lon = owner & (lons - 1)
    peer = ((owner >> log2(lons)) << log2(lows)) + (owner_lon & (lows - 1))
    far = (owner_lon >> log2(lows)) != ((place_ref[0] >> log2(lows)) & 1)
    local = (span & (owned - 1)) + jnp.where(far, owned, 0)
    iota = lambda shape, axis: lax.broadcasted_iota(jnp.int32, shape, axis)
    for i in range(rows):
        member[i * peers : (i + 1) * peers, :] = jnp.where(
            iota((peers, cells), 0) == peer[i : i + 1], 1.0, 0.0
        )
    hot = member[...].astype(bf16)
    dot = functools.partial(jnp.dot, preferred_element_type=f32)
    within = dot(hot, (iota((cells, cells), 0) < iota((cells, cells), 1)).astype(f32).astype(bf16))
    pairs = (rows * peers, rows * peers)
    to, of = iota(pairs, 0), iota(pairs, 1)
    same = (to & (peers - 1)) == (of & (peers - 1))
    lower = jnp.where(same & (of < (to & -peers)), 1.0, 0.0).astype(bf16)
    before = within + jnp.sum(dot(lower, hot), axis=1, keepdims=True)
    before = before * member[...]
    lists = jnp.zeros((3 * peers, 128), f32)
    for i in range(rows):
        block = slice(i * peers, (i + 1) * peers)
        rank = jnp.sum(before[block], axis=0, keepdims=True).astype(jnp.int32)
        pos[i : i + 1, 0:cells] = peer[i : i + 1] * stored + rank
        pos_ref[i : i + 1, 0:cells] = peer[i : i + 1] * cap + rank
        chosen = jnp.where(iota((128, cells), 0) == rank, 1.0, 0.0).astype(bf16)
        mine = member[block]
        values = jnp.concatenate(
            [mine * local[i : i + 1].astype(f32), mine * slot[i : i + 1].astype(f32), mine], axis=0
        )
        lists = lists + lax.dot_general(
            values.astype(bf16), chosen, (((1,), (1,)), ((), ())), preferred_element_type=f32
        )
    spans = jnp.where(lists[2 * peers :] > 0.5, lists[:peers], 2.0 * owned)
    slots = lists[peers : 2 * peers]
    tile = send_ref.shape[1:]
    for p in range(peers):
        send_ref[p * stored + cap] = jnp.where(
            iota(tile, 0) == 0,
            jnp.broadcast_to(spans[p : p + 1], tile),
            jnp.broadcast_to(slots[p : p + 1], tile),
        ).astype(bf16)


def flux_kernel(
    cap,
    owned,
    lats,
    lons,
    lows,
    place_ref,
    *refs,
):
    sources, (send_ref, pos_ref, dyn_hbm), rest = refs[:9], refs[9:12], refs[12:]
    held, rest = rest[:7], rest[7:]
    (
        sems,
        row_sems,
        member,
        pos,
        pos_s,
        dyn_ref,
        cell,
        wind,
        face_x,
        wind_y,
        face_y,
        edge,
        flux_y,
    ) = rest
    span_ref, slot_ref, q_ref, u_ref, v_ref, lon_ref, lat_ref = held
    west_ref, east_ref = lon_ref.at[0], lon_ref.at[1]
    south_ref, north_ref = lat_ref.at[0], lat_ref.at[1]
    odd_lon, odd_lat = parities(place_ref[0], lons)
    targets = held[:5] + (
        lon_ref.at[1 - odd_lon],
        lon_ref.at[odd_lon],
        lat_ref.at[1 - odd_lat],
        lat_ref.at[odd_lat],
    )
    rows, cells, width = q_ref.shape
    levels = u_ref.shape[2]
    tracers = width // levels
    f32 = jnp.float32
    line = (cells + 2) * tracers
    copies = [pltpu.make_async_copy(a, b, sems.at[n]) for n, (a, b) in enumerate(zip(sources, targets))]
    for copy in copies:
        copy.start()

    def spread(block, first, count, stride):
        for t in range(tracers):
            cell[pl.ds(first + t, count, stride=stride), :] = block(t).astype(f32)

    lanes = lambda t: slice(t * levels, (t + 1) * levels)
    copies[2].wait()

    def relayout(i, carry):
        spread(
            lambda t: q_ref[i, :, lanes(t)], (i + 1) * line + tracers, cells, tracers
        )
        return carry

    lax.fori_loop(0, rows, relayout, 0)
    for copy in copies[:2]:
        copy.wait()
    plan(place_ref, span_ref, slot_ref, send_ref, pos_ref, member, pos, cap, owned, lons, lows)
    pos_copy = pltpu.make_async_copy(pos, pos_s, sems.at[len(copies)])
    pos_copy.start()
    for copy in copies[3:]:
        copy.wait()
    spread(lambda t: south_ref[:, lanes(t)], tracers, cells, tracers)
    spread(lambda t: north_ref[:, lanes(t)], (rows + 1) * line + tracers, cells, tracers)
    spread(lambda t: west_ref[:, lanes(t)], line, rows, line)
    spread(lambda t: east_ref[:, lanes(t)], line + (cells + 1) * tracers, rows, line)

    edge[0:rows, :] = west_ref[:, width:].astype(f32)
    edge[rows : 2 * rows, :] = east_ref[:, width:].astype(f32)
    stride = face_x.shape[0] // rows

    def faces(i, carry):
        wind[0:1, :] = edge[pl.ds(i, 1), :]
        wind[1 : cells + 1, :] = u_ref[i].astype(f32)
        wind[cells + 1 : cells + 2, :] = edge[pl.ds(rows + i, 1), :]
        face_x[pl.ds(pl.multiple_of(i * stride, 8), stride), :] = 0.25 * (
            wind[0:stride, :] + wind[1 : stride + 1, :]
        )
        return carry

    lax.fori_loop(0, rows, faces, 0)
    wind_y[0:cells, :] = south_ref[:, width:].astype(f32)
    wind_y[cells : (rows + 1) * cells, :] = v_ref[...].reshape(rows * cells, levels).astype(f32)
    wind_y[(rows + 1) * cells :, :] = north_ref[:, width:].astype(f32)
    face_y[...] = 0.25 * (wind_y[: (rows + 1) * cells, :] + wind_y[cells:, :])
    lat = place_ref[0] >> log2(lons)
    south_open = jnp.where(lat > 0, 1.0, 0.0)
    north_open = jnp.where(lat < lats - 1, 1.0, 0.0)
    face_y[0:cells, :] = face_y[0:cells, :] * south_open
    face_y[rows * cells :, :] = face_y[rows * cells :, :] * north_open

    def tile(i, j):
        first = (i * (cells + 2) + j) * tracers
        return cell[pl.ds(pl.multiple_of(first, tracers), tracers), :]

    def spread_row(ref, r):
        return jnp.broadcast_to(ref[pl.ds(r, 1), :], (tracers, levels))

    for j in range(cells):
        low, high = tile(0, j + 1), tile(1, j + 1)
        flux_y[j * tracers : (j + 1) * tracers, :] = spread_row(face_y, j) * (low + high) - (
            DIFFUSE * south_open
        ) * (high - low)

    pos_copy.wait()

    def dyn_copy(i):
        rows_i = pl.ds(pl.multiple_of(i * cells * tracers, tracers), cells * tracers)
        return pltpu.make_async_copy(dyn_ref.at[rows_i], dyn_hbm.at[rows_i], row_sems.at[i])

    def row(i, carry):
        diffuse_y = DIFFUSE * jnp.where(i == rows - 1, north_open, 1.0)
        here = tile(i + 1, 1)
        last = tile(i + 1, 0)
        flux_w = spread_row(face_x, i * stride) * (last + here) - DIFFUSE * (here - last)
        for j in range(cells):
            after = tile(i + 1, j + 2)
            flux_e = spread_row(face_x, i * stride + j + 1) * (here + after) - DIFFUSE * (
                after - here
            )
            above = tile(i + 2, j + 1)
            flux_n = spread_row(face_y, (i + 1) * cells + j) * (here + above) - diffuse_y * (
                above - here
            )
            flux_s = flux_y[j * tracers : (j + 1) * tracers, :]
            flux_y[j * tracers : (j + 1) * tracers, :] = flux_n
            dyn = (flux_w - flux_e) + (flux_s - flux_n)
            column = i * cells + j
            dyn_ref[pl.ds(pl.multiple_of(column * tracers, tracers), tracers), :] = dyn
            send_ref[pos_s[i, j]] = (here + dyn).astype(jnp.bfloat16)
            here, flux_w = after, flux_e
        dyn_copy(i).start()
        return carry

    lax.fori_loop(0, rows, row, 0)

    def drain(i, carry):
        dyn_copy(i).wait()
        return carry

    lax.fori_loop(0, rows, drain, 0)


def turn_kernel(own_ref, pair_ref, out_ref):
    owned = own_ref.shape[0]
    for k in range(owned):
        out_ref[k] = own_ref[k].T
        out_ref[owned + k] = pair_ref[k].T


def relax_kernel(x_ref, w_ref, y_ref, pos, pos_s, sem, slots):
    tracers, levels = x_ref.shape[1:]
    peers, lanes = pos.shape
    stored = x_ref.shape[0] // peers
    cap = stored - 1
    f32 = jnp.float32
    for p in range(peers):
        listed = x_ref[p * stored + cap].astype(f32)
        pos[p : p + 1, :] = (listed[0:1] * SLOTS + listed[1:2]).astype(jnp.int32)
    copy = pltpu.make_async_copy(pos, pos_s, sem)
    copy.start()
    copy.wait()

    def place(at):
        return pl.ds(pl.multiple_of(at * tracers, tracers), tracers)

    def scatter(p, carry):
        for r in range(cap):
            slots[place(pos_s[p, r]), :] = x_ref[p * stored + r].astype(f32)
        return carry

    lax.fori_loop(0, peers, scatter, 0)
    block = SLOTS * tracers

    def span(k, carry):
        at = pl.ds(pl.multiple_of(k * block, block), block)
        x = slots[at, :]
        y = jnp.dot(x.astype(jnp.bfloat16), w_ref[k], preferred_element_type=f32)
        slots[at, :] = y - x
        return carry

    lax.fori_loop(0, w_ref.shape[0], span, 0, unroll=8)

    def gather(p, carry):
        for r in range(cap):
            y_ref[p * cap + r] = slots[place(pos_s[p, r]), :].astype(jnp.bfloat16)
        return carry

    lax.fori_loop(0, peers, gather, 0)


def finish_kernel(pos_ref, y_ref, dyn_ref, out_hbm, total, out, sems):
    rows, cells, width = out.shape
    tracers, levels = y_ref.shape[1:]

    def copy(i):
        return pltpu.make_async_copy(out.at[i], out_hbm.at[i], sems.at[i])

    def row(i, carry):
        for j in range(cells):
            at = pl.multiple_of((i * cells + j) * tracers, tracers)
            total[j * tracers : (j + 1) * tracers, :] = dyn_ref[pl.ds(at, tracers), :] + y_ref[
                pos_ref[i, j]
            ].astype(jnp.float32)
        for t in range(tracers):
            out[i, :, t * levels : (t + 1) * levels] = total[pl.ds(t, cells, stride=tracers), :]
        copy(i).start()
        return carry

    lax.fori_loop(0, rows, row, 0)

    def drain(i, carry):
        copy(i).wait()
        return carry

    lax.fori_loop(0, rows, drain, 0)


def in_pairs(x, axis, first):
    count = lax.axis_size(axis)
    pairs = [(i % count, (i + 1) % count) for i in range(first, count + first, 2)]
    return lax.ppermute(x, axis, pairs + [(b, a) for a, b in pairs])


def shards(tracers, east_wind, north_wind, span_of, slot_of, inverses):
    levels = east_wind.shape[2]
    rows, cells, width = tracers.shape
    kinds = width // levels
    columns = rows * cells
    lats, lows = lax.axis_size("lat"), lax.axis_size("lo")
    lons = lax.axis_size("hi") * lows
    peers = lats * lows
    owned = inverses.shape[0]
    cap = 2 * (3 * columns // (2 * lats * lons))
    stored = cap + 1
    f32, bf16, i32 = jnp.float32, jnp.bfloat16, jnp.int32
    dma = pltpu.SemaphoreType.DMA
    params = lambda mib: pltpu.CompilerParams(vmem_limit_bytes=mib << 20)

    side = 8
    place = lax.axis_index(("lat", "hi", "lo")).astype(i32).reshape(1)
    lon_a, lon_b, lat_a, lat_b = pl.pallas_call(
        functools.partial(edge_kernel, lons),
        out_shape=(jax.ShapeDtypeStruct((rows, width + levels), bf16),) * 2
        + (jax.ShapeDtypeStruct((cells, width + levels), bf16),) * 2,
        in_specs=[SMEM] + [ANY] * 3,
        out_specs=(VMEM,) * 4,
        scratch_shapes=[
            pltpu.VMEM((2, rows, side, width), bf16),
            pltpu.VMEM((2, rows, side, levels), bf16),
            pltpu.VMEM((rows, width + levels), f32),
            dma((8,)),
        ],
        compiler_params=params(62),
        name="edges",
    )(place, tracers, east_wind, north_wind)
    lon_a, lon_b = in_pairs(lon_a, LON_AXES, 0), in_pairs(lon_b, LON_AXES, 1)
    lat_a, lat_b = in_pairs(lat_a, "lat", 0), in_pairs(lat_b, "lat", 1)
    matrices, lon_a, lon_b = lax.optimization_barrier((inverses, lon_a, lon_b))
    pair = lax.ppermute(matrices, "hi", [(0, 1), (1, 0)])

    stride = (cells + 1 + 7) // 8 * 8
    fields = (span_of, slot_of, tracers, east_wind, north_wind, lon_a, lon_b, lat_a, lat_b)
    held = [(x.shape, x.dtype) for x in fields[:5]] + [((2,) + x.shape, x.dtype) for x in (lon_a, lat_a)]
    cost = lambda us: pl.CostEstimate(flops=us * 1_000_000_000, bytes_accessed=1 << 20, transcendentals=0)
    send, pos, dyn = pl.pallas_call(
        functools.partial(flux_kernel, cap, owned, lats, lons, lows),
        out_shape=(
            jax.ShapeDtypeStruct((peers * stored, kinds, levels), bf16),
            jax.ShapeDtypeStruct((rows, 128), i32),
            jax.ShapeDtypeStruct((columns * kinds, levels), f32),
        ),
        in_specs=[SMEM] + [ANY] * 9,
        out_specs=(VMEM, VMEM, ANY),
        scratch_shapes=[pltpu.VMEM(*x) for x in held]
        + [
            dma((10,)),
            dma((rows,)),
            pltpu.VMEM((rows * peers, cells), f32),
            pltpu.VMEM((rows, 128), i32),
            pltpu.SMEM((rows, 128), i32),
            pltpu.VMEM((columns * kinds, levels), f32),
            pltpu.VMEM(((rows + 2) * (cells + 2) * kinds, levels), f32),
            pltpu.VMEM((stride + 8, levels), f32),
            pltpu.VMEM((rows * stride, levels), f32),
            pltpu.VMEM(((rows + 2) * cells, levels), f32),
            pltpu.VMEM(((rows + 1) * cells, levels), f32),
            pltpu.VMEM((2 * rows, levels), f32),
            pltpu.VMEM((cells * kinds, levels), f32),
        ],
        compiler_params=params(62),
        cost_estimate=cost(FLUX_COST),
        name="flux",
    )(place, *fields)

    def exchange(x):
        x = x.reshape(peers, -1, kinds, levels)
        x = lax.all_to_all(x, GROUP_AXES, split_axis=0, concat_axis=0, tiled=True)
        return x.reshape(-1, kinds, levels)

    arrived = exchange(send)
    turned = pl.pallas_call(
        turn_kernel,
        out_shape=jax.ShapeDtypeStruct((2 * owned, levels, levels), bf16),
        in_specs=[VMEM] * 2,
        out_specs=VMEM,
        compiler_params=params(16),
        cost_estimate=cost(TURN_COST),
        name="turn",
    )(inverses, pair)
    physics = pl.pallas_call(
        relax_kernel,
        out_shape=jax.ShapeDtypeStruct((peers * cap, kinds, levels), bf16),
        in_specs=[VMEM] * 2,
        out_specs=VMEM,
        scratch_shapes=[
            pltpu.VMEM((peers, 128), i32),
            pltpu.SMEM((peers, 128), i32),
            dma,
            pltpu.VMEM(((2 * owned * SLOTS + 1) * kinds, levels), f32),
        ],
        compiler_params=params(24),
        name="relax",
    )(arrived, turned)

    returned = exchange(physics)
    return pl.pallas_call(
        finish_kernel,
        out_shape=jax.ShapeDtypeStruct((rows, cells, width), f32),
        in_specs=[SMEM, VMEM, VMEM],
        out_specs=ANY,
        scratch_shapes=[
            pltpu.VMEM((cells * kinds, levels), f32),
            pltpu.VMEM((rows, cells, width), f32),
            dma((rows,)),
        ],
        compiler_params=params(16),
        name="finish",
    )(pos, returned, dyn)


def solution(mesh):
    lats, lons = mesh.devices.shape
    split = Mesh(mesh.devices.reshape(lats, 2, lons // 2), ("lat", "hi", "lo"))
    block = P("lat", LON_AXES, None)
    in_specs = (
        block,
        block,
        block,
        P("lat", LON_AXES),
        P("lat", LON_AXES),
        P(("lat", "hi", "lo"), None, None),
    )
    return jax.shard_map(shards, mesh=split, in_specs=in_specs, out_specs=block, check_vma=False)
```

```python
import functools

import jax
import jax.numpy as jnp
from jax import lax
from jax.experimental import pallas as pl
from jax.experimental.pallas import tpu as pltpu
from jax.sharding import Mesh
from jax.sharding import PartitionSpec as P

RIM_VMEM = 62
BULK_COST = 5
TURN_COST = 30
SLOTS = 48
DIFFUSE = 0.1
GROUP_AXES = ("lat", "lo")
LON_AXES = ("hi", "lo")

VMEM = pl.BlockSpec(memory_space=pltpu.VMEM)
ANY = pl.BlockSpec(memory_space=pltpu.HBM)
SMEM = pl.BlockSpec(memory_space=pltpu.SMEM)


def log2(n):
    return n.bit_length() - 1


def parities(place, lons):
    return place & 1, (place >> log2(lons)) & 1


def edge_kernel(
    lons, place_ref, q_hbm, u_hbm, v_hbm, lon_a, lon_b, lat_a, lat_b, q_side, u_side, wide, sems
):
    rows, cells, width = q_hbm.shape
    side = q_side.shape[2]
    odd_lon, odd_lat = parities(place_ref[0], lons)
    copies = []

    def copy(source, target):
        copies.append(pltpu.make_async_copy(source, target, sems.at[len(copies)]))
        copies[-1].start()

    for n, odd in enumerate((odd_lon, 1 - odd_lon)):
        near = pl.ds(pl.multiple_of(jnp.where(odd == 1, 0, cells - side), side), side)
        copy(q_hbm.at[:, near, :], q_side.at[n])
        copy(u_hbm.at[:, near, :], u_side.at[n])
    for ref, odd in ((lat_a, odd_lat), (lat_b, 1 - odd_lat)):
        i = jnp.where(odd == 1, 0, rows - 1)
        copy(q_hbm.at[i], ref.at[:, 0:width])
        copy(v_hbm.at[i], ref.at[:, width:])
    for c in copies[:4]:
        c.wait()
    for n, (ref, odd) in enumerate(((lon_a, odd_lon), (lon_b, 1 - odd_lon))):
        first = odd == 1
        for i in range(rows):
            q, u = q_side[n, i].astype(jnp.float32), u_side[n, i].astype(jnp.float32)
            wide[i : i + 1, 0:width] = jnp.where(first, q[0:1], q[side - 1 :])
            wide[i : i + 1, width:] = jnp.where(first, u[0:1], u[side - 1 :])
        ref[...] = wide[...].astype(jnp.bfloat16)
    for c in copies[4:]:
        c.wait()


def plan(place_ref, span_ref, slot_ref, send_ref, pos_ref, member, pos, cap, owned, lons, lows):
    rows, cells = span_ref.shape
    stored = cap + 1
    peers = send_ref.shape[0] // stored
    f32, bf16 = jnp.float32, jnp.bfloat16
    span, slot = span_ref[...], slot_ref[...]
    owner = span >> log2(owned)
    owner_lon = owner & (lons - 1)
    far = (owner_lon >> log2(lows)) != ((place_ref[0] >> log2(lows)) & 1)
    low = (owner_lon & (lows - 1)) ^ jnp.where(far, lows // 2, 0)
    peer = ((owner >> log2(lons)) << log2(lows)) + low
    local = (span & (owned - 1)) + jnp.where(far, owned, 0)
    iota = lambda shape, axis: lax.broadcasted_iota(jnp.int32, shape, axis)
    for i in range(rows):
        member[i * peers : (i + 1) * peers, :] = jnp.where(
            iota((peers, cells), 0) == peer[i : i + 1], 1.0, 0.0
        )
    hot = member[...].astype(bf16)
    dot = functools.partial(jnp.dot, preferred_element_type=f32)
    within = dot(hot, (iota((cells, cells), 0) < iota((cells, cells), 1)).astype(f32).astype(bf16))
    pairs = (rows * peers, rows * peers)
    to, of = iota(pairs, 0), iota(pairs, 1)
    same = (to & (peers - 1)) == (of & (peers - 1))
    lower = jnp.where(same & (of < (to & -peers)), 1.0, 0.0).astype(bf16)
    before = within + jnp.sum(dot(lower, hot), axis=1, keepdims=True)
    before = before * member[...]
    lists = jnp.zeros((3 * peers, 128), f32)
    for i in range(rows):
        block = slice(i * peers, (i + 1) * peers)
        rank = jnp.sum(before[block], axis=0, keepdims=True).astype(jnp.int32)
        pos[i : i + 1, 0:cells] = peer[i : i + 1] * stored + rank
        pos_ref[i : i + 1, 0:cells] = peer[i : i + 1] * cap + rank
        chosen = jnp.where(iota((128, cells), 0) == rank, 1.0, 0.0).astype(bf16)
        mine = member[block]
        values = jnp.concatenate(
            [mine * local[i : i + 1].astype(f32), mine * slot[i : i + 1].astype(f32), mine], axis=0
        )
        lists = lists + lax.dot_general(
            values.astype(bf16), chosen, (((1,), (1,)), ((), ())), preferred_element_type=f32
        )
    spans = jnp.where(lists[2 * peers :] > 0.5, lists[:peers], 2.0 * owned)
    slots = lists[peers : 2 * peers]
    tile = send_ref.shape[1:]
    for p in range(peers):
        send_ref[p * stored + cap] = jnp.where(
            iota(tile, 0) == 0,
            jnp.broadcast_to(spans[p : p + 1], tile),
            jnp.broadcast_to(slots[p : p + 1], tile),
        ).astype(bf16)


def bulk_kernel(cap, owned, lons, lows, place_ref, *refs):
    sources, outputs, held, rest = refs[:5], refs[5:11], refs[11:16], refs[16:]
    send_hbm, back_ref, pos_ref, dyn_hbm, rim_q, rim_dyn = outputs
    span_ref, slot_ref, q_ref, u_ref, v_ref = held
    sems, row_sems, member, pos_s, send_ref, dyn_ref, cell, wind_x, face_x, wind_y, face_y, flux_y = rest
    rows, cells, width = q_ref.shape
    levels = u_ref.shape[2]
    tracers = width // levels
    columns = rows * cells
    f32 = jnp.float32
    line = cells * tracers
    copies = [pltpu.make_async_copy(a, b, sems.at[n]) for n, (a, b) in enumerate(zip(sources, held))]
    for copy in copies:
        copy.start()
    copies[2].wait()

    def relayout(i, carry):
        for t in range(tracers):
            cell[pl.ds(i * line + t, cells, stride=tracers), :] = q_ref[
                i, :, t * levels : (t + 1) * levels
            ].astype(f32)
        return carry

    lax.fori_loop(0, rows, relayout, 0)
    for copy in copies[:2]:
        copy.wait()
    plan(place_ref, span_ref, slot_ref, send_ref, back_ref, member, pos_ref, cap, owned, lons, lows)
    pos_copy = pltpu.make_async_copy(pos_ref, pos_s, sems.at[5])
    pos_copy.start()
    for copy in copies[3:]:
        copy.wait()

    wind_x[0:columns, :] = u_ref[...].reshape(columns, levels).astype(f32)
    wind_y[...] = v_ref[...].reshape(columns, levels).astype(f32)
    face_x[...] = 0.25 * (wind_x[0:columns, :] + wind_x[1 : columns + 1, :])
    face_y[0 : columns - cells, :] = 0.25 * (wind_y[: columns - cells, :] + wind_y[cells:, :])
    face_y[columns - cells :, :] = jnp.zeros((cells, levels), f32)
    flux_y[...] = jnp.zeros_like(flux_y)

    def tile(i, j):
        return pl.ds(pl.multiple_of((i * cells + j) * tracers, tracers), tracers)

    def spread_row(ref, r):
        return jnp.broadcast_to(ref[pl.ds(r, 1), :], (tracers, levels))

    pos_copy.wait()

    def dyn_copy(i):
        rows_i = pl.ds(pl.multiple_of(i * line, tracers), line)
        return pltpu.make_async_copy(dyn_ref.at[rows_i], dyn_hbm.at[rows_i], row_sems.at[i])

    def row(i, carry):
        diffuse_y = jnp.where(i == rows - 1, 0.0, DIFFUSE)
        north = jnp.minimum(i + 1, rows - 1)
        here = cell[tile(i, 0), :]
        flux_w = jnp.zeros((tracers, levels), f32)
        for j in range(cells):
            column = i * cells + j
            if j < cells - 1:
                after = cell[tile(i, j + 1), :]
                flux_e = spread_row(face_x, column) * (here + after) - DIFFUSE * (after - here)
            else:
                flux_e = jnp.zeros((tracers, levels), f32)
            above = cell[tile(north, j), :]
            flux_n = spread_row(face_y, column) * (here + above) - diffuse_y * (above - here)
            flux_s = flux_y[j * tracers : (j + 1) * tracers, :]
            flux_y[j * tracers : (j + 1) * tracers, :] = flux_n
            dyn = (flux_w - flux_e) + (flux_s - flux_n)
            dyn_ref[tile(i, j), :] = dyn
            send_ref[pos_s[i, j]] = (here + dyn).astype(jnp.bfloat16)
            if j in (0, cells - 1):
                at = pl.multiple_of((2 * cells + (j > 0) * rows + i) * tracers, tracers)
                rim_q[pl.ds(at, tracers), :] = here
                rim_dyn[pl.ds(at, tracers), :] = dyn
            here, flux_w = after, flux_e
        dyn_copy(i).start()
        return carry

    lax.fori_loop(0, rows, row, 0)
    send_copy = pltpu.make_async_copy(send_ref, send_hbm, sems.at[6])
    send_copy.start()
    for n, i in enumerate((0, rows - 1)):
        rim_q[n * line : (n + 1) * line, :] = cell[i * line : (i + 1) * line, :]
        rim_dyn[n * line : (n + 1) * line, :] = dyn_ref[i * line : (i + 1) * line, :]
    send_copy.wait()

    def drain(i, carry):
        dyn_copy(i).wait()
        return carry

    lax.fori_loop(0, rows, drain, 0)


def rim_kernel(lats, lons, place_ref, *refs):
    sources, (send_in, send_hbm, rim_ref), rest = refs[:11], refs[11:14], refs[14:]
    own_lon, own_lat, far_lon, far_lat, pos_s, rim_q, rim_dyn, side, stage, sems = rest
    rows, cells = own_lon.shape[1], own_lat.shape[1]
    levels = side.shape[1]
    tracers = rim_q.shape[0] // (2 * (rows + cells))
    width = tracers * levels
    f32 = jnp.float32
    odd_lon, odd_lat = parities(place_ref[0], lons)
    targets = (
        own_lon.at[1 - odd_lon],
        own_lon.at[odd_lon],
        own_lat.at[1 - odd_lat],
        own_lat.at[odd_lat],
        far_lon.at[1 - odd_lon],
        far_lon.at[odd_lon],
        far_lat.at[1 - odd_lat],
        far_lat.at[odd_lat],
        pos_s,
        rim_q,
        rim_dyn,
    )
    copies = [pltpu.make_async_copy(a, b, sems.at[n]) for n, (a, b) in enumerate(zip(sources, targets))]
    for copy in copies:
        copy.start()
    for copy in copies[:8]:
        copy.wait()
    lat = place_ref[0] >> log2(lons)
    lat_open = (jnp.where(lat > 0, 1.0, 0.0), jnp.where(lat < lats - 1, 1.0, 0.0))
    first = 0
    for own, far, opens in ((own_lat, far_lat, lat_open), (own_lon, far_lon, (None, None))):
        for n, opened in enumerate(opens):
            sign, diffuse = (0.25, -0.25)[n], DIFFUSE
            if opened is not None:
                sign, diffuse = sign * opened, diffuse * opened
            count = own.shape[1]
            face = sign * (own[n, :, width:].astype(f32) + far[n, :, width:].astype(f32))
            for t in range(tracers):
                lanes = slice(t * levels, (t + 1) * levels)
                here, there = own[n, :, lanes].astype(f32), far[n, :, lanes].astype(f32)
                side[pl.ds(first * tracers + t, count, stride=tracers), :] = face * (
                    here + there
                ) + diffuse * (there - here)
            first += count
    for copy in copies[8:]:
        copy.wait()
    tile = lambda n: slice(n * tracers, (n + 1) * tracers)
    west, east = 2 * cells, 2 * cells + rows
    rim = []
    for n, i in enumerate((0, rows - 1)):
        for j in range(cells):
            extra = {0: (west + i,), cells - 1: (east + i,)}.get(j, ())
            rim.append((n * cells + j, i, j, extra))
    for i in range(1, rows - 1):
        rim += [(west + i, i, 0, ()), (east + i, i, cells - 1, ())]
    sent = sems.at[len(copies)]
    for m, (n, i, j, extra) in enumerate(rim):
        dyn = rim_dyn[tile(n), :] + side[tile(n), :]
        for e in extra:
            dyn = dyn + side[tile(e), :]
        rim_ref[tile(n), :] = dyn
        stage[m] = (rim_q[tile(n), :] + dyn).astype(jnp.bfloat16)
        pltpu.make_async_copy(stage.at[m], send_hbm.at[pos_s[i, j]], sent).start()
    pltpu.make_async_copy(stage, send_hbm.at[pl.ds(0, len(rim))], sent).wait()


def turn_kernel(lows, place_ref, own_ref, outer_ref, inner_ref, out_ref):
    owned = own_ref.shape[0]
    place = place_ref[0]
    is_outer = ((place >> log2(lows)) & 1) == ((place >> (log2(lows) - 1)) & 1)
    for k in range(owned):
        out_ref[k] = own_ref[k].T

    @pl.when(is_outer)
    def _():
        for k in range(owned):
            out_ref[owned + k] = outer_ref[k].T

    @pl.when(jnp.logical_not(is_outer))
    def _():
        for k in range(owned):
            out_ref[owned + k] = inner_ref[k].T


def relax_kernel(x_ref, w_ref, y_ref, pos, pos_s, sem, slots):
    tracers, levels = x_ref.shape[1:]
    peers, lanes = pos.shape
    stored = x_ref.shape[0] // peers
    cap = stored - 1
    f32 = jnp.float32
    for p in range(peers):
        listed = x_ref[p * stored + cap].astype(f32)
        pos[p : p + 1, :] = (listed[0:1] * SLOTS + listed[1:2]).astype(jnp.int32)
    copy = pltpu.make_async_copy(pos, pos_s, sem)
    copy.start()
    copy.wait()

    def place(at):
        return pl.ds(pl.multiple_of(at * tracers, tracers), tracers)

    def scatter(p, carry):
        for r in range(cap):
            slots[place(pos_s[p, r]), :] = x_ref[p * stored + r].astype(f32)
        return carry

    lax.fori_loop(0, peers, scatter, 0)
    block = SLOTS * tracers

    def span(k, carry):
        at = pl.ds(pl.multiple_of(k * block, block), block)
        x = slots[at, :]
        y = jnp.dot(x.astype(jnp.bfloat16), w_ref[k], preferred_element_type=f32)
        slots[at, :] = y - x
        return carry

    lax.fori_loop(0, w_ref.shape[0], span, 0, unroll=8)

    def gather(p, carry):
        for r in range(cap):
            y_ref[p * cap + r] = slots[place(pos_s[p, r]), :].astype(jnp.bfloat16)
        return carry

    lax.fori_loop(0, peers, gather, 0)


def finish_kernel(pos_ref, y_ref, dyn_ref, rim_ref, out_hbm, total, out, sems):
    rows, cells, width = out.shape
    tracers, levels = y_ref.shape[1:]

    def copy(i):
        return pltpu.make_async_copy(out.at[i], out_hbm.at[i], sems.at[i])

    def tile(n):
        return pl.ds(pl.multiple_of(n * tracers, tracers), tracers)

    def row(i, dyn):
        for j in range(cells):
            total[j * tracers : (j + 1) * tracers, :] = dyn(j) + y_ref[pos_ref[i, j]].astype(
                jnp.float32
            )
        for t in range(tracers):
            out[i, :, t * levels : (t + 1) * levels] = total[pl.ds(t, cells, stride=tracers), :]
        copy(i).start()

    def inner(i, carry):
        def dyn(j):
            if j in (0, cells - 1):
                return rim_ref[tile(2 * cells + (j > 0) * rows + i), :]
            return dyn_ref[tile(i * cells + j), :]

        row(i, dyn)
        return carry

    row(0, lambda j: rim_ref[tile(j), :])
    lax.fori_loop(1, rows - 1, inner, 0)
    row(rows - 1, lambda j: rim_ref[tile(cells + j), :])
    for i in range(rows):
        copy(i).wait()


def in_pairs(x, axis, first):
    count = lax.axis_size(axis)
    pairs = [(i % count, (i + 1) % count) for i in range(first, count + first, 2)]
    return lax.ppermute(x, axis, pairs + [(b, a) for a, b in pairs])


def shards(tracers, east_wind, north_wind, span_of, slot_of, inverses):
    levels = east_wind.shape[2]
    rows, cells, width = tracers.shape
    kinds = width // levels
    columns = rows * cells
    lats, lows = lax.axis_size("lat"), lax.axis_size("lo")
    lons = lax.axis_size("hi") * lows
    peers = lats * lows
    owned = inverses.shape[0]
    cap = 2 * (3 * columns // (2 * lats * lons))
    stored = cap + 1
    f32, bf16, i32 = jnp.float32, jnp.bfloat16, jnp.int32
    dma = pltpu.SemaphoreType.DMA
    params = lambda mib: pltpu.CompilerParams(vmem_limit_bytes=mib << 20)

    side = 8
    place = lax.axis_index(("lat", "hi", "lo")).astype(i32).reshape(1)
    lon_a, lon_b, lat_a, lat_b = pl.pallas_call(
        functools.partial(edge_kernel, lons),
        out_shape=(jax.ShapeDtypeStruct((rows, width + levels), bf16),) * 2
        + (jax.ShapeDtypeStruct((cells, width + levels), bf16),) * 2,
        in_specs=[SMEM] + [ANY] * 3,
        out_specs=(VMEM,) * 4,
        scratch_shapes=[
            pltpu.VMEM((2, rows, side, width), bf16),
            pltpu.VMEM((2, rows, side, levels), bf16),
            pltpu.VMEM((rows, width + levels), f32),
            dma((8,)),
        ],
        compiler_params=params(62),
        name="edges",
    )(place, tracers, east_wind, north_wind)
    edges = (lon_a, lon_b, lat_a, lat_b)
    far_edges = (
        in_pairs(lon_a, LON_AXES, 0),
        in_pairs(lon_b, LON_AXES, 1),
        in_pairs(lat_a, "lat", 0),
        in_pairs(lat_b, "lat", 1),
    )

    def opposite(start, stop):
        pairs = [(lo, lows + (lo ^ lows // 2)) for lo in range(start, stop)]
        return pairs + [(b, a) for a, b in pairs]

    outer = lax.ppermute(inverses, LON_AXES, opposite(0, lows // 2))
    cost = lambda us: pl.CostEstimate(
        flops=us * 1_000_000_000, bytes_accessed=1 << 20, transcendentals=0
    )
    fields = (span_of, slot_of, tracers, east_wind, north_wind)
    rim_shape = (2 * (rows + cells) * kinds, levels)
    block_shape = (columns * kinds, levels)
    send_shape = (peers * stored, kinds, levels)
    send, back, pos, dyn, rim_q, rim_dyn = pl.pallas_call(
        functools.partial(bulk_kernel, cap, owned, lons, lows),
        out_shape=(
            jax.ShapeDtypeStruct(send_shape, bf16),
            jax.ShapeDtypeStruct((rows, 128), i32),
            jax.ShapeDtypeStruct((rows, 128), i32),
            jax.ShapeDtypeStruct(block_shape, f32),
            jax.ShapeDtypeStruct(rim_shape, f32),
            jax.ShapeDtypeStruct(rim_shape, f32),
        ),
        in_specs=[SMEM] + [ANY] * 5,
        out_specs=(ANY, VMEM, VMEM, ANY, VMEM, VMEM),
        scratch_shapes=[pltpu.VMEM(x.shape, x.dtype) for x in fields]
        + [
            dma((7,)),
            dma((rows,)),
            pltpu.VMEM((rows * peers, cells), f32),
            pltpu.SMEM((rows, 128), i32),
            pltpu.VMEM(send_shape, bf16),
            pltpu.VMEM(block_shape, f32),
            pltpu.VMEM(block_shape, f32),
            pltpu.VMEM((columns + 8, levels), f32),
            pltpu.VMEM((columns, levels), f32),
            pltpu.VMEM((columns, levels), f32),
            pltpu.VMEM((columns, levels), f32),
            pltpu.VMEM((cells * kinds, levels), f32),
        ],
        compiler_params=params(62),
        cost_estimate=cost(BULK_COST),
        name="bulk",
    )(place, *fields)

    matrices, pos, *far_edges = lax.optimization_barrier((inverses, pos, *far_edges))
    inner = lax.ppermute(matrices, LON_AXES, opposite(lows // 2, lows))

    rim_args = (*edges, *far_edges, pos, rim_q, rim_dyn)
    both = lambda x: pltpu.VMEM((2,) + x.shape, x.dtype)
    send, rim = pl.pallas_call(
        functools.partial(rim_kernel, lats, lons),
        out_shape=(jax.ShapeDtypeStruct(send_shape, bf16), jax.ShapeDtypeStruct(rim_shape, f32)),
        in_specs=[SMEM] + [ANY] * 12,
        out_specs=(ANY, VMEM),
        scratch_shapes=[
            both(lon_a),
            both(lat_a),
            both(lon_a),
            both(lat_a),
            pltpu.SMEM((rows, 128), i32),
            pltpu.VMEM(rim_shape, f32),
            pltpu.VMEM(rim_shape, f32),
            pltpu.VMEM(rim_shape, f32),
            pltpu.VMEM((2 * (rows + cells) - 4, kinds, levels), bf16),
            dma((12,)),
        ],
        input_output_aliases={12: 0},
        compiler_params=params(RIM_VMEM),
        name="rim",
    )(place, *rim_args, send)

    def exchange(x):
        x = x.reshape(peers, -1, kinds, levels)
        x = lax.all_to_all(x, GROUP_AXES, split_axis=0, concat_axis=0, tiled=True)
        return x.reshape(-1, kinds, levels)

    arrived = exchange(send)
    turned = pl.pallas_call(
        functools.partial(turn_kernel, lows),
        out_shape=jax.ShapeDtypeStruct((2 * owned, levels, levels), bf16),
        in_specs=[SMEM] + [VMEM] * 3,
        out_specs=VMEM,
        compiler_params=params(16),
        cost_estimate=cost(TURN_COST),
        name="turn",
    )(place, inverses, outer, inner)
    physics = pl.pallas_call(
        relax_kernel,
        out_shape=jax.ShapeDtypeStruct((peers * cap, kinds, levels), bf16),
        in_specs=[VMEM] * 2,
        out_specs=VMEM,
        scratch_shapes=[
            pltpu.VMEM((peers, 128), i32),
            pltpu.SMEM((peers, 128), i32),
            dma,
            pltpu.VMEM(((2 * owned * SLOTS + 1) * kinds, levels), f32),
        ],
        compiler_params=params(24),
        name="relax",
    )(arrived, turned)

    returned = exchange(physics)
    return pl.pallas_call(
        finish_kernel,
        out_shape=jax.ShapeDtypeStruct((rows, cells, width), f32),
        in_specs=[SMEM, VMEM, VMEM, VMEM],
        out_specs=ANY,
        scratch_shapes=[
            pltpu.VMEM((cells * kinds, levels), f32),
            pltpu.VMEM((rows, cells, width), f32),
            dma((rows,)),
        ],
        compiler_params=params(16),
        name="finish",
    )(back, returned, dyn, rim)


def solution(mesh):
    lats, lons = mesh.devices.shape
    split = Mesh(mesh.devices.reshape(lats, 2, lons // 2), ("lat", "hi", "lo"))
    block = P("lat", LON_AXES, None)
    in_specs = (
        block,
        block,
        block,
        P("lat", LON_AXES),
        P("lat", LON_AXES),
        P(("lat", "hi", "lo"), None, None),
    )
    return jax.shard_map(shards, mesh=split, in_specs=in_specs, out_specs=block, check_vma=False)
```

```python
import functools

import jax
import jax.numpy as jnp
from jax import lax
from jax.experimental import pallas as pl
from jax.experimental.pallas import tpu as pltpu
from jax.sharding import Mesh
from jax.sharding import PartitionSpec as P

RIM_VMEM = 64
BULK_COST = 5
TURN_COST = 30
INNER_COST = 1
SLOTS = 48
DIFFUSE = 0.1
GROUP_AXES = ("lat", "lo")
LON_AXES = ("hi", "lo")

VMEM = pl.BlockSpec(memory_space=pltpu.VMEM)
ANY = pl.BlockSpec(memory_space=pltpu.HBM)
SMEM = pl.BlockSpec(memory_space=pltpu.SMEM)


def log2(n):
    return n.bit_length() - 1


def parities(place, lons):
    return place & 1, (place >> log2(lons)) & 1


def edge_kernel(
    lons, place_ref, q_hbm, u_hbm, v_hbm, lon_a, lon_b, lat_a, lat_b, q_side, u_side, wide, sems
):
    rows, cells, width = q_hbm.shape
    side = q_side.shape[2]
    odd_lon, odd_lat = parities(place_ref[0], lons)
    copies = []

    def copy(source, target):
        copies.append(pltpu.make_async_copy(source, target, sems.at[len(copies)]))
        copies[-1].start()

    for n, odd in enumerate((odd_lon, 1 - odd_lon)):
        near = pl.ds(pl.multiple_of(jnp.where(odd == 1, 0, cells - side), side), side)
        copy(q_hbm.at[:, near, :], q_side.at[n])
        copy(u_hbm.at[:, near, :], u_side.at[n])
    for ref, odd in ((lat_a, odd_lat), (lat_b, 1 - odd_lat)):
        i = jnp.where(odd == 1, 0, rows - 1)
        copy(q_hbm.at[i], ref.at[:, 0:width])
        copy(v_hbm.at[i], ref.at[:, width:])
    for c in copies[:4]:
        c.wait()
    for n, (ref, odd) in enumerate(((lon_a, odd_lon), (lon_b, 1 - odd_lon))):
        first = odd == 1
        for i in range(rows):
            q, u = q_side[n, i].astype(jnp.float32), u_side[n, i].astype(jnp.float32)
            wide[i : i + 1, 0:width] = jnp.where(first, q[0:1], q[side - 1 :])
            wide[i : i + 1, width:] = jnp.where(first, u[0:1], u[side - 1 :])
        ref[...] = wide[...].astype(jnp.bfloat16)
    for c in copies[4:]:
        c.wait()


def plan(place_ref, span_ref, slot_ref, send_ref, pos_ref, member, pos, cap, owned, lons, lows):
    rows, cells = span_ref.shape
    stored = cap + 1
    peers = send_ref.shape[0] // stored
    f32, bf16 = jnp.float32, jnp.bfloat16
    span, slot = span_ref[...], slot_ref[...]
    owner = span >> log2(owned)
    owner_lon = owner & (lons - 1)
    far = (owner_lon >> log2(lows)) != ((place_ref[0] >> log2(lows)) & 1)
    low = (owner_lon & (lows - 1)) ^ jnp.where(far, lows // 2, 0)
    peer = ((owner >> log2(lons)) << log2(lows)) + low
    local = (span & (owned - 1)) + jnp.where(far, owned, 0)
    iota = lambda shape, axis: lax.broadcasted_iota(jnp.int32, shape, axis)
    for i in range(rows):
        member[i * peers : (i + 1) * peers, :] = jnp.where(
            iota((peers, cells), 0) == peer[i : i + 1], 1.0, 0.0
        )
    hot = member[...].astype(bf16)
    dot = functools.partial(jnp.dot, preferred_element_type=f32)
    within = dot(hot, (iota((cells, cells), 0) < iota((cells, cells), 1)).astype(f32).astype(bf16))
    pairs = (rows * peers, rows * peers)
    to, of = iota(pairs, 0), iota(pairs, 1)
    same = (to & (peers - 1)) == (of & (peers - 1))
    lower = jnp.where(same & (of < (to & -peers)), 1.0, 0.0).astype(bf16)
    before = within + jnp.sum(dot(lower, hot), axis=1, keepdims=True)
    before = before * member[...]
    lists = jnp.zeros((3 * peers, 128), f32)
    for i in range(rows):
        block = slice(i * peers, (i + 1) * peers)
        rank = jnp.sum(before[block], axis=0, keepdims=True).astype(jnp.int32)
        pos[i : i + 1, 0:cells] = peer[i : i + 1] * stored + rank
        pos_ref[i : i + 1, 0:cells] = peer[i : i + 1] * cap + rank
        chosen = jnp.where(iota((128, cells), 0) == rank, 1.0, 0.0).astype(bf16)
        mine = member[block]
        values = jnp.concatenate(
            [mine * local[i : i + 1].astype(f32), mine * slot[i : i + 1].astype(f32), mine], axis=0
        )
        lists = lists + lax.dot_general(
            values.astype(bf16), chosen, (((1,), (1,)), ((), ())), preferred_element_type=f32
        )
    spans = jnp.where(lists[2 * peers :] > 0.5, lists[:peers], 2.0 * owned)
    slots = lists[peers : 2 * peers]
    tile = send_ref.shape[1:]
    for p in range(peers):
        send_ref[p * stored + cap] = jnp.where(
            iota(tile, 0) == 0,
            jnp.broadcast_to(spans[p : p + 1], tile),
            jnp.broadcast_to(slots[p : p + 1], tile),
        ).astype(bf16)


def bulk_kernel(cap, owned, lons, lows, place_ref, *refs):
    sources, outputs, held, rest = refs[:5], refs[5:9], refs[9:14], refs[14:]
    send_hbm, back_hbm, pos_hbm, dyn_hbm = outputs
    span_ref, slot_ref, q_ref, u_ref, v_ref = held
    sems, row_sems, member, back_ref, pos_ref, pos_s, send_ref, dyn_ref, cell, wind_x, face_x, wind_y, face_y, flux_y = rest
    rows, cells, width = q_ref.shape
    levels = u_ref.shape[2]
    tracers = width // levels
    columns = rows * cells
    f32 = jnp.float32
    line = cells * tracers
    copies = [pltpu.make_async_copy(a, b, sems.at[n]) for n, (a, b) in enumerate(zip(sources, held))]
    for copy in copies:
        copy.start()
    for copy in copies[:2]:
        copy.wait()
    plan(place_ref, span_ref, slot_ref, send_ref, back_ref, member, pos_ref, cap, owned, lons, lows)
    places = [(pos_ref, pos_s), (pos_ref, pos_hbm), (back_ref, back_hbm)]
    places = [pltpu.make_async_copy(a, b, sems.at[5 + n]) for n, (a, b) in enumerate(places)]
    for copy in places:
        copy.start()
    copies[2].wait()

    def relayout(i, carry):
        for t in range(tracers):
            cell[pl.ds(i * line + t, cells, stride=tracers), :] = q_ref[
                i, :, t * levels : (t + 1) * levels
            ].astype(f32)
        return carry

    lax.fori_loop(0, rows, relayout, 0)
    for copy in copies[3:]:
        copy.wait()

    wind_x[0:columns, :] = u_ref[...].reshape(columns, levels).astype(f32)
    wind_y[...] = v_ref[...].reshape(columns, levels).astype(f32)
    face_x[...] = 0.25 * (wind_x[0:columns, :] + wind_x[1 : columns + 1, :])
    face_y[0 : columns - cells, :] = 0.25 * (wind_y[: columns - cells, :] + wind_y[cells:, :])
    face_y[columns - cells :, :] = jnp.zeros((cells, levels), f32)
    flux_y[...] = jnp.zeros_like(flux_y)

    def tile(i, j):
        return pl.ds(pl.multiple_of((i * cells + j) * tracers, tracers), tracers)

    def spread_row(ref, r):
        return jnp.broadcast_to(ref[pl.ds(r, 1), :], (tracers, levels))

    places[0].wait()

    def dyn_copy(i):
        return pltpu.make_async_copy(dyn_ref.at[i], dyn_hbm.at[i], row_sems.at[i])

    def row(i, carry):
        diffuse_y = jnp.where(i == rows - 1, 0.0, DIFFUSE)
        north = jnp.minimum(i + 1, rows - 1)
        here = cell[tile(i, 0), :]
        flux_w = jnp.zeros((tracers, levels), f32)
        for j in range(cells):
            column = i * cells + j
            if j < cells - 1:
                after = cell[tile(i, j + 1), :]
                flux_e = spread_row(face_x, column) * (here + after) - DIFFUSE * (after - here)
            else:
                flux_e = jnp.zeros((tracers, levels), f32)
            above = cell[tile(north, j), :]
            flux_n = spread_row(face_y, column) * (here + above) - diffuse_y * (above - here)
            flux_s = flux_y[j * tracers : (j + 1) * tracers, :]
            flux_y[j * tracers : (j + 1) * tracers, :] = flux_n
            dyn = (flux_w - flux_e) + (flux_s - flux_n)
            dyn_ref[i, j * tracers : (j + 1) * tracers, :] = dyn
            send_ref[pos_s[i, j]] = (here + dyn).astype(jnp.bfloat16)
            here, flux_w = after, flux_e
        dyn_copy(i).start()
        return carry

    lax.fori_loop(0, rows, row, 0)
    send_copy = pltpu.make_async_copy(send_ref, send_hbm, sems.at[8])
    send_copy.start()
    for copy in places[1:]:
        copy.wait()
    def drain(i, carry):
        dyn_copy(i).wait()
        return carry

    lax.fori_loop(0, rows, drain, 0)
    send_copy.wait()


def rim_kernel(lats, lons, place_ref, *refs):
    sources, dyn_hbm, (send_in, send_hbm, rim_ref), rest = refs[:9], refs[9], refs[10:13], refs[13:]
    own_lon, own_lat, far_lon, far_lat, pos_s, row_dyn, side_dyn, rim_q, side, stage, sems = rest
    rows, cells = own_lon.shape[1], own_lat.shape[1]
    levels = side.shape[1]
    tracers = row_dyn.shape[1] // cells
    width = tracers * levels
    f32 = jnp.float32
    odd_lon, odd_lat = parities(place_ref[0], lons)
    targets = (
        own_lon.at[1 - odd_lon],
        own_lon.at[odd_lon],
        own_lat.at[1 - odd_lat],
        own_lat.at[odd_lat],
        far_lon.at[1 - odd_lon],
        far_lon.at[odd_lon],
        far_lat.at[1 - odd_lat],
        far_lat.at[odd_lat],
        pos_s,
    )
    pairs = list(zip(sources, targets))
    line = cells * tracers
    west, east = 2 * cells, 2 * cells + rows
    for n, i in enumerate((0, rows - 1)):
        pairs.append((dyn_hbm.at[i], row_dyn.at[n]))
    for n, j in enumerate((0, cells - 1)):
        pairs.append((dyn_hbm.at[:, j * tracers : (j + 1) * tracers, :], side_dyn.at[n]))
    copies = [pltpu.make_async_copy(a, b, sems.at[n]) for n, (a, b) in enumerate(pairs)]
    for copy in copies:
        copy.start()
    for copy in copies[:8]:
        copy.wait()
    lat = place_ref[0] >> log2(lons)
    lat_open = (jnp.where(lat > 0, 1.0, 0.0), jnp.where(lat < lats - 1, 1.0, 0.0))
    first = 0
    for own, far, opens in ((own_lat, far_lat, lat_open), (own_lon, far_lon, (None, None))):
        for n, opened in enumerate(opens):
            sign, diffuse = (0.25, -0.25)[n], DIFFUSE
            if opened is not None:
                sign, diffuse = sign * opened, diffuse * opened
            count = own.shape[1]
            face = sign * (own[n, :, width:].astype(f32) + far[n, :, width:].astype(f32))
            for t in range(tracers):
                lanes = slice(t * levels, (t + 1) * levels)
                here, there = own[n, :, lanes].astype(f32), far[n, :, lanes].astype(f32)
                at = pl.ds(first * tracers + t, count, stride=tracers)
                rim_q[at, :] = here
                side[at, :] = face * (here + there) + diffuse * (there - here)
            first += count
    for copy in copies[8:]:
        copy.wait()
    tile = lambda n: slice(n * tracers, (n + 1) * tracers)
    rim = []
    for n, i in enumerate((0, rows - 1)):
        for j in range(cells):
            extra = {0: (west + i,), cells - 1: (east + i,)}.get(j, ())
            rim.append((n * cells + j, i, j, extra))
    for i in range(1, rows - 1):
        rim += [(west + i, i, 0, ()), (east + i, i, cells - 1, ())]
    sent = sems.at[len(copies)]
    for m, (n, i, j, extra) in enumerate(rim):
        if n < west:
            dyn = row_dyn[n // cells, tile(n % cells), :]
        else:
            dyn = side_dyn[(n - west) // rows, (n - west) % rows]
        dyn = dyn + side[tile(n), :]
        for e in extra:
            dyn = dyn + side[tile(e), :]
        rim_ref[tile(n), :] = dyn
        stage[m] = (rim_q[tile(n), :] + dyn).astype(jnp.bfloat16)
        pltpu.make_async_copy(stage.at[m], send_hbm.at[pos_s[i, j]], sent).start()
    pltpu.make_async_copy(stage, send_hbm.at[pl.ds(0, len(rim))], sent).wait()


def turn_kernel(*refs):
    refs, out_ref = refs[:-1], refs[-1]
    for n, ref in enumerate(refs):
        for k in range(ref.shape[0]):
            out_ref[n * ref.shape[0] + k] = ref[k].T


def relax_kernel(lows, place_ref, x_ref, outer_ref, inner_ref, y_ref, pos, pos_s, sem, slots):
    tracers, levels = x_ref.shape[1:]
    peers, lanes = pos.shape
    stored = x_ref.shape[0] // peers
    cap = stored - 1
    f32 = jnp.float32
    for p in range(peers):
        listed = x_ref[p * stored + cap].astype(f32)
        pos[p : p + 1, :] = (listed[0:1] * SLOTS + listed[1:2]).astype(jnp.int32)
    copy = pltpu.make_async_copy(pos, pos_s, sem)
    copy.start()
    copy.wait()

    def tile(at):
        return pl.ds(pl.multiple_of(at * tracers, tracers), tracers)

    def scatter(p, carry):
        for r in range(cap):
            slots[tile(pos_s[p, r]), :] = x_ref[p * stored + r].astype(f32)
        return carry

    lax.fori_loop(0, peers, scatter, 0)
    block = SLOTS * tracers

    def relax(first, count, w_ref, w_first):
        def span(k, carry):
            at = pl.ds(pl.multiple_of((first + k) * block, block), block)
            x = slots[at, :]
            y = jnp.dot(x.astype(jnp.bfloat16), w_ref[w_first + k], preferred_element_type=f32)
            slots[at, :] = y - x
            return carry

        lax.fori_loop(0, count, span, 0, unroll=8)

    owned = inner_ref.shape[0]
    place = place_ref[0]
    is_outer = ((place >> log2(lows)) & 1) == ((place >> (log2(lows) - 1)) & 1)
    relax(0, owned, outer_ref, 0)

    @pl.when(is_outer)
    def _():
        relax(owned, owned, outer_ref, owned)

    @pl.when(jnp.logical_not(is_outer))
    def _():
        relax(owned, owned, inner_ref, 0)

    def gather(p, carry):
        for r in range(cap):
            y_ref[p * cap + r] = slots[tile(pos_s[p, r]), :].astype(jnp.bfloat16)
        return carry

    lax.fori_loop(0, peers, gather, 0)


def finish_kernel(pos_ref, y_ref, dyn_ref, rim_ref, out_hbm, total, out, sems):
    rows, cells, width = out.shape
    tracers, levels = y_ref.shape[1:]

    def copy(i):
        return pltpu.make_async_copy(out.at[i], out_hbm.at[i], sems.at[i])

    def tile(n):
        return pl.ds(pl.multiple_of(n * tracers, tracers), tracers)

    def row(i, dyn):
        for j in range(cells):
            total[j * tracers : (j + 1) * tracers, :] = dyn(j) + y_ref[pos_ref[i, j]].astype(
                jnp.float32
            )
        for t in range(tracers):
            out[i, :, t * levels : (t + 1) * levels] = total[pl.ds(t, cells, stride=tracers), :]
        copy(i).start()

    def inner(i, carry):
        def dyn(j):
            if j in (0, cells - 1):
                return rim_ref[tile(2 * cells + (j > 0) * rows + i), :]
            return dyn_ref[i, j * tracers : (j + 1) * tracers, :]

        row(i, dyn)
        return carry

    row(0, lambda j: rim_ref[tile(j), :])
    lax.fori_loop(1, rows - 1, inner, 0)
    row(rows - 1, lambda j: rim_ref[tile(cells + j), :])
    for i in range(rows):
        copy(i).wait()


def in_pairs(x, axis, first):
    count = lax.axis_size(axis)
    pairs = [(i % count, (i + 1) % count) for i in range(first, count + first, 2)]
    return lax.ppermute(x, axis, pairs + [(b, a) for a, b in pairs])


def shards(tracers, east_wind, north_wind, span_of, slot_of, inverses):
    levels = east_wind.shape[2]
    rows, cells, width = tracers.shape
    kinds = width // levels
    columns = rows * cells
    lats, lows = lax.axis_size("lat"), lax.axis_size("lo")
    lons = lax.axis_size("hi") * lows
    peers = lats * lows
    owned = inverses.shape[0]
    cap = 2 * (3 * columns // (2 * lats * lons))
    stored = cap + 1
    f32, bf16, i32 = jnp.float32, jnp.bfloat16, jnp.int32
    dma = pltpu.SemaphoreType.DMA
    params = lambda mib: pltpu.CompilerParams(vmem_limit_bytes=mib << 20)

    side = 8
    place = lax.axis_index(("lat", "hi", "lo")).astype(i32).reshape(1)
    lon_a, lon_b, lat_a, lat_b = pl.pallas_call(
        functools.partial(edge_kernel, lons),
        out_shape=(jax.ShapeDtypeStruct((rows, width + levels), bf16),) * 2
        + (jax.ShapeDtypeStruct((cells, width + levels), bf16),) * 2,
        in_specs=[SMEM] + [ANY] * 3,
        out_specs=(VMEM,) * 4,
        scratch_shapes=[
            pltpu.VMEM((2, rows, side, width), bf16),
            pltpu.VMEM((2, rows, side, levels), bf16),
            pltpu.VMEM((rows, width + levels), f32),
            dma((8,)),
        ],
        compiler_params=params(64),
        name="edges",
    )(place, tracers, east_wind, north_wind)
    edges = (lon_a, lon_b, lat_a, lat_b)
    far_edges = (
        in_pairs(lon_a, LON_AXES, 0),
        in_pairs(lon_b, LON_AXES, 1),
        in_pairs(lat_a, "lat", 0),
        in_pairs(lat_b, "lat", 1),
    )

    def opposite(start, stop):
        pairs = [(lo, lows + (lo ^ lows // 2)) for lo in range(start, stop)]
        return pairs + [(b, a) for a, b in pairs]

    outer = lax.ppermute(inverses, LON_AXES, opposite(0, lows // 2))
    cost = lambda us: pl.CostEstimate(
        flops=us * 1_000_000_000, bytes_accessed=1 << 20, transcendentals=0
    )
    fields = (span_of, slot_of, tracers, east_wind, north_wind)
    rim_shape = (2 * (rows + cells) * kinds, levels)
    block_shape = (columns * kinds, levels)
    dyn_shape = (rows, cells * kinds, levels)
    send_shape = (peers * stored, kinds, levels)
    send, back, pos, dyn = pl.pallas_call(
        functools.partial(bulk_kernel, cap, owned, lons, lows),
        out_shape=(
            jax.ShapeDtypeStruct(send_shape, bf16),
            jax.ShapeDtypeStruct((rows, 128), i32),
            jax.ShapeDtypeStruct((rows, 128), i32),
            jax.ShapeDtypeStruct(dyn_shape, f32),
        ),
        in_specs=[SMEM] + [ANY] * 5,
        out_specs=(ANY,) * 4,
        scratch_shapes=[pltpu.VMEM(x.shape, x.dtype) for x in fields]
        + [
            dma((9,)),
            dma((rows,)),
            pltpu.VMEM((rows * peers, cells), f32),
            pltpu.VMEM((rows, 128), i32),
            pltpu.VMEM((rows, 128), i32),
            pltpu.SMEM((rows, 128), i32),
            pltpu.VMEM(send_shape, bf16),
            pltpu.VMEM(dyn_shape, f32),
            pltpu.VMEM(block_shape, f32),
            pltpu.VMEM((columns + 8, levels), f32),
            pltpu.VMEM((columns, levels), f32),
            pltpu.VMEM((columns, levels), f32),
            pltpu.VMEM((columns, levels), f32),
            pltpu.VMEM((cells * kinds, levels), f32),
        ],
        compiler_params=params(64),
        cost_estimate=cost(BULK_COST),
        name="bulk",
    )(place, *fields)


    rim_args = (*edges, *far_edges, pos, dyn)
    both = lambda x: pltpu.VMEM((2,) + x.shape, x.dtype)
    send, rim = pl.pallas_call(
        functools.partial(rim_kernel, lats, lons),
        out_shape=(jax.ShapeDtypeStruct(send_shape, bf16), jax.ShapeDtypeStruct(rim_shape, f32)),
        in_specs=[SMEM] + [ANY] * 11,
        out_specs=(ANY, VMEM),
        scratch_shapes=[
            both(lon_a),
            both(lat_a),
            both(lon_a),
            both(lat_a),
            pltpu.SMEM((rows, 128), i32),
            pltpu.VMEM((2,) + dyn_shape[1:], f32),
            pltpu.VMEM((2, rows, kinds, levels), f32),
            pltpu.VMEM(rim_shape, f32),
            pltpu.VMEM(rim_shape, f32),
            pltpu.VMEM((2 * (rows + cells) - 4, kinds, levels), bf16),
            dma((14,)),
        ],
        input_output_aliases={11: 0},
        compiler_params=params(RIM_VMEM),
        name="rim",
    )(place, *rim_args, send)

    matrices, send = lax.optimization_barrier((inverses, send))
    inner = lax.ppermute(matrices, LON_AXES, opposite(lows // 2, lows))

    def exchange(x):
        x = x.reshape(peers, -1, kinds, levels)
        x = lax.all_to_all(x, GROUP_AXES, split_axis=0, concat_axis=0, tiled=True)
        return x.reshape(-1, kinds, levels)

    arrived = exchange(send)
    def turned(us, *arrays):
        return pl.pallas_call(
            turn_kernel,
            out_shape=jax.ShapeDtypeStruct((len(arrays) * owned, levels, levels), bf16),
            in_specs=[VMEM] * len(arrays),
            out_specs=VMEM,
            compiler_params=params(16),
            cost_estimate=cost(us),
            name="turn",
        )(*arrays)

    physics = pl.pallas_call(
        functools.partial(relax_kernel, lows),
        out_shape=jax.ShapeDtypeStruct((peers * cap, kinds, levels), bf16),
        in_specs=[SMEM] + [VMEM] * 3,
        out_specs=VMEM,
        scratch_shapes=[
            pltpu.VMEM((peers, 128), i32),
            pltpu.SMEM((peers, 128), i32),
            dma,
            pltpu.VMEM(((2 * owned * SLOTS + 1) * kinds, levels), f32),
        ],
        compiler_params=params(24),
        name="relax",
    )(place, arrived, turned(TURN_COST, inverses, outer), turned(INNER_COST, inner))

    returned = exchange(physics)
    return pl.pallas_call(
        finish_kernel,
        out_shape=jax.ShapeDtypeStruct((rows, cells, width), f32),
        in_specs=[SMEM, VMEM, VMEM, VMEM],
        out_specs=ANY,
        scratch_shapes=[
            pltpu.VMEM((cells * kinds, levels), f32),
            pltpu.VMEM((rows, cells, width), f32),
            dma((rows,)),
        ],
        compiler_params=params(16),
        name="finish",
    )(back, returned, dyn, rim)


def solution(mesh):
    lats, lons = mesh.devices.shape
    split = Mesh(mesh.devices.reshape(lats, 2, lons // 2), ("lat", "hi", "lo"))
    block = P("lat", LON_AXES, None)
    in_specs = (
        block,
        block,
        block,
        P("lat", LON_AXES),
        P("lat", LON_AXES),
        P(("lat", "hi", "lo"), None, None),
    )
    return jax.shard_map(shards, mesh=split, in_specs=in_specs, out_specs=block, check_vma=False)
```

```python
import functools

import jax
import jax.numpy as jnp
from jax import lax
from jax.experimental import pallas as pl
from jax.experimental.pallas import tpu as pltpu
from jax.sharding import Mesh
from jax.sharding import PartitionSpec as P

FLUX_COST = 10
TURN_COST = 30
INNER_COST = 1
SLOTS = 48
DIFFUSE = 0.1
GROUP_AXES = ("lat", "lo")
LON_AXES = ("hi", "lo")

VMEM = pl.BlockSpec(memory_space=pltpu.VMEM)
ANY = pl.BlockSpec(memory_space=pltpu.HBM)
SMEM = pl.BlockSpec(memory_space=pltpu.SMEM)


def log2(n):
    return n.bit_length() - 1


def parities(place, lons):
    return place & 1, (place >> log2(lons)) & 1


def edge_kernel(
    lons, place_ref, q_hbm, u_hbm, v_hbm, lon_a, lon_b, lat_a, lat_b, q_side, u_side, wide, sems
):
    rows, cells, width = q_hbm.shape
    side = q_side.shape[2]
    odd_lon, odd_lat = parities(place_ref[0], lons)
    copies = []

    def copy(source, target):
        copies.append(pltpu.make_async_copy(source, target, sems.at[len(copies)]))
        copies[-1].start()

    for n, odd in enumerate((odd_lon, 1 - odd_lon)):
        near = pl.ds(pl.multiple_of(jnp.where(odd == 1, 0, cells - side), side), side)
        copy(q_hbm.at[:, near, :], q_side.at[n])
        copy(u_hbm.at[:, near, :], u_side.at[n])
    for ref, odd in ((lat_a, odd_lat), (lat_b, 1 - odd_lat)):
        i = jnp.where(odd == 1, 0, rows - 1)
        copy(q_hbm.at[i], ref.at[:, 0:width])
        copy(v_hbm.at[i], ref.at[:, width:])
    for c in copies[:4]:
        c.wait()
    for n, (ref, odd) in enumerate(((lon_a, odd_lon), (lon_b, 1 - odd_lon))):
        first = odd == 1
        for i in range(rows):
            q, u = q_side[n, i].astype(jnp.float32), u_side[n, i].astype(jnp.float32)
            wide[i : i + 1, 0:width] = jnp.where(first, q[0:1], q[side - 1 :])
            wide[i : i + 1, width:] = jnp.where(first, u[0:1], u[side - 1 :])
        ref[...] = wide[...].astype(jnp.bfloat16)
    for c in copies[4:]:
        c.wait()


def plan(place_ref, span_ref, slot_ref, send_ref, pos_ref, member, pos, cap, owned, lons, lows):
    rows, cells = span_ref.shape
    stored = cap + 1
    peers = send_ref.shape[0] // stored
    f32, bf16 = jnp.float32, jnp.bfloat16
    span, slot = span_ref[...], slot_ref[...]
    owner = span >> log2(owned)
    owner_lon = owner & (lons - 1)
    far = (owner_lon >> log2(lows)) != ((place_ref[0] >> log2(lows)) & 1)
    low = (owner_lon & (lows - 1)) ^ jnp.where(far, lows // 2, 0)
    peer = ((owner >> log2(lons)) << log2(lows)) + low
    local = (span & (owned - 1)) + jnp.where(far, owned, 0)
    iota = lambda shape, axis: lax.broadcasted_iota(jnp.int32, shape, axis)
    for i in range(rows):
        member[i * peers : (i + 1) * peers, :] = jnp.where(
            iota((peers, cells), 0) == peer[i : i + 1], 1.0, 0.0
        )
    hot = member[...].astype(bf16)
    dot = functools.partial(jnp.dot, preferred_element_type=f32)
    within = dot(hot, (iota((cells, cells), 0) < iota((cells, cells), 1)).astype(f32).astype(bf16))
    pairs = (rows * peers, rows * peers)
    to, of = iota(pairs, 0), iota(pairs, 1)
    same = (to & (peers - 1)) == (of & (peers - 1))
    lower = jnp.where(same & (of < (to & -peers)), 1.0, 0.0).astype(bf16)
    before = within + jnp.sum(dot(lower, hot), axis=1, keepdims=True)
    before = before * member[...]
    lists = jnp.zeros((3 * peers, 128), f32)
    for i in range(rows):
        block = slice(i * peers, (i + 1) * peers)
        rank = jnp.sum(before[block], axis=0, keepdims=True).astype(jnp.int32)
        pos[i : i + 1, 0:cells] = peer[i : i + 1] * stored + rank
        pos_ref[i : i + 1, 0:cells] = peer[i : i + 1] * cap + rank
        chosen = jnp.where(iota((128, cells), 0) == rank, 1.0, 0.0).astype(bf16)
        mine = member[block]
        values = jnp.concatenate(
            [mine * local[i : i + 1].astype(f32), mine * slot[i : i + 1].astype(f32), mine], axis=0
        )
        lists = lists + lax.dot_general(
            values.astype(bf16), chosen, (((1,), (1,)), ((), ())), preferred_element_type=f32
        )
    spans = jnp.where(lists[2 * peers :] > 0.5, lists[:peers], 2.0 * owned)
    slots = lists[peers : 2 * peers]
    tile = send_ref.shape[1:]
    for p in range(peers):
        send_ref[p * stored + cap] = jnp.where(
            iota(tile, 0) == 0,
            jnp.broadcast_to(spans[p : p + 1], tile),
            jnp.broadcast_to(slots[p : p + 1], tile),
        ).astype(bf16)


def flux_kernel(
    cap,
    owned,
    lats,
    lons,
    lows,
    place_ref,
    *refs,
):
    sources, (send_hbm, back_hbm, dyn_hbm), rest = refs[:9], refs[9:12], refs[12:]
    held, rest = rest[:7], rest[7:]
    (
        sems,
        row_sems,
        member,
        back,
        pos,
        pos_s,
        send_ref,
        dyn_ref,
        cell,
        wind,
        face_x,
        wind_y,
        face_y,
        edge,
        flux_y,
    ) = rest
    span_ref, slot_ref, q_ref, u_ref, v_ref, lon_ref, lat_ref = held
    west_ref, east_ref = lon_ref.at[0], lon_ref.at[1]
    south_ref, north_ref = lat_ref.at[0], lat_ref.at[1]
    odd_lon, odd_lat = parities(place_ref[0], lons)
    targets = held[:5] + (
        lon_ref.at[1 - odd_lon],
        lon_ref.at[odd_lon],
        lat_ref.at[1 - odd_lat],
        lat_ref.at[odd_lat],
    )
    rows, cells, width = q_ref.shape
    levels = u_ref.shape[2]
    tracers = width // levels
    f32 = jnp.float32
    line = (cells + 2) * tracers
    copies = [pltpu.make_async_copy(a, b, sems.at[n]) for n, (a, b) in enumerate(zip(sources, targets))]
    for copy in copies:
        copy.start()

    def spread(block, first, count, stride):
        for t in range(tracers):
            cell[pl.ds(first + t, count, stride=stride), :] = block(t).astype(f32)

    lanes = lambda t: slice(t * levels, (t + 1) * levels)
    for copy in copies[:2]:
        copy.wait()
    plan(place_ref, span_ref, slot_ref, send_ref, back, member, pos, cap, owned, lons, lows)
    pos_copy = pltpu.make_async_copy(pos, pos_s, sems.at[len(copies)])
    pos_copy.start()
    back_copy = pltpu.make_async_copy(back, back_hbm, sems.at[len(copies) + 1])
    back_copy.start()
    copies[2].wait()

    def relayout(i, carry):
        spread(
            lambda t: q_ref[i, :, lanes(t)], (i + 1) * line + tracers, cells, tracers
        )
        return carry

    lax.fori_loop(0, rows, relayout, 0)
    for copy in copies[3:]:
        copy.wait()
    spread(lambda t: south_ref[:, lanes(t)], tracers, cells, tracers)
    spread(lambda t: north_ref[:, lanes(t)], (rows + 1) * line + tracers, cells, tracers)
    spread(lambda t: west_ref[:, lanes(t)], line, rows, line)
    spread(lambda t: east_ref[:, lanes(t)], line + (cells + 1) * tracers, rows, line)

    edge[0:rows, :] = west_ref[:, width:].astype(f32)
    edge[rows : 2 * rows, :] = east_ref[:, width:].astype(f32)
    stride = face_x.shape[0] // rows

    def faces(i, carry):
        wind[0:1, :] = edge[pl.ds(i, 1), :]
        wind[1 : cells + 1, :] = u_ref[i].astype(f32)
        wind[cells + 1 : cells + 2, :] = edge[pl.ds(rows + i, 1), :]
        face_x[pl.ds(pl.multiple_of(i * stride, 8), stride), :] = 0.25 * (
            wind[0:stride, :] + wind[1 : stride + 1, :]
        )
        return carry

    lax.fori_loop(0, rows, faces, 0)
    wind_y[0:cells, :] = south_ref[:, width:].astype(f32)
    wind_y[cells : (rows + 1) * cells, :] = v_ref[...].reshape(rows * cells, levels).astype(f32)
    wind_y[(rows + 1) * cells :, :] = north_ref[:, width:].astype(f32)
    face_y[...] = 0.25 * (wind_y[: (rows + 1) * cells, :] + wind_y[cells:, :])
    lat = place_ref[0] >> log2(lons)
    south_open = jnp.where(lat > 0, 1.0, 0.0)
    north_open = jnp.where(lat < lats - 1, 1.0, 0.0)
    face_y[0:cells, :] = face_y[0:cells, :] * south_open
    face_y[rows * cells :, :] = face_y[rows * cells :, :] * north_open

    def tile(i, j):
        first = (i * (cells + 2) + j) * tracers
        return cell[pl.ds(pl.multiple_of(first, tracers), tracers), :]

    def spread_row(ref, r):
        return jnp.broadcast_to(ref[pl.ds(r, 1), :], (tracers, levels))

    for j in range(cells):
        low, high = tile(0, j + 1), tile(1, j + 1)
        flux_y[j * tracers : (j + 1) * tracers, :] = spread_row(face_y, j) * (low + high) - (
            DIFFUSE * south_open
        ) * (high - low)

    pos_copy.wait()

    def dyn_copy(i):
        return pltpu.make_async_copy(dyn_ref.at[i], dyn_hbm.at[i], row_sems.at[i])

    def row(i, carry):
        diffuse_y = DIFFUSE * jnp.where(i == rows - 1, north_open, 1.0)
        here = tile(i + 1, 1)
        last = tile(i + 1, 0)
        flux_w = spread_row(face_x, i * stride) * (last + here) - DIFFUSE * (here - last)
        for j in range(cells):
            after = tile(i + 1, j + 2)
            flux_e = spread_row(face_x, i * stride + j + 1) * (here + after) - DIFFUSE * (
                after - here
            )
            above = tile(i + 2, j + 1)
            flux_n = spread_row(face_y, (i + 1) * cells + j) * (here + above) - diffuse_y * (
                above - here
            )
            flux_s = flux_y[j * tracers : (j + 1) * tracers, :]
            flux_y[j * tracers : (j + 1) * tracers, :] = flux_n
            dyn = (flux_w - flux_e) + (flux_s - flux_n)
            dyn_ref[i, j * tracers : (j + 1) * tracers, :] = dyn
            send_ref[pos_s[i, j]] = (here + dyn).astype(jnp.bfloat16)
            here, flux_w = after, flux_e
        dyn_copy(i).start()
        return carry

    lax.fori_loop(0, rows, row, 0)

    send_copy = pltpu.make_async_copy(send_ref, send_hbm, sems.at[len(copies) + 2])
    send_copy.start()
    back_copy.wait()

    def drain(i, carry):
        dyn_copy(i).wait()
        return carry

    lax.fori_loop(0, rows, drain, 0)
    send_copy.wait()


def turn_kernel(*refs):
    refs, out_ref = refs[:-1], refs[-1]
    for n, ref in enumerate(refs):
        for k in range(ref.shape[0]):
            out_ref[n * ref.shape[0] + k] = ref[k].T


def relax_kernel(lows, place_ref, x_ref, outer_ref, inner_ref, y_ref, pos, pos_s, sem, slots):
    tracers, levels = x_ref.shape[1:]
    peers, lanes = pos.shape
    stored = x_ref.shape[0] // peers
    cap = stored - 1
    f32 = jnp.float32
    for p in range(peers):
        listed = x_ref[p * stored + cap].astype(f32)
        pos[p : p + 1, :] = (listed[0:1] * SLOTS + listed[1:2]).astype(jnp.int32)
    copy = pltpu.make_async_copy(pos, pos_s, sem)
    copy.start()
    copy.wait()

    def tile(at):
        return pl.ds(pl.multiple_of(at * tracers, tracers), tracers)

    def scatter(p, carry):
        for r in range(cap):
            slots[tile(pos_s[p, r]), :] = x_ref[p * stored + r].astype(f32)
        return carry

    lax.fori_loop(0, peers, scatter, 0)
    block = SLOTS * tracers

    def relax(first, count, w_ref, w_first):
        def span(k, carry):
            at = pl.ds(pl.multiple_of((first + k) * block, block), block)
            x = slots[at, :]
            y = jnp.dot(x.astype(jnp.bfloat16), w_ref[w_first + k], preferred_element_type=f32)
            slots[at, :] = y - x
            return carry

        lax.fori_loop(0, count, span, 0, unroll=8)

    owned = inner_ref.shape[0]
    place = place_ref[0]
    is_outer = ((place >> log2(lows)) & 1) == ((place >> (log2(lows) - 1)) & 1)
    relax(0, owned, outer_ref, 0)

    @pl.when(is_outer)
    def _():
        relax(owned, owned, outer_ref, owned)

    @pl.when(jnp.logical_not(is_outer))
    def _():
        relax(owned, owned, inner_ref, 0)

    def gather(p, carry):
        for r in range(cap):
            y_ref[p * cap + r] = slots[tile(pos_s[p, r]), :].astype(jnp.bfloat16)
        return carry

    lax.fori_loop(0, peers, gather, 0)


def finish_kernel(pos_ref, y_ref, dyn_ref, out_hbm, total, out, sems):
    rows, cells, width = out.shape
    tracers, levels = y_ref.shape[1:]

    def copy(i):
        return pltpu.make_async_copy(out.at[i], out_hbm.at[i], sems.at[i])

    def row(i, carry):
        for j in range(cells):
            tile = slice(j * tracers, (j + 1) * tracers)
            total[tile, :] = dyn_ref[i, tile, :] + y_ref[pos_ref[i, j]].astype(jnp.float32)
        for t in range(tracers):
            out[i, :, t * levels : (t + 1) * levels] = total[pl.ds(t, cells, stride=tracers), :]
        copy(i).start()
        return carry

    lax.fori_loop(0, rows, row, 0)
    for i in range(rows):
        copy(i).wait()


def in_pairs(x, axis, first):
    count = lax.axis_size(axis)
    pairs = [(i % count, (i + 1) % count) for i in range(first, count + first, 2)]
    return lax.ppermute(x, axis, pairs + [(b, a) for a, b in pairs])


def shards(tracers, east_wind, north_wind, span_of, slot_of, inverses):
    levels = east_wind.shape[2]
    rows, cells, width = tracers.shape
    kinds = width // levels
    columns = rows * cells
    lats, lows = lax.axis_size("lat"), lax.axis_size("lo")
    lons = lax.axis_size("hi") * lows
    peers = lats * lows
    owned = inverses.shape[0]
    cap = 2 * (3 * columns // (2 * lats * lons))
    stored = cap + 1
    f32, bf16, i32 = jnp.float32, jnp.bfloat16, jnp.int32
    dma = pltpu.SemaphoreType.DMA
    params = lambda mib: pltpu.CompilerParams(vmem_limit_bytes=mib << 20)

    side = 8
    place = lax.axis_index(("lat", "hi", "lo")).astype(i32).reshape(1)
    lon_a, lon_b, lat_a, lat_b = pl.pallas_call(
        functools.partial(edge_kernel, lons),
        out_shape=(jax.ShapeDtypeStruct((rows, width + levels), bf16),) * 2
        + (jax.ShapeDtypeStruct((cells, width + levels), bf16),) * 2,
        in_specs=[SMEM] + [ANY] * 3,
        out_specs=(VMEM,) * 4,
        scratch_shapes=[
            pltpu.VMEM((2, rows, side, width), bf16),
            pltpu.VMEM((2, rows, side, levels), bf16),
            pltpu.VMEM((rows, width + levels), f32),
            dma((8,)),
        ],
        compiler_params=params(64),
        name="edges",
    )(place, tracers, east_wind, north_wind)
    far_edges = (
        in_pairs(lon_a, LON_AXES, 0),
        in_pairs(lon_b, LON_AXES, 1),
        in_pairs(lat_a, "lat", 0),
        in_pairs(lat_b, "lat", 1),
    )

    def opposite(start, stop):
        pairs = [(lo, lows + (lo ^ lows // 2)) for lo in range(start, stop)]
        return pairs + [(b, a) for a, b in pairs]

    outer = lax.ppermute(inverses, LON_AXES, opposite(0, lows // 2))
    cost = lambda us: pl.CostEstimate(
        flops=us * 1_000_000_000, bytes_accessed=1 << 20, transcendentals=0
    )
    fields = (span_of, slot_of, tracers, east_wind, north_wind, *far_edges)
    held = [(x.shape, x.dtype) for x in fields[:5]]
    held += [((2,) + x.shape, x.dtype) for x in (lon_a, lat_a)]
    stride = (cells + 1 + 7) // 8 * 8
    dyn_shape = (rows, cells * kinds, levels)
    send_shape = (peers * stored, kinds, levels)
    send, back, dyn = pl.pallas_call(
        functools.partial(flux_kernel, cap, owned, lats, lons, lows),
        out_shape=(
            jax.ShapeDtypeStruct(send_shape, bf16),
            jax.ShapeDtypeStruct((rows, 128), i32),
            jax.ShapeDtypeStruct(dyn_shape, f32),
        ),
        in_specs=[SMEM] + [ANY] * 9,
        out_specs=(ANY,) * 3,
        scratch_shapes=[pltpu.VMEM(*x) for x in held]
        + [
            dma((12,)),
            dma((rows,)),
            pltpu.VMEM((rows * peers, cells), f32),
            pltpu.VMEM((rows, 128), i32),
            pltpu.VMEM((rows, 128), i32),
            pltpu.SMEM((rows, 128), i32),
            pltpu.VMEM(send_shape, bf16),
            pltpu.VMEM(dyn_shape, f32),
            pltpu.VMEM(((rows + 2) * (cells + 2) * kinds, levels), f32),
            pltpu.VMEM((stride + 8, levels), f32),
            pltpu.VMEM((rows * stride, levels), f32),
            pltpu.VMEM(((rows + 2) * cells, levels), f32),
            pltpu.VMEM(((rows + 1) * cells, levels), f32),
            pltpu.VMEM((2 * rows, levels), f32),
            pltpu.VMEM((cells * kinds, levels), f32),
        ],
        compiler_params=params(64),
        cost_estimate=cost(FLUX_COST),
        name="flux",
    )(place, *fields)

    matrices, send = lax.optimization_barrier((inverses, send))
    inner = lax.ppermute(matrices, LON_AXES, opposite(lows // 2, lows))

    def exchange(x):
        x = x.reshape(peers, -1, kinds, levels)
        x = lax.all_to_all(x, GROUP_AXES, split_axis=0, concat_axis=0, tiled=True)
        return x.reshape(-1, kinds, levels)

    arrived = exchange(send)
    def turned(us, *arrays):
        return pl.pallas_call(
            turn_kernel,
            out_shape=jax.ShapeDtypeStruct((len(arrays) * owned, levels, levels), bf16),
            in_specs=[VMEM] * len(arrays),
            out_specs=VMEM,
            compiler_params=params(16),
            cost_estimate=cost(us),
            name="turn",
        )(*arrays)

    physics = pl.pallas_call(
        functools.partial(relax_kernel, lows),
        out_shape=jax.ShapeDtypeStruct((peers * cap, kinds, levels), bf16),
        in_specs=[SMEM] + [VMEM] * 3,
        out_specs=VMEM,
        scratch_shapes=[
            pltpu.VMEM((peers, 128), i32),
            pltpu.SMEM((peers, 128), i32),
            dma,
            pltpu.VMEM(((2 * owned * SLOTS + 1) * kinds, levels), f32),
        ],
        compiler_params=params(24),
        name="relax",
    )(place, arrived, turned(TURN_COST, inverses, outer), turned(INNER_COST, inner))

    returned = exchange(physics)
    return pl.pallas_call(
        finish_kernel,
        out_shape=jax.ShapeDtypeStruct((rows, cells, width), f32),
        in_specs=[SMEM, VMEM, VMEM],
        out_specs=ANY,
        scratch_shapes=[
            pltpu.VMEM((cells * kinds, levels), f32),
            pltpu.VMEM((rows, cells, width), f32),
            dma((rows,)),
        ],
        compiler_params=params(16),
        name="finish",
    )(back, returned, dyn)


def solution(mesh):
    lats, lons = mesh.devices.shape
    split = Mesh(mesh.devices.reshape(lats, 2, lons // 2), ("lat", "hi", "lo"))
    block = P("lat", LON_AXES, None)
    in_specs = (
        block,
        block,
        block,
        P("lat", LON_AXES),
        P("lat", LON_AXES),
        P(("lat", "hi", "lo"), None, None),
    )
    return jax.shard_map(shards, mesh=split, in_specs=in_specs, out_specs=block, check_vma=False)
```

```python
import functools

import jax
import jax.numpy as jnp
from jax import lax
from jax.experimental import pallas as pl
from jax.experimental.pallas import tpu as pltpu
from jax.sharding import Mesh
from jax.sharding import PartitionSpec as P

FLUX_COST = 10
TURN_COST = 30
INNER_COST = 1
SLOTS = 48
DIFFUSE = 0.1
GROUP_AXES = ("lat", "lo")
LON_AXES = ("hi", "lo")

VMEM = pl.BlockSpec(memory_space=pltpu.VMEM)
ANY = pl.BlockSpec(memory_space=pltpu.HBM)
SMEM = pl.BlockSpec(memory_space=pltpu.SMEM)


def log2(n):
    return n.bit_length() - 1


def parities(place, lons):
    return place & 1, (place >> log2(lons)) & 1


def edge_kernel(
    lons, place_ref, q_hbm, u_hbm, v_hbm, lon_a, lon_b, lat_a, lat_b, q_side, u_side, wide, ready, row, sems
):
    rows, cells, width = q_hbm.shape
    side = q_side.shape[2]
    odd_lon, odd_lat = parities(place_ref[0], lons)
    copies = []

    def copy(source, target):
        copies.append(pltpu.make_async_copy(source, target, sems.at[len(copies)]))
        copies[-1].start()

    for n, odd in enumerate((odd_lon, 1 - odd_lon)):
        near = pl.ds(pl.multiple_of(jnp.where(odd == 1, 0, cells - side), side), side)
        copy(q_hbm.at[:, near, :], q_side.at[n])
        copy(u_hbm.at[:, near, :], u_side.at[n])
    for n, odd in enumerate((odd_lat, 1 - odd_lat)):
        i = jnp.where(odd == 1, 0, rows - 1)
        copy(q_hbm.at[i], row.at[n, :, 0:width])
        copy(v_hbm.at[i], row.at[n, :, width:])
    for c in copies[4:]:
        c.wait()
    copy(row.at[0], lat_a)
    copy(row.at[1], lat_b)
    for c in copies[:4]:
        c.wait()
    for n, (ref, odd) in enumerate(((lon_a, odd_lon), (lon_b, 1 - odd_lon))):
        first = odd == 1
        for i in range(rows):
            q, u = q_side[n, i].astype(jnp.float32), u_side[n, i].astype(jnp.float32)
            wide[i : i + 1, 0:width] = jnp.where(first, q[0:1], q[side - 1 :])
            wide[i : i + 1, width:] = jnp.where(first, u[0:1], u[side - 1 :])
        ready[n] = wide[...].astype(jnp.bfloat16)
        copy(ready.at[n], ref)
    for c in copies[8:]:
        c.wait()


def plan(place_ref, span_ref, slot_ref, send_ref, pos_ref, member, pos, cap, owned, lons, lows):
    rows, cells = span_ref.shape
    stored = cap + 1
    peers = send_ref.shape[0] // stored
    f32, bf16 = jnp.float32, jnp.bfloat16
    span, slot = span_ref[...], slot_ref[...]
    owner = span >> log2(owned)
    owner_lon = owner & (lons - 1)
    far = (owner_lon >> log2(lows)) != ((place_ref[0] >> log2(lows)) & 1)
    low = (owner_lon & (lows - 1)) ^ jnp.where(far, lows // 2, 0)
    peer = ((owner >> log2(lons)) << log2(lows)) + low
    local = (span & (owned - 1)) + jnp.where(far, owned, 0)
    iota = lambda shape, axis: lax.broadcasted_iota(jnp.int32, shape, axis)
    for i in range(rows):
        member[i * peers : (i + 1) * peers, :] = jnp.where(
            iota((peers, cells), 0) == peer[i : i + 1], 1.0, 0.0
        )
    hot = member[...].astype(bf16)
    dot = functools.partial(jnp.dot, preferred_element_type=f32)
    within = dot(hot, (iota((cells, cells), 0) < iota((cells, cells), 1)).astype(f32).astype(bf16))
    pairs = (rows * peers, rows * peers)
    to, of = iota(pairs, 0), iota(pairs, 1)
    same = (to & (peers - 1)) == (of & (peers - 1))
    lower = jnp.where(same & (of < (to & -peers)), 1.0, 0.0).astype(bf16)
    before = within + jnp.sum(dot(lower, hot), axis=1, keepdims=True)
    before = before * member[...]
    lists = jnp.zeros((3 * peers, 128), f32)
    for i in range(rows):
        block = slice(i * peers, (i + 1) * peers)
        rank = jnp.sum(before[block], axis=0, keepdims=True).astype(jnp.int32)
        pos[i : i + 1, 0:cells] = peer[i : i + 1] * stored + rank
        pos_ref[i : i + 1, 0:cells] = peer[i : i + 1] * cap + rank
        chosen = jnp.where(iota((128, cells), 0) == rank, 1.0, 0.0).astype(bf16)
        mine = member[block]
        values = jnp.concatenate(
            [mine * local[i : i + 1].astype(f32), mine * slot[i : i + 1].astype(f32), mine], axis=0
        )
        lists = lists + lax.dot_general(
            values.astype(bf16), chosen, (((1,), (1,)), ((), ())), preferred_element_type=f32
        )
    spans = jnp.where(lists[2 * peers :] > 0.5, lists[:peers], 2.0 * owned)
    slots = lists[peers : 2 * peers]
    tile = send_ref.shape[1:]
    for p in range(peers):
        send_ref[p * stored + cap] = jnp.where(
            iota(tile, 0) == 0,
            jnp.broadcast_to(spans[p : p + 1], tile),
            jnp.broadcast_to(slots[p : p + 1], tile),
        ).astype(bf16)


def flux_kernel(
    cap,
    owned,
    lats,
    lons,
    lows,
    place_ref,
    *refs,
):
    sources, (send_hbm, back_hbm, dyn_hbm), rest = refs[:9], refs[9:12], refs[12:]
    held, rest = rest[:7], rest[7:]
    (
        sems,
        row_sems,
        member,
        back,
        pos,
        pos_s,
        send_ref,
        dyn_ref,
        cell,
        wind,
        face_x,
        wind_y,
        face_y,
        edge,
        flux_y,
    ) = rest
    span_ref, slot_ref, q_ref, u_ref, v_ref, lon_ref, lat_ref = held
    west_ref, east_ref = lon_ref.at[0], lon_ref.at[1]
    south_ref, north_ref = lat_ref.at[0], lat_ref.at[1]
    odd_lon, odd_lat = parities(place_ref[0], lons)
    targets = held[:5] + (
        lon_ref.at[1 - odd_lon],
        lon_ref.at[odd_lon],
        lat_ref.at[1 - odd_lat],
        lat_ref.at[odd_lat],
    )
    rows, cells, width = q_ref.shape
    levels = u_ref.shape[2]
    tracers = width // levels
    f32 = jnp.float32
    line = (cells + 2) * tracers
    copies = [pltpu.make_async_copy(a, b, sems.at[n]) for n, (a, b) in enumerate(zip(sources, targets))]
    for copy in copies:
        copy.start()

    def spread(block, first, count, stride):
        for t in range(tracers):
            cell[pl.ds(first + t, count, stride=stride), :] = block(t).astype(f32)

    lanes = lambda t: slice(t * levels, (t + 1) * levels)
    for copy in copies[:2]:
        copy.wait()
    plan(place_ref, span_ref, slot_ref, send_ref, back, member, pos, cap, owned, lons, lows)
    pos_copy = pltpu.make_async_copy(pos, pos_s, sems.at[len(copies)])
    pos_copy.start()
    back_copy = pltpu.make_async_copy(back, back_hbm, sems.at[len(copies) + 1])
    back_copy.start()
    copies[2].wait()

    def relayout(i, carry):
        spread(
            lambda t: q_ref[i, :, lanes(t)], (i + 1) * line + tracers, cells, tracers
        )
        return carry

    lax.fori_loop(0, rows, relayout, 0)
    for copy in copies[3:]:
        copy.wait()
    spread(lambda t: south_ref[:, lanes(t)], tracers, cells, tracers)
    spread(lambda t: north_ref[:, lanes(t)], (rows + 1) * line + tracers, cells, tracers)
    spread(lambda t: west_ref[:, lanes(t)], line, rows, line)
    spread(lambda t: east_ref[:, lanes(t)], line + (cells + 1) * tracers, rows, line)

    edge[0:rows, :] = west_ref[:, width:].astype(f32)
    edge[rows : 2 * rows, :] = east_ref[:, width:].astype(f32)
    stride = face_x.shape[0] // rows

    def faces(i, carry):
        wind[0:1, :] = edge[pl.ds(i, 1), :]
        wind[1 : cells + 1, :] = u_ref[i].astype(f32)
        wind[cells + 1 : cells + 2, :] = edge[pl.ds(rows + i, 1), :]
        face_x[pl.ds(pl.multiple_of(i * stride, 8), stride), :] = 0.25 * (
            wind[0:stride, :] + wind[1 : stride + 1, :]
        )
        return carry

    lax.fori_loop(0, rows, faces, 0)
    wind_y[0:cells, :] = south_ref[:, width:].astype(f32)
    wind_y[cells : (rows + 1) * cells, :] = v_ref[...].reshape(rows * cells, levels).astype(f32)
    wind_y[(rows + 1) * cells :, :] = north_ref[:, width:].astype(f32)
    face_y[...] = 0.25 * (wind_y[: (rows + 1) * cells, :] + wind_y[cells:, :])
    lat = place_ref[0] >> log2(lons)
    south_open = jnp.where(lat > 0, 1.0, 0.0)
    north_open = jnp.where(lat < lats - 1, 1.0, 0.0)
    face_y[0:cells, :] = face_y[0:cells, :] * south_open
    face_y[rows * cells :, :] = face_y[rows * cells :, :] * north_open

    def tile(i, j):
        first = (i * (cells + 2) + j) * tracers
        return cell[pl.ds(pl.multiple_of(first, tracers), tracers), :]

    def spread_row(ref, r):
        return jnp.broadcast_to(ref[pl.ds(r, 1), :], (tracers, levels))

    for j in range(cells):
        low, high = tile(0, j + 1), tile(1, j + 1)
        flux_y[j * tracers : (j + 1) * tracers, :] = spread_row(face_y, j) * (low + high) - (
            DIFFUSE * south_open
        ) * (high - low)

    pos_copy.wait()

    def dyn_copy(i):
        return pltpu.make_async_copy(dyn_ref.at[i], dyn_hbm.at[i], row_sems.at[i])

    def row(i, carry):
        diffuse_y = DIFFUSE * jnp.where(i == rows - 1, north_open, 1.0)
        here = tile(i + 1, 1)
        last = tile(i + 1, 0)
        flux_w = spread_row(face_x, i * stride) * (last + here) - DIFFUSE * (here - last)
        for j in range(cells):
            after = tile(i + 1, j + 2)
            flux_e = spread_row(face_x, i * stride + j + 1) * (here + after) - DIFFUSE * (
                after - here
            )
            above = tile(i + 2, j + 1)
            flux_n = spread_row(face_y, (i + 1) * cells + j) * (here + above) - diffuse_y * (
                above - here
            )
            flux_s = flux_y[j * tracers : (j + 1) * tracers, :]
            flux_y[j * tracers : (j + 1) * tracers, :] = flux_n
            dyn = (flux_w - flux_e) + (flux_s - flux_n)
            dyn_ref[i, j * tracers : (j + 1) * tracers, :] = dyn
            send_ref[pos_s[i, j]] = (here + dyn).astype(jnp.bfloat16)
            here, flux_w = after, flux_e
        dyn_copy(i).start()
        return carry

    lax.fori_loop(0, rows, row, 0)

    send_copy = pltpu.make_async_copy(send_ref, send_hbm, sems.at[len(copies) + 2])
    send_copy.start()
    back_copy.wait()

    def drain(i, carry):
        dyn_copy(i).wait()
        return carry

    lax.fori_loop(0, rows, drain, 0)
    send_copy.wait()


def turn_kernel(*refs):
    refs, out_ref = refs[:-1], refs[-1]
    for n, ref in enumerate(refs):
        for k in range(ref.shape[0]):
            out_ref[n * ref.shape[0] + k] = ref[k].T


def relax_kernel(lows, place_ref, x_ref, outer_ref, inner_ref, y_ref, pos, pos_s, sem, slots):
    tracers, levels = x_ref.shape[1:]
    peers, lanes = pos.shape
    stored = x_ref.shape[0] // peers
    cap = stored - 1
    f32 = jnp.float32
    for p in range(peers):
        listed = x_ref[p * stored + cap].astype(f32)
        pos[p : p + 1, :] = (listed[0:1] * SLOTS + listed[1:2]).astype(jnp.int32)
    copy = pltpu.make_async_copy(pos, pos_s, sem)
    copy.start()
    copy.wait()

    def tile(at):
        return pl.ds(pl.multiple_of(at * tracers, tracers), tracers)

    def scatter(p, carry):
        for r in range(cap):
            slots[tile(pos_s[p, r]), :] = x_ref[p * stored + r].astype(f32)
        return carry

    lax.fori_loop(0, peers, scatter, 0, unroll=4)
    block = SLOTS * tracers

    def relax(first, count, w_ref, w_first):
        def span(k, carry):
            at = pl.ds(pl.multiple_of((first + k) * block, block), block)
            x = slots[at, :]
            y = jnp.dot(x.astype(jnp.bfloat16), w_ref[w_first + k], preferred_element_type=f32)
            slots[at, :] = y - x
            return carry

        lax.fori_loop(0, count, span, 0, unroll=16)

    owned = inner_ref.shape[0]
    place = place_ref[0]
    is_outer = ((place >> log2(lows)) & 1) == ((place >> (log2(lows) - 1)) & 1)
    relax(0, owned, outer_ref, 0)

    @pl.when(is_outer)
    def _():
        relax(owned, owned, outer_ref, owned)

    @pl.when(jnp.logical_not(is_outer))
    def _():
        relax(owned, owned, inner_ref, 0)

    def gather(p, carry):
        for r in range(cap):
            y_ref[p * cap + r] = slots[tile(pos_s[p, r]), :].astype(jnp.bfloat16)
        return carry

    lax.fori_loop(0, peers, gather, 0, unroll=4)


def finish_kernel(pos_ref, y_ref, dyn_ref, out_hbm, total, out, sems):
    rows, cells, width = out.shape
    tracers, levels = y_ref.shape[1:]

    def copy(i):
        return pltpu.make_async_copy(out.at[i], out_hbm.at[i], sems.at[i])

    def row(i, carry):
        for j in range(cells):
            tile = slice(j * tracers, (j + 1) * tracers)
            total[tile, :] = dyn_ref[i, tile, :] + y_ref[pos_ref[i, j]].astype(jnp.float32)
        for t in range(tracers):
            out[i, :, t * levels : (t + 1) * levels] = total[pl.ds(t, cells, stride=tracers), :]
        copy(i).start()
        return carry

    lax.fori_loop(0, rows, row, 0)
    for i in range(rows):
        copy(i).wait()


def in_pairs(x, axis, first):
    count = lax.axis_size(axis)
    pairs = [(i % count, (i + 1) % count) for i in range(first, count + first, 2)]
    return lax.ppermute(x, axis, pairs + [(b, a) for a, b in pairs])


def shards(tracers, east_wind, north_wind, span_of, slot_of, inverses):
    levels = east_wind.shape[2]
    rows, cells, width = tracers.shape
    kinds = width // levels
    columns = rows * cells
    lats, lows = lax.axis_size("lat"), lax.axis_size("lo")
    lons = lax.axis_size("hi") * lows
    peers = lats * lows
    owned = inverses.shape[0]
    cap = 2 * (3 * columns // (2 * lats * lons))
    stored = cap + 1
    f32, bf16, i32 = jnp.float32, jnp.bfloat16, jnp.int32
    dma = pltpu.SemaphoreType.DMA
    params = lambda mib: pltpu.CompilerParams(vmem_limit_bytes=mib << 20)

    side = 8
    place = lax.axis_index(("lat", "hi", "lo")).astype(i32).reshape(1)
    lon_a, lon_b, lat_a, lat_b = pl.pallas_call(
        functools.partial(edge_kernel, lons),
        out_shape=(jax.ShapeDtypeStruct((rows, width + levels), bf16),) * 2
        + (jax.ShapeDtypeStruct((cells, width + levels), bf16),) * 2,
        in_specs=[SMEM] + [ANY] * 3,
        out_specs=(ANY,) * 4,
        scratch_shapes=[
            pltpu.VMEM((2, rows, side, width), bf16),
            pltpu.VMEM((2, rows, side, levels), bf16),
            pltpu.VMEM((rows, width + levels), f32),
            pltpu.VMEM((2, rows, width + levels), bf16),
            pltpu.VMEM((2, cells, width + levels), bf16),
            dma((12,)),
        ],
        compiler_params=params(64),
        name="edges",
    )(place, tracers, east_wind, north_wind)
    far_edges = (
        in_pairs(lon_a, LON_AXES, 0),
        in_pairs(lon_b, LON_AXES, 1),
        in_pairs(lat_a, "lat", 0),
        in_pairs(lat_b, "lat", 1),
    )

    def opposite(start, stop):
        pairs = [(lo, lows + (lo ^ lows // 2)) for lo in range(start, stop)]
        return pairs + [(b, a) for a, b in pairs]

    outer = lax.ppermute(inverses, LON_AXES, opposite(0, lows // 2))
    cost = lambda us: pl.CostEstimate(
        flops=us * 1_000_000_000, bytes_accessed=1 << 20, transcendentals=0
    )
    fields = (span_of, slot_of, tracers, east_wind, north_wind, *far_edges)
    held = [(x.shape, x.dtype) for x in fields[:5]]
    held += [((2,) + x.shape, x.dtype) for x in (lon_a, lat_a)]
    stride = (cells + 1 + 7) // 8 * 8
    dyn_shape = (rows, cells * kinds, levels)
    send_shape = (peers * stored, kinds, levels)
    send, back, dyn = pl.pallas_call(
        functools.partial(flux_kernel, cap, owned, lats, lons, lows),
        out_shape=(
            jax.ShapeDtypeStruct(send_shape, bf16),
            jax.ShapeDtypeStruct((rows, 128), i32),
            jax.ShapeDtypeStruct(dyn_shape, f32),
        ),
        in_specs=[SMEM] + [ANY] * 9,
        out_specs=(ANY,) * 3,
        scratch_shapes=[pltpu.VMEM(*x) for x in held]
        + [
            dma((12,)),
            dma((rows,)),
            pltpu.VMEM((rows * peers, cells), f32),
            pltpu.VMEM((rows, 128), i32),
            pltpu.VMEM((rows, 128), i32),
            pltpu.SMEM((rows, 128), i32),
            pltpu.VMEM(send_shape, bf16),
            pltpu.VMEM(dyn_shape, f32),
            pltpu.VMEM(((rows + 2) * (cells + 2) * kinds, levels), f32),
            pltpu.VMEM((stride + 8, levels), f32),
            pltpu.VMEM((rows * stride, levels), f32),
            pltpu.VMEM(((rows + 2) * cells, levels), f32),
            pltpu.VMEM(((rows + 1) * cells, levels), f32),
            pltpu.VMEM((2 * rows, levels), f32),
            pltpu.VMEM((cells * kinds, levels), f32),
        ],
        compiler_params=params(64),
        cost_estimate=cost(FLUX_COST),
        name="flux",
    )(place, *fields)

    matrices, send = lax.optimization_barrier((inverses, send))
    inner = lax.ppermute(matrices, LON_AXES, opposite(lows // 2, lows))

    def exchange(x):
        x = x.reshape(peers, -1, kinds, levels)
        x = lax.all_to_all(x, GROUP_AXES, split_axis=0, concat_axis=0, tiled=True)
        return x.reshape(-1, kinds, levels)

    arrived = exchange(send)
    def turned(us, *arrays):
        return pl.pallas_call(
            turn_kernel,
            out_shape=jax.ShapeDtypeStruct((len(arrays) * owned, levels, levels), bf16),
            in_specs=[VMEM] * len(arrays),
            out_specs=VMEM,
            compiler_params=params(16),
            cost_estimate=cost(us),
            name="turn",
        )(*arrays)

    physics = pl.pallas_call(
        functools.partial(relax_kernel, lows),
        out_shape=jax.ShapeDtypeStruct((peers * cap, kinds, levels), bf16),
        in_specs=[SMEM] + [VMEM] * 3,
        out_specs=VMEM,
        scratch_shapes=[
            pltpu.VMEM((peers, 128), i32),
            pltpu.SMEM((peers, 128), i32),
            dma,
            pltpu.VMEM(((2 * owned * SLOTS + 1) * kinds, levels), f32),
        ],
        compiler_params=params(24),
        name="relax",
    )(place, arrived, turned(TURN_COST, inverses, outer), turned(INNER_COST, inner))

    returned = exchange(physics)
    return pl.pallas_call(
        finish_kernel,
        out_shape=jax.ShapeDtypeStruct((rows, cells, width), f32),
        in_specs=[SMEM, VMEM, VMEM],
        out_specs=ANY,
        scratch_shapes=[
            pltpu.VMEM((cells * kinds, levels), f32),
            pltpu.VMEM((rows, cells, width), f32),
            dma((rows,)),
        ],
        compiler_params=params(16),
        name="finish",
    )(back, returned, dyn)


def solution(mesh):
    lats, lons = mesh.devices.shape
    split = Mesh(mesh.devices.reshape(lats, 2, lons // 2), ("lat", "hi", "lo"))
    block = P("lat", LON_AXES, None)
    in_specs = (
        block,
        block,
        block,
        P("lat", LON_AXES),
        P("lat", LON_AXES),
        P(("lat", "hi", "lo"), None, None),
    )
    return jax.shard_map(shards, mesh=split, in_specs=in_specs, out_specs=block, check_vma=False)
```

```python
import functools

import jax
import jax.numpy as jnp
from jax import lax
from jax.experimental import pallas as pl
from jax.experimental.pallas import tpu as pltpu
from jax.sharding import Mesh
from jax.sharding import PartitionSpec as P

FLUX_COST = 10
TURN_COST = 30
INNER_COST = 1
SLOTS = 48
DIFFUSE = 0.1
GROUP_AXES = ("lat", "lo")
LON_AXES = ("hi", "lo")

VMEM = pl.BlockSpec(memory_space=pltpu.VMEM)
ANY = pl.BlockSpec(memory_space=pltpu.HBM)
SMEM = pl.BlockSpec(memory_space=pltpu.SMEM)


def log2(n):
    return n.bit_length() - 1


def parities(place, lons):
    return place & 1, (place >> log2(lons)) & 1


def edge_kernel(
    lons, place_ref, q_hbm, u_hbm, v_hbm, lon_a, lon_b, lat_a, lat_b, q_side, u_side, wide, ready, row, sems
):
    rows, cells, width = q_hbm.shape
    side = q_side.shape[2]
    odd_lon, odd_lat = parities(place_ref[0], lons)
    copies = []

    def copy(source, target):
        copies.append(pltpu.make_async_copy(source, target, sems.at[len(copies)]))
        copies[-1].start()

    for n, odd in enumerate((odd_lon, 1 - odd_lon)):
        near = pl.ds(pl.multiple_of(jnp.where(odd == 1, 0, cells - side), side), side)
        copy(q_hbm.at[:, near, :], q_side.at[n])
        copy(u_hbm.at[:, near, :], u_side.at[n])
    for n, odd in enumerate((odd_lat, 1 - odd_lat)):
        i = jnp.where(odd == 1, 0, rows - 1)
        copy(q_hbm.at[i], row.at[n, :, 0:width])
        copy(v_hbm.at[i], row.at[n, :, width:])
    for c in copies[4:]:
        c.wait()
    copy(row.at[0], lat_a)
    copy(row.at[1], lat_b)
    for c in copies[:4]:
        c.wait()
    for n, (ref, odd) in enumerate(((lon_a, odd_lon), (lon_b, 1 - odd_lon))):
        first = odd == 1
        for i in range(rows):
            q, u = q_side[n, i].astype(jnp.float32), u_side[n, i].astype(jnp.float32)
            wide[i : i + 1, 0:width] = jnp.where(first, q[0:1], q[side - 1 :])
            wide[i : i + 1, width:] = jnp.where(first, u[0:1], u[side - 1 :])
        ready[n] = wide[...].astype(jnp.bfloat16)
        copy(ready.at[n], ref)
    for c in copies[8:]:
        c.wait()


def plan(place_ref, span_ref, slot_ref, send_ref, pos_ref, member, pos, cap, owned, lons, lows):
    rows, cells = span_ref.shape
    stored = cap + 1
    peers = send_ref.shape[0] // stored
    f32, bf16 = jnp.float32, jnp.bfloat16
    span, slot = span_ref[...], slot_ref[...]
    owner = span >> log2(owned)
    owner_lon = owner & (lons - 1)
    far = (owner_lon >> log2(lows)) != ((place_ref[0] >> log2(lows)) & 1)
    low = (owner_lon & (lows - 1)) ^ jnp.where(far, lows // 2, 0)
    peer = ((owner >> log2(lons)) << log2(lows)) + low
    local = (span & (owned - 1)) + jnp.where(far, owned, 0)
    iota = lambda shape, axis: lax.broadcasted_iota(jnp.int32, shape, axis)
    for i in range(rows):
        member[i * peers : (i + 1) * peers, :] = jnp.where(
            iota((peers, cells), 0) == peer[i : i + 1], 1.0, 0.0
        )
    hot = member[...].astype(bf16)
    dot = functools.partial(jnp.dot, preferred_element_type=f32)
    within = dot(hot, (iota((cells, cells), 0) < iota((cells, cells), 1)).astype(f32).astype(bf16))
    pairs = (rows * peers, rows * peers)
    to, of = iota(pairs, 0), iota(pairs, 1)
    same = (to & (peers - 1)) == (of & (peers - 1))
    lower = jnp.where(same & (of < (to & -peers)), 1.0, 0.0).astype(bf16)
    before = within + jnp.sum(dot(lower, hot), axis=1, keepdims=True)
    before = before * member[...]
    lists = jnp.zeros((3 * peers, 128), f32)
    for i in range(rows):
        block = slice(i * peers, (i + 1) * peers)
        rank = jnp.sum(before[block], axis=0, keepdims=True).astype(jnp.int32)
        pos[i : i + 1, 0:cells] = peer[i : i + 1] * stored + rank
        pos_ref[i : i + 1, 0:cells] = peer[i : i + 1] * cap + rank
        chosen = jnp.where(iota((128, cells), 0) == rank, 1.0, 0.0).astype(bf16)
        mine = member[block]
        values = jnp.concatenate(
            [mine * local[i : i + 1].astype(f32), mine * slot[i : i + 1].astype(f32), mine], axis=0
        )
        lists = lists + lax.dot_general(
            values.astype(bf16), chosen, (((1,), (1,)), ((), ())), preferred_element_type=f32
        )
    spans = jnp.where(lists[2 * peers :] > 0.5, lists[:peers], 2.0 * owned)
    slots = lists[peers : 2 * peers]
    tile = send_ref.shape[1:]
    for p in range(peers):
        send_ref[p * stored + cap] = jnp.where(
            iota(tile, 0) == 0,
            jnp.broadcast_to(spans[p : p + 1], tile),
            jnp.broadcast_to(slots[p : p + 1], tile),
        ).astype(bf16)


def flux_kernel(
    cap,
    owned,
    lats,
    lons,
    lows,
    place_ref,
    *refs,
):
    sources, (send_hbm, back_hbm, dyn_hbm), rest = refs[:9], refs[9:12], refs[12:]
    held, rest = rest[:7], rest[7:]
    (
        sems,
        row_sems,
        member,
        back,
        pos,
        pos_s,
        send_ref,
        dyn_ref,
        cell,
        wind,
        face_x,
        wind_y,
        face_y,
        edge,
        flux_y,
    ) = rest
    span_ref, slot_ref, q_ref, u_ref, v_ref, lon_ref, lat_ref = held
    west_ref, east_ref = lon_ref.at[0], lon_ref.at[1]
    south_ref, north_ref = lat_ref.at[0], lat_ref.at[1]
    odd_lon, odd_lat = parities(place_ref[0], lons)
    targets = held[:5] + (
        lon_ref.at[1 - odd_lon],
        lon_ref.at[odd_lon],
        lat_ref.at[1 - odd_lat],
        lat_ref.at[odd_lat],
    )
    rows, cells, width = q_ref.shape
    levels = u_ref.shape[2]
    tracers = width // levels
    f32 = jnp.float32
    line = (cells + 2) * tracers
    copies = [pltpu.make_async_copy(a, b, sems.at[n]) for n, (a, b) in enumerate(zip(sources, targets))]
    for copy in copies:
        copy.start()

    def spread(block, first, count, stride):
        for t in range(tracers):
            cell[pl.ds(first + t, count, stride=stride), :] = block(t).astype(f32)

    lanes = lambda t: slice(t * levels, (t + 1) * levels)
    for copy in copies[:2]:
        copy.wait()
    plan(place_ref, span_ref, slot_ref, send_ref, back, member, pos, cap, owned, lons, lows)
    pos_copy = pltpu.make_async_copy(pos, pos_s, sems.at[len(copies)])
    pos_copy.start()
    back_copy = pltpu.make_async_copy(back, back_hbm, sems.at[len(copies) + 1])
    back_copy.start()
    copies[2].wait()

    def relayout(i, carry):
        spread(
            lambda t: q_ref[i, :, lanes(t)], (i + 1) * line + tracers, cells, tracers
        )
        return carry

    lax.fori_loop(0, rows, relayout, 0)
    for copy in copies[3:]:
        copy.wait()
    spread(lambda t: south_ref[:, lanes(t)], tracers, cells, tracers)
    spread(lambda t: north_ref[:, lanes(t)], (rows + 1) * line + tracers, cells, tracers)
    spread(lambda t: west_ref[:, lanes(t)], line, rows, line)
    spread(lambda t: east_ref[:, lanes(t)], line + (cells + 1) * tracers, rows, line)

    edge[0:rows, :] = west_ref[:, width:].astype(f32)
    edge[rows : 2 * rows, :] = east_ref[:, width:].astype(f32)
    stride = face_x.shape[0] // rows

    def faces(i, carry):
        wind[0:1, :] = edge[pl.ds(i, 1), :]
        wind[1 : cells + 1, :] = u_ref[i].astype(f32)
        wind[cells + 1 : cells + 2, :] = edge[pl.ds(rows + i, 1), :]
        face_x[pl.ds(pl.multiple_of(i * stride, 8), stride), :] = 0.25 * (
            wind[0:stride, :] + wind[1 : stride + 1, :]
        )
        return carry

    lax.fori_loop(0, rows, faces, 0)
    wind_y[0:cells, :] = south_ref[:, width:].astype(f32)
    wind_y[cells : (rows + 1) * cells, :] = v_ref[...].reshape(rows * cells, levels).astype(f32)
    wind_y[(rows + 1) * cells :, :] = north_ref[:, width:].astype(f32)
    face_y[...] = 0.25 * (wind_y[: (rows + 1) * cells, :] + wind_y[cells:, :])
    lat = place_ref[0] >> log2(lons)
    south_open = jnp.where(lat > 0, 1.0, 0.0)
    north_open = jnp.where(lat < lats - 1, 1.0, 0.0)
    face_y[0:cells, :] = face_y[0:cells, :] * south_open
    face_y[rows * cells :, :] = face_y[rows * cells :, :] * north_open

    def tile(i, j):
        first = (i * (cells + 2) + j) * tracers
        return cell[pl.ds(pl.multiple_of(first, tracers), tracers), :]

    def spread_row(ref, r):
        return jnp.broadcast_to(ref[pl.ds(r, 1), :], (tracers, levels))

    for j in range(cells):
        low, high = tile(0, j + 1), tile(1, j + 1)
        flux_y[j * tracers : (j + 1) * tracers, :] = spread_row(face_y, j) * (low + high) - (
            DIFFUSE * south_open
        ) * (high - low)

    pos_copy.wait()

    def dyn_copy(i):
        return pltpu.make_async_copy(dyn_ref.at[i], dyn_hbm.at[i], row_sems.at[i])

    def row(i, carry):
        diffuse_y = DIFFUSE * jnp.where(i == rows - 1, north_open, 1.0)
        here = tile(i + 1, 1)
        last = tile(i + 1, 0)
        flux_w = spread_row(face_x, i * stride) * (last + here) - DIFFUSE * (here - last)
        for j in range(cells):
            after = tile(i + 1, j + 2)
            flux_e = spread_row(face_x, i * stride + j + 1) * (here + after) - DIFFUSE * (
                after - here
            )
            above = tile(i + 2, j + 1)
            flux_n = spread_row(face_y, (i + 1) * cells + j) * (here + above) - diffuse_y * (
                above - here
            )
            flux_s = flux_y[j * tracers : (j + 1) * tracers, :]
            flux_y[j * tracers : (j + 1) * tracers, :] = flux_n
            dyn = (flux_w - flux_e) + (flux_s - flux_n)
            dyn_ref[i, j * tracers : (j + 1) * tracers, :] = dyn
            send_ref[pos_s[i, j]] = (here + dyn).astype(jnp.bfloat16)
            here, flux_w = after, flux_e
        dyn_copy(i).start()
        return carry

    lax.fori_loop(0, rows, row, 0)

    send_copy = pltpu.make_async_copy(send_ref, send_hbm, sems.at[len(copies) + 2])
    send_copy.start()
    back_copy.wait()

    def drain(i, carry):
        dyn_copy(i).wait()
        return carry

    lax.fori_loop(0, rows, drain, 0)
    send_copy.wait()


def turn_kernel(*refs):
    refs, out_ref = refs[:-1], refs[-1]
    for n, ref in enumerate(refs):
        for k in range(ref.shape[0]):
            out_ref[n * ref.shape[0] + k] = ref[k].T


def relax_kernel(lows, place_ref, x_ref, outer_ref, inner_ref, y_ref, pos, pos_s, sem, slots):
    tracers, levels = x_ref.shape[1:]
    peers, lanes = pos.shape
    stored = x_ref.shape[0] // peers
    cap = stored - 1
    f32 = jnp.float32
    for p in range(peers):
        listed = x_ref[p * stored + cap].astype(f32)
        pos[p : p + 1, :] = (listed[0:1] * SLOTS + listed[1:2]).astype(jnp.int32)
    copy = pltpu.make_async_copy(pos, pos_s, sem)
    copy.start()
    copy.wait()

    def tile(at):
        return pl.ds(pl.multiple_of(at * tracers, tracers), tracers)

    def scatter(p, carry):
        for r in range(cap):
            slots[tile(pos_s[p, r]), :] = x_ref[p * stored + r].astype(f32)
        return carry

    lax.fori_loop(0, peers, scatter, 0, unroll=16)
    block = SLOTS * tracers

    def relax(first, count, w_ref, w_first):
        def span(k, carry):
            at = pl.ds(pl.multiple_of((first + k) * block, block), block)
            x = slots[at, :]
            y = jnp.dot(x.astype(jnp.bfloat16), w_ref[w_first + k], preferred_element_type=f32)
            slots[at, :] = y - x
            return carry

        lax.fori_loop(0, count, span, 0, unroll=16)

    owned = inner_ref.shape[0]
    place = place_ref[0]
    is_outer = ((place >> log2(lows)) & 1) == ((place >> (log2(lows) - 1)) & 1)
    relax(0, owned, outer_ref, 0)

    @pl.when(is_outer)
    def _():
        relax(owned, owned, outer_ref, owned)

    @pl.when(jnp.logical_not(is_outer))
    def _():
        relax(owned, owned, inner_ref, 0)

    def gather(p, carry):
        for r in range(cap):
            y_ref[p * cap + r] = slots[tile(pos_s[p, r]), :].astype(jnp.bfloat16)
        return carry

    lax.fori_loop(0, peers, gather, 0, unroll=16)


def finish_kernel(pos_ref, y_ref, dyn_ref, out_hbm, total, out, sems):
    rows, cells, width = out.shape
    tracers, levels = y_ref.shape[1:]

    def copy(i):
        return pltpu.make_async_copy(out.at[i], out_hbm.at[i], sems.at[i])

    def row(i, carry):
        for j in range(cells):
            tile = slice(j * tracers, (j + 1) * tracers)
            total[tile, :] = dyn_ref[i, tile, :] + y_ref[pos_ref[i, j]].astype(jnp.float32)
        for t in range(tracers):
            out[i, :, t * levels : (t + 1) * levels] = total[pl.ds(t, cells, stride=tracers), :]
        copy(i).start()
        return carry

    lax.fori_loop(0, rows, row, 0)
    for i in range(rows):
        copy(i).wait()


def in_pairs(x, axis, first):
    count = lax.axis_size(axis)
    pairs = [(i % count, (i + 1) % count) for i in range(first, count + first, 2)]
    return lax.ppermute(x, axis, pairs + [(b, a) for a, b in pairs])


def shards(tracers, east_wind, north_wind, span_of, slot_of, inverses):
    levels = east_wind.shape[2]
    rows, cells, width = tracers.shape
    kinds = width // levels
    columns = rows * cells
    lats, lows = lax.axis_size("lat"), lax.axis_size("lo")
    lons = lax.axis_size("hi") * lows
    peers = lats * lows
    owned = inverses.shape[0]
    cap = 2 * (3 * columns // (2 * lats * lons))
    stored = cap + 1
    f32, bf16, i32 = jnp.float32, jnp.bfloat16, jnp.int32
    dma = pltpu.SemaphoreType.DMA
    params = lambda mib: pltpu.CompilerParams(vmem_limit_bytes=mib << 20)

    side = 8
    place = lax.axis_index(("lat", "hi", "lo")).astype(i32).reshape(1)
    lon_a, lon_b, lat_a, lat_b = pl.pallas_call(
        functools.partial(edge_kernel, lons),
        out_shape=(jax.ShapeDtypeStruct((rows, width + levels), bf16),) * 2
        + (jax.ShapeDtypeStruct((cells, width + levels), bf16),) * 2,
        in_specs=[SMEM] + [ANY] * 3,
        out_specs=(ANY,) * 4,
        scratch_shapes=[
            pltpu.VMEM((2, rows, side, width), bf16),
            pltpu.VMEM((2, rows, side, levels), bf16),
            pltpu.VMEM((rows, width + levels), f32),
            pltpu.VMEM((2, rows, width + levels), bf16),
            pltpu.VMEM((2, cells, width + levels), bf16),
            dma((12,)),
        ],
        compiler_params=params(64),
        name="edges",
    )(place, tracers, east_wind, north_wind)
    far_edges = (
        in_pairs(lon_a, LON_AXES, 0),
        in_pairs(lon_b, LON_AXES, 1),
        in_pairs(lat_a, "lat", 0),
        in_pairs(lat_b, "lat", 1),
    )

    def opposite(start, stop):
        pairs = [(lo, lows + (lo ^ lows // 2)) for lo in range(start, stop)]
        return pairs + [(b, a) for a, b in pairs]

    outer = lax.ppermute(inverses, LON_AXES, opposite(0, lows // 2))
    cost = lambda us: pl.CostEstimate(
        flops=us * 1_000_000_000, bytes_accessed=1 << 20, transcendentals=0
    )
    fields = (span_of, slot_of, tracers, east_wind, north_wind, *far_edges)
    held = [(x.shape, x.dtype) for x in fields[:5]]
    held += [((2,) + x.shape, x.dtype) for x in (lon_a, lat_a)]
    stride = (cells + 1 + 7) // 8 * 8
    dyn_shape = (rows, cells * kinds, levels)
    send_shape = (peers * stored, kinds, levels)
    send, back, dyn = pl.pallas_call(
        functools.partial(flux_kernel, cap, owned, lats, lons, lows),
        out_shape=(
            jax.ShapeDtypeStruct(send_shape, bf16),
            jax.ShapeDtypeStruct((rows, 128), i32),
            jax.ShapeDtypeStruct(dyn_shape, f32),
        ),
        in_specs=[SMEM] + [ANY] * 9,
        out_specs=(ANY,) * 3,
        scratch_shapes=[pltpu.VMEM(*x) for x in held]
        + [
            dma((12,)),
            dma((rows,)),
            pltpu.VMEM((rows * peers, cells), f32),
            pltpu.VMEM((rows, 128), i32),
            pltpu.VMEM((rows, 128), i32),
            pltpu.SMEM((rows, 128), i32),
            pltpu.VMEM(send_shape, bf16),
            pltpu.VMEM(dyn_shape, f32),
            pltpu.VMEM(((rows + 2) * (cells + 2) * kinds, levels), f32),
            pltpu.VMEM((stride + 8, levels), f32),
            pltpu.VMEM((rows * stride, levels), f32),
            pltpu.VMEM(((rows + 2) * cells, levels), f32),
            pltpu.VMEM(((rows + 1) * cells, levels), f32),
            pltpu.VMEM((2 * rows, levels), f32),
            pltpu.VMEM((cells * kinds, levels), f32),
        ],
        compiler_params=params(64),
        cost_estimate=cost(FLUX_COST),
        name="flux",
    )(place, *fields)

    matrices, send = lax.optimization_barrier((inverses, send))
    inner = lax.ppermute(matrices, LON_AXES, opposite(lows // 2, lows))

    def exchange(x):
        x = x.reshape(peers, -1, kinds, levels)
        x = lax.all_to_all(x, GROUP_AXES, split_axis=0, concat_axis=0, tiled=True)
        return x.reshape(-1, kinds, levels)

    arrived = exchange(send)
    def turned(us, *arrays):
        return pl.pallas_call(
            turn_kernel,
            out_shape=jax.ShapeDtypeStruct((len(arrays) * owned, levels, levels), bf16),
            in_specs=[VMEM] * len(arrays),
            out_specs=VMEM,
            compiler_params=params(16),
            cost_estimate=cost(us),
            name="turn",
        )(*arrays)

    physics = pl.pallas_call(
        functools.partial(relax_kernel, lows),
        out_shape=jax.ShapeDtypeStruct((peers * cap, kinds, levels), bf16),
        in_specs=[SMEM] + [VMEM] * 3,
        out_specs=VMEM,
        scratch_shapes=[
            pltpu.VMEM((peers, 128), i32),
            pltpu.SMEM((peers, 128), i32),
            dma,
            pltpu.VMEM(((2 * owned * SLOTS + 1) * kinds, levels), f32),
        ],
        compiler_params=params(24),
        name="relax",
    )(place, arrived, turned(TURN_COST, inverses, outer), turned(INNER_COST, inner))

    returned = exchange(physics)
    return pl.pallas_call(
        finish_kernel,
        out_shape=jax.ShapeDtypeStruct((rows, cells, width), f32),
        in_specs=[SMEM, VMEM, VMEM],
        out_specs=ANY,
        scratch_shapes=[
            pltpu.VMEM((cells * kinds, levels), f32),
            pltpu.VMEM((rows, cells, width), f32),
            dma((rows,)),
        ],
        compiler_params=params(16),
        name="finish",
    )(back, returned, dyn)


def solution(mesh):
    lats, lons = mesh.devices.shape
    split = Mesh(mesh.devices.reshape(lats, 2, lons // 2), ("lat", "hi", "lo"))
    block = P("lat", LON_AXES, None)
    in_specs = (
        block,
        block,
        block,
        P("lat", LON_AXES),
        P("lat", LON_AXES),
        P(("lat", "hi", "lo"), None, None),
    )
    return jax.shard_map(shards, mesh=split, in_specs=in_specs, out_specs=block, check_vma=False)
```

```python
import functools

import jax
import jax.numpy as jnp
from jax import lax
from jax.experimental import pallas as pl
from jax.experimental.pallas import tpu as pltpu
from jax.sharding import Mesh
from jax.sharding import PartitionSpec as P

FLUX_COST = 10
TURN_COST = 30
INNER_COST = 1
SLOTS = 48
DIFFUSE = 0.1
GROUP_AXES = ("lat", "lo")
LON_AXES = ("hi", "lo")

VMEM = pl.BlockSpec(memory_space=pltpu.VMEM)
ANY = pl.BlockSpec(memory_space=pltpu.HBM)
SMEM = pl.BlockSpec(memory_space=pltpu.SMEM)


def log2(n):
    return n.bit_length() - 1


def parities(place, lons):
    return place & 1, (place >> log2(lons)) & 1


def edge_kernel(
    lons, place_ref, q_hbm, u_hbm, v_hbm, lon_a, lon_b, lat_a, lat_b, q_side, u_side, wide, ready, row, sems
):
    rows, cells, width = q_hbm.shape
    side = q_side.shape[2]
    odd_lon, odd_lat = parities(place_ref[0], lons)
    copies = []

    def copy(source, target):
        copies.append(pltpu.make_async_copy(source, target, sems.at[len(copies)]))
        copies[-1].start()

    for n, odd in enumerate((odd_lon, 1 - odd_lon)):
        near = pl.ds(pl.multiple_of(jnp.where(odd == 1, 0, cells - side), side), side)
        copy(q_hbm.at[:, near, :], q_side.at[n])
        copy(u_hbm.at[:, near, :], u_side.at[n])
    for n, odd in enumerate((odd_lat, 1 - odd_lat)):
        i = jnp.where(odd == 1, 0, rows - 1)
        copy(q_hbm.at[i], row.at[n, :, 0:width])
        copy(v_hbm.at[i], row.at[n, :, width:])
    for c in copies[4:]:
        c.wait()
    copy(row.at[0], lat_a)
    copy(row.at[1], lat_b)
    for c in copies[:4]:
        c.wait()
    for n, (ref, odd) in enumerate(((lon_a, odd_lon), (lon_b, 1 - odd_lon))):
        first = odd == 1
        for i in range(rows):
            q, u = q_side[n, i].astype(jnp.float32), u_side[n, i].astype(jnp.float32)
            wide[i : i + 1, 0:width] = jnp.where(first, q[0:1], q[side - 1 :])
            wide[i : i + 1, width:] = jnp.where(first, u[0:1], u[side - 1 :])
        ready[n] = wide[...].astype(jnp.bfloat16)
        copy(ready.at[n], ref)
    for c in copies[8:]:
        c.wait()


def plan(place_ref, span_ref, slot_ref, send_ref, pos_ref, member, pos, cap, owned, lons, lows):
    rows, cells = span_ref.shape
    stored = cap + 1
    peers = send_ref.shape[0] // stored
    f32, bf16 = jnp.float32, jnp.bfloat16
    span, slot = span_ref[...], slot_ref[...]
    owner = span >> log2(owned)
    owner_lon = owner & (lons - 1)
    far = (owner_lon >> log2(lows)) != ((place_ref[0] >> log2(lows)) & 1)
    low = (owner_lon & (lows - 1)) ^ jnp.where(far, lows // 2, 0)
    peer = ((owner >> log2(lons)) << log2(lows)) + low
    local = (span & (owned - 1)) + jnp.where(far, owned, 0)
    iota = lambda shape, axis: lax.broadcasted_iota(jnp.int32, shape, axis)
    for i in range(rows):
        member[i * peers : (i + 1) * peers, :] = jnp.where(
            iota((peers, cells), 0) == peer[i : i + 1], 1.0, 0.0
        )
    hot = member[...].astype(bf16)
    dot = functools.partial(jnp.dot, preferred_element_type=f32)
    within = dot(hot, (iota((cells, cells), 0) < iota((cells, cells), 1)).astype(f32).astype(bf16))
    pairs = (rows * peers, rows * peers)
    to, of = iota(pairs, 0), iota(pairs, 1)
    same = (to & (peers - 1)) == (of & (peers - 1))
    lower = jnp.where(same & (of < (to & -peers)), 1.0, 0.0).astype(bf16)
    before = within + jnp.sum(dot(lower, hot), axis=1, keepdims=True)
    before = before * member[...]
    lists = jnp.zeros((3 * peers, 128), f32)
    for i in range(rows):
        block = slice(i * peers, (i + 1) * peers)
        rank = jnp.sum(before[block], axis=0, keepdims=True).astype(jnp.int32)
        pos[i : i + 1, 0:cells] = peer[i : i + 1] * stored + rank
        pos_ref[i : i + 1, 0:cells] = peer[i : i + 1] * cap + rank
        chosen = jnp.where(iota((128, cells), 0) == rank, 1.0, 0.0).astype(bf16)
        mine = member[block]
        values = jnp.concatenate(
            [mine * local[i : i + 1].astype(f32), mine * slot[i : i + 1].astype(f32), mine], axis=0
        )
        lists = lists + lax.dot_general(
            values.astype(bf16), chosen, (((1,), (1,)), ((), ())), preferred_element_type=f32
        )
    spans = jnp.where(lists[2 * peers :] > 0.5, lists[:peers], 2.0 * owned)
    slots = lists[peers : 2 * peers]
    tile = send_ref.shape[1:]
    for p in range(peers):
        send_ref[p * stored + cap] = jnp.where(
            iota(tile, 0) == 0,
            jnp.broadcast_to(spans[p : p + 1], tile),
            jnp.broadcast_to(slots[p : p + 1], tile),
        ).astype(bf16)


def flux_kernel(
    cap,
    owned,
    lats,
    lons,
    lows,
    place_ref,
    *refs,
):
    sources, (send_hbm, back_hbm, dyn_hbm), rest = refs[:9], refs[9:12], refs[12:]
    held, rest = rest[:7], rest[7:]
    (
        sems,
        row_sems,
        member,
        back,
        pos,
        pos_s,
        send_ref,
        dyn_ref,
        cell,
        wind,
        face_x,
        wind_y,
        face_y,
        edge,
        flux_y,
    ) = rest
    span_ref, slot_ref, q_ref, u_ref, v_ref, lon_ref, lat_ref = held
    west_ref, east_ref = lon_ref.at[0], lon_ref.at[1]
    south_ref, north_ref = lat_ref.at[0], lat_ref.at[1]
    odd_lon, odd_lat = parities(place_ref[0], lons)
    targets = held[:5] + (
        lon_ref.at[1 - odd_lon],
        lon_ref.at[odd_lon],
        lat_ref.at[1 - odd_lat],
        lat_ref.at[odd_lat],
    )
    rows, cells, width = q_ref.shape
    levels = u_ref.shape[2]
    tracers = width // levels
    f32 = jnp.float32
    line = (cells + 2) * tracers
    copies = [pltpu.make_async_copy(a, b, sems.at[n]) for n, (a, b) in enumerate(zip(sources, targets))]
    for copy in copies:
        copy.start()

    def spread(block, first, count, stride):
        for t in range(tracers):
            cell[pl.ds(first + t, count, stride=stride), :] = block(t).astype(f32)

    lanes = lambda t: slice(t * levels, (t + 1) * levels)
    for copy in copies[:2]:
        copy.wait()
    plan(place_ref, span_ref, slot_ref, send_ref, back, member, pos, cap, owned, lons, lows)
    pos_copy = pltpu.make_async_copy(pos, pos_s, sems.at[len(copies)])
    pos_copy.start()
    back_copy = pltpu.make_async_copy(back, back_hbm, sems.at[len(copies) + 1])
    back_copy.start()
    copies[2].wait()

    def relayout(i, carry):
        spread(
            lambda t: q_ref[i, :, lanes(t)], (i + 1) * line + tracers, cells, tracers
        )
        return carry

    lax.fori_loop(0, rows, relayout, 0, unroll=4)
    for copy in copies[3:]:
        copy.wait()
    spread(lambda t: south_ref[:, lanes(t)], tracers, cells, tracers)
    spread(lambda t: north_ref[:, lanes(t)], (rows + 1) * line + tracers, cells, tracers)
    spread(lambda t: west_ref[:, lanes(t)], line, rows, line)
    spread(lambda t: east_ref[:, lanes(t)], line + (cells + 1) * tracers, rows, line)

    edge[0:rows, :] = west_ref[:, width:].astype(f32)
    edge[rows : 2 * rows, :] = east_ref[:, width:].astype(f32)
    stride = face_x.shape[0] // rows

    def faces(i, carry):
        wind[0:1, :] = edge[pl.ds(i, 1), :]
        wind[1 : cells + 1, :] = u_ref[i].astype(f32)
        wind[cells + 1 : cells + 2, :] = edge[pl.ds(rows + i, 1), :]
        face_x[pl.ds(pl.multiple_of(i * stride, 8), stride), :] = 0.25 * (
            wind[0:stride, :] + wind[1 : stride + 1, :]
        )
        return carry

    lax.fori_loop(0, rows, faces, 0, unroll=4)
    wind_y[0:cells, :] = south_ref[:, width:].astype(f32)
    wind_y[cells : (rows + 1) * cells, :] = v_ref[...].reshape(rows * cells, levels).astype(f32)
    wind_y[(rows + 1) * cells :, :] = north_ref[:, width:].astype(f32)
    face_y[...] = 0.25 * (wind_y[: (rows + 1) * cells, :] + wind_y[cells:, :])
    lat = place_ref[0] >> log2(lons)
    south_open = jnp.where(lat > 0, 1.0, 0.0)
    north_open = jnp.where(lat < lats - 1, 1.0, 0.0)
    face_y[0:cells, :] = face_y[0:cells, :] * south_open
    face_y[rows * cells :, :] = face_y[rows * cells :, :] * north_open

    def tile(i, j):
        first = (i * (cells + 2) + j) * tracers
        return cell[pl.ds(pl.multiple_of(first, tracers), tracers), :]

    def spread_row(ref, r):
        return jnp.broadcast_to(ref[pl.ds(r, 1), :], (tracers, levels))

    for j in range(cells):
        low, high = tile(0, j + 1), tile(1, j + 1)
        flux_y[j * tracers : (j + 1) * tracers, :] = spread_row(face_y, j) * (low + high) - (
            DIFFUSE * south_open
        ) * (high - low)

    pos_copy.wait()

    def dyn_copy(i):
        return pltpu.make_async_copy(dyn_ref.at[i], dyn_hbm.at[i], row_sems.at[i])

    def row(i, carry):
        diffuse_y = DIFFUSE * jnp.where(i == rows - 1, north_open, 1.0)
        here = tile(i + 1, 1)
        last = tile(i + 1, 0)
        flux_w = spread_row(face_x, i * stride) * (last + here) - DIFFUSE * (here - last)
        for j in range(cells):
            after = tile(i + 1, j + 2)
            flux_e = spread_row(face_x, i * stride + j + 1) * (here + after) - DIFFUSE * (
                after - here
            )
            above = tile(i + 2, j + 1)
            flux_n = spread_row(face_y, (i + 1) * cells + j) * (here + above) - diffuse_y * (
                above - here
            )
            flux_s = flux_y[j * tracers : (j + 1) * tracers, :]
            flux_y[j * tracers : (j + 1) * tracers, :] = flux_n
            dyn = (flux_w - flux_e) + (flux_s - flux_n)
            dyn_ref[i, j * tracers : (j + 1) * tracers, :] = dyn
            send_ref[pos_s[i, j]] = (here + dyn).astype(jnp.bfloat16)
            here, flux_w = after, flux_e
        dyn_copy(i).start()
        return carry

    lax.fori_loop(0, rows, row, 0, unroll=2)

    send_copy = pltpu.make_async_copy(send_ref, send_hbm, sems.at[len(copies) + 2])
    send_copy.start()
    back_copy.wait()

    def drain(i, carry):
        dyn_copy(i).wait()
        return carry

    lax.fori_loop(0, rows, drain, 0)
    send_copy.wait()


def turn_kernel(*refs):
    refs, out_ref = refs[:-1], refs[-1]
    for n, ref in enumerate(refs):
        for k in range(ref.shape[0]):
            out_ref[n * ref.shape[0] + k] = ref[k].T


def relax_kernel(lows, place_ref, x_ref, outer_ref, inner_ref, y_ref, pos, pos_s, sem, slots):
    tracers, levels = x_ref.shape[1:]
    peers, lanes = pos.shape
    stored = x_ref.shape[0] // peers
    cap = stored - 1
    f32 = jnp.float32
    for p in range(peers):
        listed = x_ref[p * stored + cap].astype(f32)
        pos[p : p + 1, :] = (listed[0:1] * SLOTS + listed[1:2]).astype(jnp.int32)
    copy = pltpu.make_async_copy(pos, pos_s, sem)
    copy.start()
    copy.wait()

    def tile(at):
        return pl.ds(pl.multiple_of(at * tracers, tracers), tracers)

    def scatter(p, carry):
        for r in range(cap):
            slots[tile(pos_s[p, r]), :] = x_ref[p * stored + r].astype(f32)
        return carry

    lax.fori_loop(0, peers, scatter, 0, unroll=16)
    block = SLOTS * tracers

    def relax(first, count, w_ref, w_first):
        def span(k, carry):
            at = pl.ds(pl.multiple_of((first + k) * block, block), block)
            x = slots[at, :]
            y = jnp.dot(x.astype(jnp.bfloat16), w_ref[w_first + k], preferred_element_type=f32)
            slots[at, :] = y - x
            return carry

        lax.fori_loop(0, count, span, 0, unroll=16)

    owned = inner_ref.shape[0]
    place = place_ref[0]
    is_outer = ((place >> log2(lows)) & 1) == ((place >> (log2(lows) - 1)) & 1)
    relax(0, owned, outer_ref, 0)

    @pl.when(is_outer)
    def _():
        relax(owned, owned, outer_ref, owned)

    @pl.when(jnp.logical_not(is_outer))
    def _():
        relax(owned, owned, inner_ref, 0)

    def gather(p, carry):
        for r in range(cap):
            y_ref[p * cap + r] = slots[tile(pos_s[p, r]), :].astype(jnp.bfloat16)
        return carry

    lax.fori_loop(0, peers, gather, 0, unroll=16)


def finish_kernel(pos_ref, y_ref, dyn_ref, out_hbm, total, out, sems):
    rows, cells, width = out.shape
    tracers, levels = y_ref.shape[1:]

    def copy(i):
        return pltpu.make_async_copy(out.at[i], out_hbm.at[i], sems.at[i])

    def row(i, carry):
        for j in range(cells):
            tile = slice(j * tracers, (j + 1) * tracers)
            total[tile, :] = dyn_ref[i, tile, :] + y_ref[pos_ref[i, j]].astype(jnp.float32)
        for t in range(tracers):
            out[i, :, t * levels : (t + 1) * levels] = total[pl.ds(t, cells, stride=tracers), :]
        copy(i).start()
        return carry

    lax.fori_loop(0, rows, row, 0)
    for i in range(rows):
        copy(i).wait()


def in_pairs(x, axis, first):
    count = lax.axis_size(axis)
    pairs = [(i % count, (i + 1) % count) for i in range(first, count + first, 2)]
    return lax.ppermute(x, axis, pairs + [(b, a) for a, b in pairs])


def shards(tracers, east_wind, north_wind, span_of, slot_of, inverses):
    levels = east_wind.shape[2]
    rows, cells, width = tracers.shape
    kinds = width // levels
    columns = rows * cells
    lats, lows = lax.axis_size("lat"), lax.axis_size("lo")
    lons = lax.axis_size("hi") * lows
    peers = lats * lows
    owned = inverses.shape[0]
    cap = 2 * (3 * columns // (2 * lats * lons))
    stored = cap + 1
    f32, bf16, i32 = jnp.float32, jnp.bfloat16, jnp.int32
    dma = pltpu.SemaphoreType.DMA
    params = lambda mib: pltpu.CompilerParams(vmem_limit_bytes=mib << 20)

    side = 8
    place = lax.axis_index(("lat", "hi", "lo")).astype(i32).reshape(1)
    lon_a, lon_b, lat_a, lat_b = pl.pallas_call(
        functools.partial(edge_kernel, lons),
        out_shape=(jax.ShapeDtypeStruct((rows, width + levels), bf16),) * 2
        + (jax.ShapeDtypeStruct((cells, width + levels), bf16),) * 2,
        in_specs=[SMEM] + [ANY] * 3,
        out_specs=(ANY,) * 4,
        scratch_shapes=[
            pltpu.VMEM((2, rows, side, width), bf16),
            pltpu.VMEM((2, rows, side, levels), bf16),
            pltpu.VMEM((rows, width + levels), f32),
            pltpu.VMEM((2, rows, width + levels), bf16),
            pltpu.VMEM((2, cells, width + levels), bf16),
            dma((12,)),
        ],
        compiler_params=params(64),
        name="edges",
    )(place, tracers, east_wind, north_wind)
    far_edges = (
        in_pairs(lon_a, LON_AXES, 0),
        in_pairs(lon_b, LON_AXES, 1),
        in_pairs(lat_a, "lat", 0),
        in_pairs(lat_b, "lat", 1),
    )

    def opposite(start, stop):
        pairs = [(lo, lows + (lo ^ lows // 2)) for lo in range(start, stop)]
        return pairs + [(b, a) for a, b in pairs]

    outer = lax.ppermute(inverses, LON_AXES, opposite(0, lows // 2))
    cost = lambda us: pl.CostEstimate(
        flops=us * 1_000_000_000, bytes_accessed=1 << 20, transcendentals=0
    )
    fields = (span_of, slot_of, tracers, east_wind, north_wind, *far_edges)
    held = [(x.shape, x.dtype) for x in fields[:5]]
    held += [((2,) + x.shape, x.dtype) for x in (lon_a, lat_a)]
    stride = (cells + 1 + 7) // 8 * 8
    dyn_shape = (rows, cells * kinds, levels)
    send_shape = (peers * stored, kinds, levels)
    send, back, dyn = pl.pallas_call(
        functools.partial(flux_kernel, cap, owned, lats, lons, lows),
        out_shape=(
            jax.ShapeDtypeStruct(send_shape, bf16),
            jax.ShapeDtypeStruct((rows, 128), i32),
            jax.ShapeDtypeStruct(dyn_shape, f32),
        ),
        in_specs=[SMEM] + [ANY] * 9,
        out_specs=(ANY,) * 3,
        scratch_shapes=[pltpu.VMEM(*x) for x in held]
        + [
            dma((12,)),
            dma((rows,)),
            pltpu.VMEM((rows * peers, cells), f32),
            pltpu.VMEM((rows, 128), i32),
            pltpu.VMEM((rows, 128), i32),
            pltpu.SMEM((rows, 128), i32),
            pltpu.VMEM(send_shape, bf16),
            pltpu.VMEM(dyn_shape, f32),
            pltpu.VMEM(((rows + 2) * (cells + 2) * kinds, levels), f32),
            pltpu.VMEM((stride + 8, levels), f32),
            pltpu.VMEM((rows * stride, levels), f32),
            pltpu.VMEM(((rows + 2) * cells, levels), f32),
            pltpu.VMEM(((rows + 1) * cells, levels), f32),
            pltpu.VMEM((2 * rows, levels), f32),
            pltpu.VMEM((cells * kinds, levels), f32),
        ],
        compiler_params=params(64),
        cost_estimate=cost(FLUX_COST),
        name="flux",
    )(place, *fields)

    matrices, send = lax.optimization_barrier((inverses, send))
    inner = lax.ppermute(matrices, LON_AXES, opposite(lows // 2, lows))

    def exchange(x):
        x = x.reshape(peers, -1, kinds, levels)
        x = lax.all_to_all(x, GROUP_AXES, split_axis=0, concat_axis=0, tiled=True)
        return x.reshape(-1, kinds, levels)

    arrived = exchange(send)
    def turned(us, *arrays):
        return pl.pallas_call(
            turn_kernel,
            out_shape=jax.ShapeDtypeStruct((len(arrays) * owned, levels, levels), bf16),
            in_specs=[VMEM] * len(arrays),
            out_specs=VMEM,
            compiler_params=params(16),
            cost_estimate=cost(us),
            name="turn",
        )(*arrays)

    physics = pl.pallas_call(
        functools.partial(relax_kernel, lows),
        out_shape=jax.ShapeDtypeStruct((peers * cap, kinds, levels), bf16),
        in_specs=[SMEM] + [VMEM] * 3,
        out_specs=VMEM,
        scratch_shapes=[
            pltpu.VMEM((peers, 128), i32),
            pltpu.SMEM((peers, 128), i32),
            dma,
            pltpu.VMEM(((2 * owned * SLOTS + 1) * kinds, levels), f32),
        ],
        compiler_params=params(24),
        name="relax",
    )(place, arrived, turned(TURN_COST, inverses, outer), turned(INNER_COST, inner))

    returned = exchange(physics)
    return pl.pallas_call(
        finish_kernel,
        out_shape=jax.ShapeDtypeStruct((rows, cells, width), f32),
        in_specs=[SMEM, VMEM, VMEM],
        out_specs=ANY,
        scratch_shapes=[
            pltpu.VMEM((cells * kinds, levels), f32),
            pltpu.VMEM((rows, cells, width), f32),
            dma((rows,)),
        ],
        compiler_params=params(16),
        name="finish",
    )(back, returned, dyn)


def solution(mesh):
    lats, lons = mesh.devices.shape
    split = Mesh(mesh.devices.reshape(lats, 2, lons // 2), ("lat", "hi", "lo"))
    block = P("lat", LON_AXES, None)
    in_specs = (
        block,
        block,
        block,
        P("lat", LON_AXES),
        P("lat", LON_AXES),
        P(("lat", "hi", "lo"), None, None),
    )
    return jax.shard_map(shards, mesh=split, in_specs=in_specs, out_specs=block, check_vma=False)
```

```python
import functools

import jax
import jax.numpy as jnp
from jax import lax
from jax.experimental import pallas as pl
from jax.experimental.pallas import tpu as pltpu
from jax.sharding import Mesh
from jax.sharding import PartitionSpec as P

FLUX_COST = 10
TURN_COST = 30
INNER_COST = 1
SLOTS = 48
DIFFUSE = 0.1
GROUP_AXES = ("lat", "lo")
LON_AXES = ("hi", "lo")

VMEM = pl.BlockSpec(memory_space=pltpu.VMEM)
ANY = pl.BlockSpec(memory_space=pltpu.HBM)
SMEM = pl.BlockSpec(memory_space=pltpu.SMEM)


def log2(n):
    return n.bit_length() - 1


def parities(place, lons):
    return place & 1, (place >> log2(lons)) & 1


def edge_kernel(
    lons, place_ref, q_hbm, u_hbm, v_hbm, lon_a, lon_b, lat_a, lat_b, q_side, u_side, wide, ready, row, sems
):
    rows, cells, width = q_hbm.shape
    side = q_side.shape[2]
    odd_lon, odd_lat = parities(place_ref[0], lons)
    copies = []

    def copy(source, target):
        copies.append(pltpu.make_async_copy(source, target, sems.at[len(copies)]))
        copies[-1].start()

    for n, odd in enumerate((odd_lon, 1 - odd_lon)):
        near = pl.ds(pl.multiple_of(jnp.where(odd == 1, 0, cells - side), side), side)
        copy(q_hbm.at[:, near, :], q_side.at[n])
        copy(u_hbm.at[:, near, :], u_side.at[n])
    for n, odd in enumerate((odd_lat, 1 - odd_lat)):
        i = jnp.where(odd == 1, 0, rows - 1)
        copy(q_hbm.at[i], row.at[n, :, 0:width])
        copy(v_hbm.at[i], row.at[n, :, width:])
    for c in copies[4:]:
        c.wait()
    copy(row.at[0], lat_a)
    copy(row.at[1], lat_b)
    for c in copies[:4]:
        c.wait()
    for n, (ref, odd) in enumerate(((lon_a, odd_lon), (lon_b, 1 - odd_lon))):
        first = odd == 1
        for i in range(rows):
            q, u = q_side[n, i].astype(jnp.float32), u_side[n, i].astype(jnp.float32)
            wide[i : i + 1, 0:width] = jnp.where(first, q[0:1], q[side - 1 :])
            wide[i : i + 1, width:] = jnp.where(first, u[0:1], u[side - 1 :])
        ready[n] = wide[...].astype(jnp.bfloat16)
        copy(ready.at[n], ref)
    for c in copies[8:]:
        c.wait()


def plan(place_ref, span_ref, slot_ref, send_ref, pos_ref, member, pos, cap, owned, lons, lows):
    rows, cells = span_ref.shape
    stored = cap + 1
    peers = send_ref.shape[0] // stored
    f32, bf16 = jnp.float32, jnp.bfloat16
    span, slot = span_ref[...], slot_ref[...]
    owner = span >> log2(owned)
    owner_lon = owner & (lons - 1)
    far = (owner_lon >> log2(lows)) != ((place_ref[0] >> log2(lows)) & 1)
    low = (owner_lon & (lows - 1)) ^ jnp.where(far, lows // 2, 0)
    peer = ((owner >> log2(lons)) << log2(lows)) + low
    local = (span & (owned - 1)) + jnp.where(far, owned, 0)
    iota = lambda shape, axis: lax.broadcasted_iota(jnp.int32, shape, axis)
    for i in range(rows):
        member[i * peers : (i + 1) * peers, :] = jnp.where(
            iota((peers, cells), 0) == peer[i : i + 1], 1.0, 0.0
        )
    hot = member[...].astype(bf16)
    dot = functools.partial(jnp.dot, preferred_element_type=f32)
    within = dot(hot, (iota((cells, cells), 0) < iota((cells, cells), 1)).astype(f32).astype(bf16))
    pairs = (rows * peers, rows * peers)
    to, of = iota(pairs, 0), iota(pairs, 1)
    same = (to & (peers - 1)) == (of & (peers - 1))
    lower = jnp.where(same & (of < (to & -peers)), 1.0, 0.0).astype(bf16)
    before = within + jnp.sum(dot(lower, hot), axis=1, keepdims=True)
    before = before * member[...]
    lists = jnp.zeros((3 * peers, 128), f32)
    for i in range(rows):
        block = slice(i * peers, (i + 1) * peers)
        rank = jnp.sum(before[block], axis=0, keepdims=True).astype(jnp.int32)
        pos[i : i + 1, 0:cells] = peer[i : i + 1] * stored + rank
        pos_ref[i : i + 1, 0:cells] = peer[i : i + 1] * cap + rank
        chosen = jnp.where(iota((128, cells), 0) == rank, 1.0, 0.0).astype(bf16)
        mine = member[block]
        values = jnp.concatenate(
            [mine * local[i : i + 1].astype(f32), mine * slot[i : i + 1].astype(f32), mine], axis=0
        )
        lists = lists + lax.dot_general(
            values.astype(bf16), chosen, (((1,), (1,)), ((), ())), preferred_element_type=f32
        )
    spans = jnp.where(lists[2 * peers :] > 0.5, lists[:peers], 2.0 * owned)
    slots = lists[peers : 2 * peers]
    tile = send_ref.shape[1:]
    for p in range(peers):
        send_ref[p * stored + cap] = jnp.where(
            iota(tile, 0) == 0,
            jnp.broadcast_to(spans[p : p + 1], tile),
            jnp.broadcast_to(slots[p : p + 1], tile),
        ).astype(bf16)


def flux_kernel(
    cap,
    owned,
    lats,
    lons,
    lows,
    place_ref,
    *refs,
):
    sources, (send_hbm, back_hbm, dyn_hbm), rest = refs[:9], refs[9:12], refs[12:]
    held, rest = rest[:7], rest[7:]
    (
        sems,
        row_sems,
        member,
        back,
        pos,
        pos_s,
        send_ref,
        dyn_ref,
        cell,
        wind,
        face_x,
        wind_y,
        face_y,
        edge,
        flux_y,
    ) = rest
    span_ref, slot_ref, q_ref, u_ref, v_ref, lon_ref, lat_ref = held
    west_ref, east_ref = lon_ref.at[0], lon_ref.at[1]
    south_ref, north_ref = lat_ref.at[0], lat_ref.at[1]
    odd_lon, odd_lat = parities(place_ref[0], lons)
    targets = held[:5] + (
        lon_ref.at[1 - odd_lon],
        lon_ref.at[odd_lon],
        lat_ref.at[1 - odd_lat],
        lat_ref.at[odd_lat],
    )
    rows, cells, width = q_ref.shape
    levels = u_ref.shape[2]
    tracers = width // levels
    f32 = jnp.float32
    line = (cells + 2) * tracers
    copies = [pltpu.make_async_copy(a, b, sems.at[n]) for n, (a, b) in enumerate(zip(sources, targets))]
    for copy in copies:
        copy.start()

    def spread(block, first, count, stride):
        for t in range(tracers):
            cell[pl.ds(first + t, count, stride=stride), :] = block(t).astype(f32)

    lanes = lambda t: slice(t * levels, (t + 1) * levels)
    for copy in copies[:2]:
        copy.wait()
    plan(place_ref, span_ref, slot_ref, send_ref, back, member, pos, cap, owned, lons, lows)
    pos_copy = pltpu.make_async_copy(pos, pos_s, sems.at[len(copies)])
    pos_copy.start()
    back_copy = pltpu.make_async_copy(back, back_hbm, sems.at[len(copies) + 1])
    back_copy.start()
    copies[2].wait()

    def relayout(i, carry):
        spread(
            lambda t: q_ref[i, :, lanes(t)], (i + 1) * line + tracers, cells, tracers
        )
        return carry

    lax.fori_loop(0, rows, relayout, 0, unroll=4)
    for copy in copies[3:]:
        copy.wait()
    spread(lambda t: south_ref[:, lanes(t)], tracers, cells, tracers)
    spread(lambda t: north_ref[:, lanes(t)], (rows + 1) * line + tracers, cells, tracers)
    spread(lambda t: west_ref[:, lanes(t)], line, rows, line)
    spread(lambda t: east_ref[:, lanes(t)], line + (cells + 1) * tracers, rows, line)

    edge[0:rows, :] = west_ref[:, width:].astype(f32)
    edge[rows : 2 * rows, :] = east_ref[:, width:].astype(f32)
    stride = face_x.shape[0] // rows

    def faces(i, carry):
        wind[0:1, :] = edge[pl.ds(i, 1), :]
        wind[1 : cells + 1, :] = u_ref[i].astype(f32)
        wind[cells + 1 : cells + 2, :] = edge[pl.ds(rows + i, 1), :]
        face_x[pl.ds(pl.multiple_of(i * stride, 8), stride), :] = 0.25 * (
            wind[0:stride, :] + wind[1 : stride + 1, :]
        )
        return carry

    lax.fori_loop(0, rows, faces, 0, unroll=4)
    wind_y[0:cells, :] = south_ref[:, width:].astype(f32)
    wind_y[cells : (rows + 1) * cells, :] = v_ref[...].reshape(rows * cells, levels).astype(f32)
    wind_y[(rows + 1) * cells :, :] = north_ref[:, width:].astype(f32)
    face_y[...] = 0.25 * (wind_y[: (rows + 1) * cells, :] + wind_y[cells:, :])
    lat = place_ref[0] >> log2(lons)
    south_open = jnp.where(lat > 0, 1.0, 0.0)
    north_open = jnp.where(lat < lats - 1, 1.0, 0.0)
    face_y[0:cells, :] = face_y[0:cells, :] * south_open
    face_y[rows * cells :, :] = face_y[rows * cells :, :] * north_open

    def tile(i, j):
        first = (i * (cells + 2) + j) * tracers
        return cell[pl.ds(pl.multiple_of(first, tracers), tracers), :]

    def spread_row(ref, r):
        return jnp.broadcast_to(ref[pl.ds(r, 1), :], (tracers, levels))

    for j in range(cells):
        low, high = tile(0, j + 1), tile(1, j + 1)
        flux_y[j * tracers : (j + 1) * tracers, :] = spread_row(face_y, j) * (low + high) - (
            DIFFUSE * south_open
        ) * (high - low)

    pos_copy.wait()

    def dyn_copy(i):
        return pltpu.make_async_copy(dyn_ref.at[i], dyn_hbm.at[i], row_sems.at[i])

    def row(i, carry):
        diffuse_y = DIFFUSE * jnp.where(i == rows - 1, north_open, 1.0)
        here = tile(i + 1, 1)
        last = tile(i + 1, 0)
        flux_w = spread_row(face_x, i * stride) * (last + here) - DIFFUSE * (here - last)
        for j in range(cells):
            after = tile(i + 1, j + 2)
            flux_e = spread_row(face_x, i * stride + j + 1) * (here + after) - DIFFUSE * (
                after - here
            )
            above = tile(i + 2, j + 1)
            flux_n = spread_row(face_y, (i + 1) * cells + j) * (here + above) - diffuse_y * (
                above - here
            )
            flux_s = flux_y[j * tracers : (j + 1) * tracers, :]
            flux_y[j * tracers : (j + 1) * tracers, :] = flux_n
            dyn = (flux_w - flux_e) + (flux_s - flux_n)
            dyn_ref[i, j * tracers : (j + 1) * tracers, :] = dyn
            send_ref[pos_s[i, j]] = (here + dyn).astype(jnp.bfloat16)
            here, flux_w = after, flux_e
        dyn_copy(i).start()
        return carry

    lax.fori_loop(0, rows, row, 0, unroll=2)

    send_copy = pltpu.make_async_copy(send_ref, send_hbm, sems.at[len(copies) + 2])
    send_copy.start()
    back_copy.wait()

    def drain(i, carry):
        dyn_copy(i).wait()
        return carry

    lax.fori_loop(0, rows, drain, 0)
    send_copy.wait()


def turn_kernel(own_ref, outer_ref, out_ref):
    for n, ref in enumerate((own_ref, outer_ref)):
        for k in range(ref.shape[0]):
            out_ref[n * ref.shape[0] + k] = ref[k].T


def inner_kernel(lows, place_ref, inner_ref, turned_ref, out_ref):
    owned = inner_ref.shape[0]
    place = place_ref[0]
    is_outer = ((place >> log2(lows)) & 1) == ((place >> (log2(lows) - 1)) & 1)
    out_ref[0:owned] = turned_ref[0:owned]

    @pl.when(is_outer)
    def _():
        out_ref[owned:] = turned_ref[owned:]

    @pl.when(jnp.logical_not(is_outer))
    def _():
        for k in range(owned):
            out_ref[owned + k] = inner_ref[k].T


def relax_kernel(x_ref, w_ref, y_ref, pos, pos_s, sem, slots):
    tracers, levels = x_ref.shape[1:]
    peers, lanes = pos.shape
    stored = x_ref.shape[0] // peers
    cap = stored - 1
    f32 = jnp.float32
    for p in range(peers):
        listed = x_ref[p * stored + cap].astype(f32)
        pos[p : p + 1, :] = (listed[0:1] * SLOTS + listed[1:2]).astype(jnp.int32)
    copy = pltpu.make_async_copy(pos, pos_s, sem)
    copy.start()
    copy.wait()

    def tile(at):
        return pl.ds(pl.multiple_of(at * tracers, tracers), tracers)

    def scatter(p, carry):
        for r in range(cap):
            slots[tile(pos_s[p, r]), :] = x_ref[p * stored + r].astype(f32)
        return carry

    lax.fori_loop(0, peers, scatter, 0, unroll=16)
    block = SLOTS * tracers

    def span(k, carry):
        at = pl.ds(pl.multiple_of(k * block, block), block)
        x = slots[at, :]
        y = jnp.dot(x.astype(jnp.bfloat16), w_ref[k], preferred_element_type=f32)
        slots[at, :] = y - x
        return carry

    lax.fori_loop(0, w_ref.shape[0], span, 0, unroll=32)

    def gather(p, carry):
        for r in range(cap):
            y_ref[p * cap + r] = slots[tile(pos_s[p, r]), :].astype(jnp.bfloat16)
        return carry

    lax.fori_loop(0, peers, gather, 0, unroll=16)


def finish_kernel(pos_ref, y_ref, dyn_ref, out_hbm, total, out, sems):
    rows, cells, width = out.shape
    tracers, levels = y_ref.shape[1:]

    def copy(i):
        return pltpu.make_async_copy(out.at[i], out_hbm.at[i], sems.at[i])

    def row(i, carry):
        for j in range(cells):
            tile = slice(j * tracers, (j + 1) * tracers)
            total[tile, :] = dyn_ref[i, tile, :] + y_ref[pos_ref[i, j]].astype(jnp.float32)
        for t in range(tracers):
            out[i, :, t * levels : (t + 1) * levels] = total[pl.ds(t, cells, stride=tracers), :]
        copy(i).start()
        return carry

    lax.fori_loop(0, rows, row, 0, unroll=2)
    for i in range(rows):
        copy(i).wait()


def in_pairs(x, axis, first):
    count = lax.axis_size(axis)
    pairs = [(i % count, (i + 1) % count) for i in range(first, count + first, 2)]
    return lax.ppermute(x, axis, pairs + [(b, a) for a, b in pairs])


def shards(tracers, east_wind, north_wind, span_of, slot_of, inverses):
    levels = east_wind.shape[2]
    rows, cells, width = tracers.shape
    kinds = width // levels
    columns = rows * cells
    lats, lows = lax.axis_size("lat"), lax.axis_size("lo")
    lons = lax.axis_size("hi") * lows
    peers = lats * lows
    owned = inverses.shape[0]
    cap = 2 * (3 * columns // (2 * lats * lons))
    stored = cap + 1
    f32, bf16, i32 = jnp.float32, jnp.bfloat16, jnp.int32
    dma = pltpu.SemaphoreType.DMA
    params = lambda mib: pltpu.CompilerParams(vmem_limit_bytes=mib << 20)

    side = 8
    place = lax.axis_index(("lat", "hi", "lo")).astype(i32).reshape(1)
    lon_a, lon_b, lat_a, lat_b = pl.pallas_call(
        functools.partial(edge_kernel, lons),
        out_shape=(jax.ShapeDtypeStruct((rows, width + levels), bf16),) * 2
        + (jax.ShapeDtypeStruct((cells, width + levels), bf16),) * 2,
        in_specs=[SMEM] + [ANY] * 3,
        out_specs=(ANY,) * 4,
        scratch_shapes=[
            pltpu.VMEM((2, rows, side, width), bf16),
            pltpu.VMEM((2, rows, side, levels), bf16),
            pltpu.VMEM((rows, width + levels), f32),
            pltpu.VMEM((2, rows, width + levels), bf16),
            pltpu.VMEM((2, cells, width + levels), bf16),
            dma((12,)),
        ],
        compiler_params=params(64),
        name="edges",
    )(place, tracers, east_wind, north_wind)
    far_edges = (
        in_pairs(lon_a, LON_AXES, 0),
        in_pairs(lon_b, LON_AXES, 1),
        in_pairs(lat_a, "lat", 0),
        in_pairs(lat_b, "lat", 1),
    )

    def opposite(start, stop):
        pairs = [(lo, lows + (lo ^ lows // 2)) for lo in range(start, stop)]
        return pairs + [(b, a) for a, b in pairs]

    outer = lax.ppermute(inverses, LON_AXES, opposite(0, lows // 2))
    cost = lambda us: pl.CostEstimate(
        flops=us * 1_000_000_000, bytes_accessed=1 << 20, transcendentals=0
    )
    fields = (span_of, slot_of, tracers, east_wind, north_wind, *far_edges)
    held = [(x.shape, x.dtype) for x in fields[:5]]
    held += [((2,) + x.shape, x.dtype) for x in (lon_a, lat_a)]
    stride = (cells + 1 + 7) // 8 * 8
    dyn_shape = (rows, cells * kinds, levels)
    send_shape = (peers * stored, kinds, levels)
    send, back, dyn = pl.pallas_call(
        functools.partial(flux_kernel, cap, owned, lats, lons, lows),
        out_shape=(
            jax.ShapeDtypeStruct(send_shape, bf16),
            jax.ShapeDtypeStruct((rows, 128), i32),
            jax.ShapeDtypeStruct(dyn_shape, f32),
        ),
        in_specs=[SMEM] + [ANY] * 9,
        out_specs=(ANY,) * 3,
        scratch_shapes=[pltpu.VMEM(*x) for x in held]
        + [
            dma((12,)),
            dma((rows,)),
            pltpu.VMEM((rows * peers, cells), f32),
            pltpu.VMEM((rows, 128), i32),
            pltpu.VMEM((rows, 128), i32),
            pltpu.SMEM((rows, 128), i32),
            pltpu.VMEM(send_shape, bf16),
            pltpu.VMEM(dyn_shape, f32),
            pltpu.VMEM(((rows + 2) * (cells + 2) * kinds, levels), f32),
            pltpu.VMEM((stride + 8, levels), f32),
            pltpu.VMEM((rows * stride, levels), f32),
            pltpu.VMEM(((rows + 2) * cells, levels), f32),
            pltpu.VMEM(((rows + 1) * cells, levels), f32),
            pltpu.VMEM((2 * rows, levels), f32),
            pltpu.VMEM((cells * kinds, levels), f32),
        ],
        compiler_params=params(64),
        cost_estimate=cost(FLUX_COST),
        name="flux",
    )(place, *fields)

    matrices, send = lax.optimization_barrier((inverses, send))
    inner = lax.ppermute(matrices, LON_AXES, opposite(lows // 2, lows))

    def exchange(x):
        x = x.reshape(peers, -1, kinds, levels)
        x = lax.all_to_all(x, GROUP_AXES, split_axis=0, concat_axis=0, tiled=True)
        return x.reshape(-1, kinds, levels)

    arrived = exchange(send)
    turned_shape = jax.ShapeDtypeStruct((2 * owned, levels, levels), bf16)
    turned = pl.pallas_call(
        turn_kernel,
        out_shape=turned_shape,
        in_specs=[VMEM] * 2,
        out_specs=VMEM,
        compiler_params=params(16),
        cost_estimate=cost(TURN_COST),
        name="turn",
    )(inverses, outer)
    turned = pl.pallas_call(
        functools.partial(inner_kernel, lows),
        out_shape=turned_shape,
        in_specs=[SMEM] + [VMEM] * 2,
        out_specs=VMEM,
        compiler_params=params(16),
        cost_estimate=cost(INNER_COST),
        name="inner",
    )(place, inner, turned)
    physics = pl.pallas_call(
        relax_kernel,
        out_shape=jax.ShapeDtypeStruct((peers * cap, kinds, levels), bf16),
        in_specs=[VMEM] * 2,
        out_specs=VMEM,
        scratch_shapes=[
            pltpu.VMEM((peers, 128), i32),
            pltpu.SMEM((peers, 128), i32),
            dma,
            pltpu.VMEM(((2 * owned * SLOTS + 1) * kinds, levels), f32),
        ],
        compiler_params=params(24),
        name="relax",
    )(arrived, turned)

    returned = exchange(physics)
    return pl.pallas_call(
        finish_kernel,
        out_shape=jax.ShapeDtypeStruct((rows, cells, width), f32),
        in_specs=[SMEM, VMEM, VMEM],
        out_specs=ANY,
        scratch_shapes=[
            pltpu.VMEM((cells * kinds, levels), f32),
            pltpu.VMEM((rows, cells, width), f32),
            dma((rows,)),
        ],
        compiler_params=params(16),
        name="finish",
    )(back, returned, dyn)


def solution(mesh):
    lats, lons = mesh.devices.shape
    split = Mesh(mesh.devices.reshape(lats, 2, lons // 2), ("lat", "hi", "lo"))
    block = P("lat", LON_AXES, None)
    in_specs = (
        block,
        block,
        block,
        P("lat", LON_AXES),
        P("lat", LON_AXES),
        P(("lat", "hi", "lo"), None, None),
    )
    return jax.shard_map(shards, mesh=split, in_specs=in_specs, out_specs=block, check_vma=False)
```

```python
import functools

import jax
import jax.numpy as jnp
from jax import lax
from jax.experimental import pallas as pl
from jax.experimental.pallas import tpu as pltpu
from jax.sharding import Mesh
from jax.sharding import PartitionSpec as P

FLUX_COST = 10
TURN_COST = 30
INNER_COST = 1
SLOTS = 48
DIFFUSE = 0.1
GROUP_AXES = ("lat", "lo")
LON_AXES = ("hi", "lo")

VMEM = pl.BlockSpec(memory_space=pltpu.VMEM)
ANY = pl.BlockSpec(memory_space=pltpu.HBM)
SMEM = pl.BlockSpec(memory_space=pltpu.SMEM)


def log2(n):
    return n.bit_length() - 1


def parities(place, lons):
    return place & 1, (place >> log2(lons)) & 1


def edge_kernel(
    lons, place_ref, q_hbm, u_hbm, v_hbm, lon_a, lon_b, lat_a, lat_b, q_side, u_side, wide, ready, row, sems
):
    rows, cells, width = q_hbm.shape
    side = q_side.shape[2]
    odd_lon, odd_lat = parities(place_ref[0], lons)
    copies = []

    def copy(source, target):
        copies.append(pltpu.make_async_copy(source, target, sems.at[len(copies)]))
        copies[-1].start()

    for n, odd in enumerate((odd_lon, 1 - odd_lon)):
        near = pl.ds(pl.multiple_of(jnp.where(odd == 1, 0, cells - side), side), side)
        copy(q_hbm.at[:, near, :], q_side.at[n])
        copy(u_hbm.at[:, near, :], u_side.at[n])
    for n, odd in enumerate((odd_lat, 1 - odd_lat)):
        i = jnp.where(odd == 1, 0, rows - 1)
        copy(q_hbm.at[i], row.at[n, :, 0:width])
        copy(v_hbm.at[i], row.at[n, :, width:])
    for c in copies[4:]:
        c.wait()
    copy(row.at[0], lat_a)
    copy(row.at[1], lat_b)
    for c in copies[:4]:
        c.wait()
    for n, (ref, odd) in enumerate(((lon_a, odd_lon), (lon_b, 1 - odd_lon))):
        first = odd == 1
        for i in range(rows):
            q, u = q_side[n, i].astype(jnp.float32), u_side[n, i].astype(jnp.float32)
            wide[i : i + 1, 0:width] = jnp.where(first, q[0:1], q[side - 1 :])
            wide[i : i + 1, width:] = jnp.where(first, u[0:1], u[side - 1 :])
        ready[n] = wide[...].astype(jnp.bfloat16)
        copy(ready.at[n], ref)
    for c in copies[8:]:
        c.wait()


def plan(place_ref, span_ref, slot_ref, send_ref, pos_ref, member, pos, cap, owned, lons, lows):
    rows, cells = span_ref.shape
    stored = cap + 1
    peers = send_ref.shape[0] // stored
    f32, bf16 = jnp.float32, jnp.bfloat16
    span, slot = span_ref[...], slot_ref[...]
    owner = span >> log2(owned)
    owner_lon = owner & (lons - 1)
    far = (owner_lon >> log2(lows)) != ((place_ref[0] >> log2(lows)) & 1)
    low = (owner_lon & (lows - 1)) ^ jnp.where(far, lows // 2, 0)
    peer = ((owner >> log2(lons)) << log2(lows)) + low
    local = (span & (owned - 1)) + jnp.where(far, owned, 0)
    iota = lambda shape, axis: lax.broadcasted_iota(jnp.int32, shape, axis)
    for i in range(rows):
        member[i * peers : (i + 1) * peers, :] = jnp.where(
            iota((peers, cells), 0) == peer[i : i + 1], 1.0, 0.0
        )
    hot = member[...].astype(bf16)
    dot = functools.partial(jnp.dot, preferred_element_type=f32)
    within = dot(hot, (iota((cells, cells), 0) < iota((cells, cells), 1)).astype(f32).astype(bf16))
    pairs = (rows * peers, rows * peers)
    to, of = iota(pairs, 0), iota(pairs, 1)
    same = (to & (peers - 1)) == (of & (peers - 1))
    lower = jnp.where(same & (of < (to & -peers)), 1.0, 0.0).astype(bf16)
    before = within + jnp.sum(dot(lower, hot), axis=1, keepdims=True)
    before = before * member[...]
    lists = jnp.zeros((3 * peers, 128), f32)
    for i in range(rows):
        block = slice(i * peers, (i + 1) * peers)
        rank = jnp.sum(before[block], axis=0, keepdims=True).astype(jnp.int32)
        pos[i : i + 1, 0:cells] = peer[i : i + 1] * stored + rank
        pos_ref[i : i + 1, 0:cells] = peer[i : i + 1] * cap + rank
        chosen = jnp.where(iota((128, cells), 0) == rank, 1.0, 0.0).astype(bf16)
        mine = member[block]
        values = jnp.concatenate(
            [mine * local[i : i + 1].astype(f32), mine * slot[i : i + 1].astype(f32), mine], axis=0
        )
        lists = lists + lax.dot_general(
            values.astype(bf16), chosen, (((1,), (1,)), ((), ())), preferred_element_type=f32
        )
    spans = jnp.where(lists[2 * peers :] > 0.5, lists[:peers], 2.0 * owned)
    slots = lists[peers : 2 * peers]
    tile = send_ref.shape[1:]
    for p in range(peers):
        send_ref[p * stored + cap] = jnp.where(
            iota(tile, 0) == 0,
            jnp.broadcast_to(spans[p : p + 1], tile),
            jnp.broadcast_to(slots[p : p + 1], tile),
        ).astype(bf16)


def flux_kernel(
    cap,
    owned,
    lats,
    lons,
    lows,
    place_ref,
    *refs,
):
    sources, (send_hbm, back_hbm, dyn_hbm), rest = refs[:9], refs[9:12], refs[12:]
    held, rest = rest[:7], rest[7:]
    (
        sems,
        row_sems,
        member,
        back,
        pos,
        pos_s,
        send_ref,
        dyn_ref,
        cell,
        wind,
        face_x,
        wind_y,
        face_y,
        edge,
        flux_y,
    ) = rest
    span_ref, slot_ref, q_ref, u_ref, v_ref, lon_ref, lat_ref = held
    west_ref, east_ref = lon_ref.at[0], lon_ref.at[1]
    south_ref, north_ref = lat_ref.at[0], lat_ref.at[1]
    odd_lon, odd_lat = parities(place_ref[0], lons)
    targets = held[:5] + (
        lon_ref.at[1 - odd_lon],
        lon_ref.at[odd_lon],
        lat_ref.at[1 - odd_lat],
        lat_ref.at[odd_lat],
    )
    rows, cells, width = q_ref.shape
    levels = u_ref.shape[2]
    tracers = width // levels
    f32 = jnp.float32
    line = (cells + 2) * tracers
    copies = [pltpu.make_async_copy(a, b, sems.at[n]) for n, (a, b) in enumerate(zip(sources, targets))]
    for copy in copies:
        copy.start()

    def spread(block, first, count, stride):
        for t in range(tracers):
            cell[pl.ds(first + t, count, stride=stride), :] = block(t).astype(f32)

    lanes = lambda t: slice(t * levels, (t + 1) * levels)
    for copy in copies[:2]:
        copy.wait()
    plan(place_ref, span_ref, slot_ref, send_ref, back, member, pos, cap, owned, lons, lows)
    pos_copy = pltpu.make_async_copy(pos, pos_s, sems.at[len(copies)])
    pos_copy.start()
    back_copy = pltpu.make_async_copy(back, back_hbm, sems.at[len(copies) + 1])
    back_copy.start()
    copies[2].wait()

    def relayout(i, carry):
        spread(
            lambda t: q_ref[i, :, lanes(t)], (i + 1) * line + tracers, cells, tracers
        )
        return carry

    lax.fori_loop(0, rows, relayout, 0, unroll=16)
    for copy in copies[3:]:
        copy.wait()
    spread(lambda t: south_ref[:, lanes(t)], tracers, cells, tracers)
    spread(lambda t: north_ref[:, lanes(t)], (rows + 1) * line + tracers, cells, tracers)
    spread(lambda t: west_ref[:, lanes(t)], line, rows, line)
    spread(lambda t: east_ref[:, lanes(t)], line + (cells + 1) * tracers, rows, line)

    edge[0:rows, :] = west_ref[:, width:].astype(f32)
    edge[rows : 2 * rows, :] = east_ref[:, width:].astype(f32)
    stride = face_x.shape[0] // rows

    def faces(i, carry):
        wind[0:1, :] = edge[pl.ds(i, 1), :]
        wind[1 : cells + 1, :] = u_ref[i].astype(f32)
        wind[cells + 1 : cells + 2, :] = edge[pl.ds(rows + i, 1), :]
        face_x[pl.ds(pl.multiple_of(i * stride, 8), stride), :] = 0.25 * (
            wind[0:stride, :] + wind[1 : stride + 1, :]
        )
        return carry

    lax.fori_loop(0, rows, faces, 0, unroll=16)
    wind_y[0:cells, :] = south_ref[:, width:].astype(f32)
    wind_y[cells : (rows + 1) * cells, :] = v_ref[...].reshape(rows * cells, levels).astype(f32)
    wind_y[(rows + 1) * cells :, :] = north_ref[:, width:].astype(f32)
    face_y[...] = 0.25 * (wind_y[: (rows + 1) * cells, :] + wind_y[cells:, :])
    lat = place_ref[0] >> log2(lons)
    south_open = jnp.where(lat > 0, 1.0, 0.0)
    north_open = jnp.where(lat < lats - 1, 1.0, 0.0)
    face_y[0:cells, :] = face_y[0:cells, :] * south_open
    face_y[rows * cells :, :] = face_y[rows * cells :, :] * north_open

    def tile(i, j):
        first = (i * (cells + 2) + j) * tracers
        return cell[pl.ds(pl.multiple_of(first, tracers), tracers), :]

    def spread_row(ref, r):
        return jnp.broadcast_to(ref[pl.ds(r, 1), :], (tracers, levels))

    for j in range(cells):
        low, high = tile(0, j + 1), tile(1, j + 1)
        flux_y[j * tracers : (j + 1) * tracers, :] = spread_row(face_y, j) * (low + high) - (
            DIFFUSE * south_open
        ) * (high - low)

    pos_copy.wait()

    def dyn_copy(i):
        return pltpu.make_async_copy(dyn_ref.at[i], dyn_hbm.at[i], row_sems.at[i])

    def row(i, carry):
        diffuse_y = DIFFUSE * jnp.where(i == rows - 1, north_open, 1.0)
        here = tile(i + 1, 1)
        last = tile(i + 1, 0)
        flux_w = spread_row(face_x, i * stride) * (last + here) - DIFFUSE * (here - last)
        for j in range(cells):
            after = tile(i + 1, j + 2)
            flux_e = spread_row(face_x, i * stride + j + 1) * (here + after) - DIFFUSE * (
                after - here
            )
            above = tile(i + 2, j + 1)
            flux_n = spread_row(face_y, (i + 1) * cells + j) * (here + above) - diffuse_y * (
                above - here
            )
            flux_s = flux_y[j * tracers : (j + 1) * tracers, :]
            flux_y[j * tracers : (j + 1) * tracers, :] = flux_n
            dyn = (flux_w - flux_e) + (flux_s - flux_n)
            dyn_ref[i, j * tracers : (j + 1) * tracers, :] = dyn
            send_ref[pos_s[i, j]] = (here + dyn).astype(jnp.bfloat16)
            here, flux_w = after, flux_e
        dyn_copy(i).start()
        return carry

    lax.fori_loop(0, rows, row, 0, unroll=2)

    send_copy = pltpu.make_async_copy(send_ref, send_hbm, sems.at[len(copies) + 2])
    send_copy.start()
    back_copy.wait()

    def drain(i, carry):
        dyn_copy(i).wait()
        return carry

    lax.fori_loop(0, rows, drain, 0)
    send_copy.wait()


def turn_kernel(*refs):
    refs, out_ref = refs[:-1], refs[-1]
    for n, ref in enumerate(refs):
        for k in range(ref.shape[0]):
            out_ref[n * ref.shape[0] + k] = ref[k].T


def relax_kernel(lows, place_ref, x_ref, outer_ref, inner_ref, y_ref, pos, pos_s, sem, slots):
    tracers, levels = x_ref.shape[1:]
    peers, lanes = pos.shape
    stored = x_ref.shape[0] // peers
    cap = stored - 1
    f32 = jnp.float32
    for p in range(peers):
        listed = x_ref[p * stored + cap].astype(f32)
        pos[p : p + 1, :] = (listed[0:1] * SLOTS + listed[1:2]).astype(jnp.int32)
    copy = pltpu.make_async_copy(pos, pos_s, sem)
    copy.start()
    copy.wait()

    def tile(at):
        return pl.ds(pl.multiple_of(at * tracers, tracers), tracers)

    def scatter(p, carry):
        for r in range(cap):
            slots[tile(pos_s[p, r]), :] = x_ref[p * stored + r].astype(f32)
        return carry

    lax.fori_loop(0, peers, scatter, 0, unroll=16)
    block = SLOTS * tracers

    def relax(first, count, w_ref, w_first):
        def span(k, carry):
            at = pl.ds(pl.multiple_of((first + k) * block, block), block)
            x = slots[at, :]
            y = jnp.dot(x.astype(jnp.bfloat16), w_ref[w_first + k], preferred_element_type=f32)
            slots[at, :] = y - x
            return carry

        lax.fori_loop(0, count, span, 0, unroll=16)

    owned = inner_ref.shape[0]
    place = place_ref[0]
    is_outer = ((place >> log2(lows)) & 1) == ((place >> (log2(lows) - 1)) & 1)
    relax(0, owned, outer_ref, 0)

    @pl.when(is_outer)
    def _():
        relax(owned, owned, outer_ref, owned)

    @pl.when(jnp.logical_not(is_outer))
    def _():
        relax(owned, owned, inner_ref, 0)

    def gather(p, carry):
        for r in range(cap):
            y_ref[p * cap + r] = slots[tile(pos_s[p, r]), :].astype(jnp.bfloat16)
        return carry

    lax.fori_loop(0, peers, gather, 0, unroll=16)


def finish_kernel(pos_ref, y_ref, dyn_ref, out_hbm, total, out, sems):
    rows, cells, width = out.shape
    tracers, levels = y_ref.shape[1:]

    def copy(i):
        return pltpu.make_async_copy(out.at[i], out_hbm.at[i], sems.at[i])

    def row(i, carry):
        for j in range(cells):
            tile = slice(j * tracers, (j + 1) * tracers)
            total[tile, :] = dyn_ref[i, tile, :] + y_ref[pos_ref[i, j]].astype(jnp.float32)
        for t in range(tracers):
            out[i, :, t * levels : (t + 1) * levels] = total[pl.ds(t, cells, stride=tracers), :]
        copy(i).start()
        return carry

    lax.fori_loop(0, rows, row, 0)
    for i in range(rows):
        copy(i).wait()


def in_pairs(x, axis, first):
    count = lax.axis_size(axis)
    pairs = [(i % count, (i + 1) % count) for i in range(first, count + first, 2)]
    return lax.ppermute(x, axis, pairs + [(b, a) for a, b in pairs])


def shards(tracers, east_wind, north_wind, span_of, slot_of, inverses):
    levels = east_wind.shape[2]
    rows, cells, width = tracers.shape
    kinds = width // levels
    columns = rows * cells
    lats, lows = lax.axis_size("lat"), lax.axis_size("lo")
    lons = lax.axis_size("hi") * lows
    peers = lats * lows
    owned = inverses.shape[0]
    cap = 2 * (3 * columns // (2 * lats * lons))
    stored = cap + 1
    f32, bf16, i32 = jnp.float32, jnp.bfloat16, jnp.int32
    dma = pltpu.SemaphoreType.DMA
    params = lambda mib: pltpu.CompilerParams(vmem_limit_bytes=mib << 20)

    side = 8
    place = lax.axis_index(("lat", "hi", "lo")).astype(i32).reshape(1)
    lon_a, lon_b, lat_a, lat_b = pl.pallas_call(
        functools.partial(edge_kernel, lons),
        out_shape=(jax.ShapeDtypeStruct((rows, width + levels), bf16),) * 2
        + (jax.ShapeDtypeStruct((cells, width + levels), bf16),) * 2,
        in_specs=[SMEM] + [ANY] * 3,
        out_specs=(ANY,) * 4,
        scratch_shapes=[
            pltpu.VMEM((2, rows, side, width), bf16),
            pltpu.VMEM((2, rows, side, levels), bf16),
            pltpu.VMEM((rows, width + levels), f32),
            pltpu.VMEM((2, rows, width + levels), bf16),
            pltpu.VMEM((2, cells, width + levels), bf16),
            dma((12,)),
        ],
        compiler_params=params(64),
        name="edges",
    )(place, tracers, east_wind, north_wind)
    far_edges = (
        in_pairs(lon_a, LON_AXES, 0),
        in_pairs(lon_b, LON_AXES, 1),
        in_pairs(lat_a, "lat", 0),
        in_pairs(lat_b, "lat", 1),
    )

    def opposite(start, stop):
        pairs = [(lo, lows + (lo ^ lows // 2)) for lo in range(start, stop)]
        return pairs + [(b, a) for a, b in pairs]

    outer = lax.ppermute(inverses, LON_AXES, opposite(0, lows // 2))
    cost = lambda us: pl.CostEstimate(
        flops=us * 1_000_000_000, bytes_accessed=1 << 20, transcendentals=0
    )
    fields = (span_of, slot_of, tracers, east_wind, north_wind, *far_edges)
    held = [(x.shape, x.dtype) for x in fields[:5]]
    held += [((2,) + x.shape, x.dtype) for x in (lon_a, lat_a)]
    stride = (cells + 1 + 7) // 8 * 8
    dyn_shape = (rows, cells * kinds, levels)
    send_shape = (peers * stored, kinds, levels)
    send, back, dyn = pl.pallas_call(
        functools.partial(flux_kernel, cap, owned, lats, lons, lows),
        out_shape=(
            jax.ShapeDtypeStruct(send_shape, bf16),
            jax.ShapeDtypeStruct((rows, 128), i32),
            jax.ShapeDtypeStruct(dyn_shape, f32),
        ),
        in_specs=[SMEM] + [ANY] * 9,
        out_specs=(ANY,) * 3,
        scratch_shapes=[pltpu.VMEM(*x) for x in held]
        + [
            dma((12,)),
            dma((rows,)),
            pltpu.VMEM((rows * peers, cells), f32),
            pltpu.VMEM((rows, 128), i32),
            pltpu.VMEM((rows, 128), i32),
            pltpu.SMEM((rows, 128), i32),
            pltpu.VMEM(send_shape, bf16),
            pltpu.VMEM(dyn_shape, f32),
            pltpu.VMEM(((rows + 2) * (cells + 2) * kinds, levels), f32),
            pltpu.VMEM((stride + 8, levels), f32),
            pltpu.VMEM((rows * stride, levels), f32),
            pltpu.VMEM(((rows + 2) * cells, levels), f32),
            pltpu.VMEM(((rows + 1) * cells, levels), f32),
            pltpu.VMEM((2 * rows, levels), f32),
            pltpu.VMEM((cells * kinds, levels), f32),
        ],
        compiler_params=params(64),
        cost_estimate=cost(FLUX_COST),
        name="flux",
    )(place, *fields)

    matrices, send = lax.optimization_barrier((inverses, send))
    inner = lax.ppermute(matrices, LON_AXES, opposite(lows // 2, lows))

    def exchange(x):
        x = x.reshape(peers, -1, kinds, levels)
        x = lax.all_to_all(x, GROUP_AXES, split_axis=0, concat_axis=0, tiled=True)
        return x.reshape(-1, kinds, levels)

    arrived = exchange(send)
    def turned(us, *arrays):
        return pl.pallas_call(
            turn_kernel,
            out_shape=jax.ShapeDtypeStruct((len(arrays) * owned, levels, levels), bf16),
            in_specs=[VMEM] * len(arrays),
            out_specs=VMEM,
            compiler_params=params(16),
            cost_estimate=cost(us),
            name="turn",
        )(*arrays)

    physics = pl.pallas_call(
        functools.partial(relax_kernel, lows),
        out_shape=jax.ShapeDtypeStruct((peers * cap, kinds, levels), bf16),
        in_specs=[SMEM] + [VMEM] * 3,
        out_specs=VMEM,
        scratch_shapes=[
            pltpu.VMEM((peers, 128), i32),
            pltpu.SMEM((peers, 128), i32),
            dma,
            pltpu.VMEM(((2 * owned * SLOTS + 1) * kinds, levels), f32),
        ],
        compiler_params=params(24),
        name="relax",
    )(place, arrived, turned(TURN_COST, inverses, outer), turned(INNER_COST, inner))

    returned = exchange(physics)
    return pl.pallas_call(
        finish_kernel,
        out_shape=jax.ShapeDtypeStruct((rows, cells, width), f32),
        in_specs=[SMEM, VMEM, VMEM],
        out_specs=ANY,
        scratch_shapes=[
            pltpu.VMEM((cells * kinds, levels), f32),
            pltpu.VMEM((rows, cells, width), f32),
            dma((rows,)),
        ],
        compiler_params=params(16),
        name="finish",
    )(back, returned, dyn)


def solution(mesh):
    lats, lons = mesh.devices.shape
    split = Mesh(mesh.devices.reshape(lats, 2, lons // 2), ("lat", "hi", "lo"))
    block = P("lat", LON_AXES, None)
    in_specs = (
        block,
        block,
        block,
        P("lat", LON_AXES),
        P("lat", LON_AXES),
        P(("lat", "hi", "lo"), None, None),
    )
    return jax.shard_map(shards, mesh=split, in_specs=in_specs, out_specs=block, check_vma=False)
```
